32 devices in a mesh: seq: 8 (over z, y), tensor: 4 (over x, core).
Axes of the slice: x: 2, y: 2, z: 4, core: 2. Of those that a mesh axis runs over, the one named last changes fastest.
Arguments:
- layer_in: bfloat16 [6, 1024, 2048], P(None, ('seq', 'tensor')), may hold values from -6 to 6
- cotangent: bfloat16 [6, 1024, 2048], P(None, ('seq', 'tensor')), may hold values from -6 to 6
- doc_lengths: int32 [6, 8], replicated, may hold values from 1 to 768, 1024 in all within a row
- pad_counts: int32 [6], replicated, may hold values from 0 to 127
- gain_attn: float32 [2048], replicated, may hold values from 0.5 to 1.5
- gain_ffn: float32 [2048], replicated, may hold values from 0.5 to 1.5
- w_qkv: bfloat16 [3, 2048, 2048], P(None, None, 'tensor'), may hold values from -0.125 to 0.125
- a_qkv: bfloat16 [3, 2048, 16], replicated, may hold values from -0.125 to 0.125
- b_qkv: bfloat16 [3, 16, 2048], P(None, None, 'tensor'), may hold values from -0.75 to 0.75
- m_qkv: float32 [3, 2048], P(None, 'tensor'), may hold values from 0.6 to 1.6
- w_out: bfloat16 [2048, 2048], P('tensor'), may hold values from -0.1875 to 0.1875
- a_out: bfloat16 [2048, 16], P('tensor'), may hold values from -0.125 to 0.125
- b_out: bfloat16 [16, 2048], replicated, may hold values from -0.75 to 0.75
- m_out: float32 [2048], replicated, may hold values from 3 to 30
- w_gateup: bfloat16 [2, 2048, 5632], P(None, None, 'tensor'), may hold values from -0.125 to 0.125
- a_gateup: bfloat16 [2, 2048, 16], replicated, may hold values from -0.125 to 0.125
- b_gateup: bfloat16 [2, 16, 5632], P(None, None, 'tensor'), may hold values from -0.75 to 0.75
- m_gateup: float32 [2, 5632], P(None, 'tensor'), may hold values from 0.5 to 3
- w_down: bfloat16 [5632, 2048], P('tensor'), may hold values from -0.109375 to 0.109375
- a_down: bfloat16 [5632, 16], P('tensor'), may hold values from -0.078125 to 0.078125
- b_down: bfloat16 [16, 2048], replicated, may hold values from -0.75 to 0.75
- m_down: float32 [2048], replicated, may hold values from 0.5 to 4
Outputs:
- layer_out: bfloat16 [6, 1024, 2048], P(None, ('seq', 'tensor'))
- grad_in: float32 [6, 1024, 2048], P(None, ('seq', 'tensor'))
- grad_a_qkv: float32 [3, 2048, 16], replicated
- grad_b_qkv: float32 [3, 16, 2048], P(None, None, 'tensor')
- grad_m_qkv: float32 [3, 2048], P(None, 'tensor')
- grad_a_out: float32 [2048, 16], P('tensor')
- grad_b_out: float32 [16, 2048], replicated
- grad_m_out: float32 [2048], replicated
- grad_a_gateup: float32 [2, 2048, 16], replicated
- grad_b_gateup: float32 [2, 16, 5632], P(None, None, 'tensor')
- grad_m_gateup: float32 [2, 5632], P(None, 'tensor')
- grad_a_down: float32 [5632, 16], P('tensor')
- grad_b_down: float32 [16, 2048], replicated
- grad_m_down: float32 [2048], replicated
The draws below stay inside these ranges and needn't reach their ends.
Inputs may be any that keep to these rules, and one draw needn't show every extreme that they name: `doc_lengths`: each row's 8 document lengths sum to 1024.
All inputs are finite; a program needn't handle non-finite values.
Results may differ from the reference program's by a relative error of at most 0.03.
Values may be sent and summed in bfloat16 or wider, within the bound.
No kernel may reach another device: no remote copies, remote signals or barrier semaphores. Data moves between devices by JAX's collectives and lax.ppermute only.
A program may use at most 512 MiB of HBM per device.

```python
import math
import jax
import jax.numpy as jnp
import numpy as np
from jax import lax

D = 2048
HEADS = 16
HEAD_DIM = 128
FF = 5632
RANK = 16
ROWS = 6
NDOC = 8
HH = 2048
LENGTH = 1024


def plant(values, key, low, top_value):
    longest = values.shape.index(max(values.shape))
    spots = []
    for shift in (0, 1):
        where = [jax.random.randint(jax.random.fold_in(key, axis), (), 0, length) for axis, length in enumerate(values.shape)]
        where[longest] = (where[longest] + shift) % values.shape[longest]
        spots.append(tuple(where))
    return values.at[spots[0]].set(low).at[spots[1]].set(top_value)


def with_spikes(entries, key, source, target, parts, factor):
    owner, partner = [(jnp.arange(entries.shape[dim]) // (entries.shape[dim] // parts)).reshape([-1 if axis == dim else 1 for axis in range(entries.ndim)]) for dim in (source, target)]
    chosen = jax.random.permutation(key, parts)[partner]
    strong = (owner == chosen) | (owner == (partner + parts // 2) % parts)
    return jnp.where(strong, factor * entries, entries)


def levels(rng, extent, pieces, smallest, top_value):
    level = 1.0
    for axis_at, parts in pieces:
        steps = jax.random.uniform(jax.random.fold_in(jax.random.fold_in(rng, 6), axis_at), (parts,), jnp.float32, smallest / len(pieces), top_value / len(pieces))
        level = level * jnp.repeat(jnp.exp(steps), extent[axis_at] // parts).reshape((-1,) + (1,) * (len(extent) - 1 - axis_at))
    return level


def profile(amount, total, bound, skew):
    portions = [(1 << 20) // math.isqrt(rank ** skew) + 1 for rank in range(2, amount + 1)]
    rest, given = total - bound - (amount - 1), [1] * (amount - 1)
    while rest > 0:
        movable = [i for i in range(amount - 1) if given[i] < bound]
        mass, remaining = sum([portions[i] for i in movable]), rest
        for i in movable:
            addition = min(bound - given[i], max(1, remaining * portions[i] // mass), rest)
            given[i] = given[i] + addition
            rest = rest - addition
    return np.array([bound] + given)


def ragged(rng, count, total, limit, slope):
    if count == 2:
        one = jax.random.randint(rng, (), max(1, total - limit), min(limit, total - 1) + 1)
        return jnp.stack([one, total - one])
    sizes = jnp.asarray(profile(count, total, limit, slope), jnp.int32)
    pairs = (count - 1) // 2
    giver, receiver = sizes[1:1 + 2 * pairs:2], sizes[2:2 + 2 * pairs:2]
    slack = jnp.minimum(giver - 1, limit - receiver)
    shifted = jax.random.randint(jax.random.fold_in(rng, 1), (pairs,), 0, 1 << 20) % (slack + 1)
    sizes = sizes.at[1:1 + 2 * pairs:2].set(giver - shifted).at[2:2 + 2 * pairs:2].set(receiver + shifted)
    return sizes[jax.random.permutation(jax.random.fold_in(rng, 2), count)]


def normal_values(rng, shape, width, reach, cuts=(), kind=jnp.bfloat16):
    level = levels(rng, shape, cuts, -0.22, 0.18) if cuts else 1.0
    drawn = jax.random.normal(rng, shape, jnp.float32) * width * level
    return jnp.minimum(jnp.maximum(drawn, -reach), reach).astype(kind)


def bell_draw_with(own_key, dims, scale, limit, split, heavy, kind=jnp.bfloat16):
    values = scale * jax.random.normal(own_key, dims, jnp.float32)
    if split:
        values = values * levels(own_key, dims, split, -0.22, 0.18)
    return jnp.clip(with_spikes(values, jax.random.fold_in(own_key, 3), *heavy), -limit, limit).astype(kind)


def setup_inputs(seed: int = 0) -> dict:
    key_of = jax.random.split(jax.random.key(seed), 23)
    layer_in = normal_values(key_of[0], (ROWS, LENGTH, D), 1.0, 6.0, ((1, 32),))
    cotangent = normal_values(key_of[1], (ROWS, LENGTH, D), 1.0, 6.0, ((1, 32),))
    doc_lengths = jax.vmap(lambda own: ragged(own, NDOC, LENGTH, 3 * LENGTH // 4, 2))(jax.random.split(key_of[2], ROWS)).reshape((ROWS, NDOC)).astype(jnp.int32)
    pad_counts = plant(jax.random.randint(key_of[3], (ROWS,), 0, LENGTH // 8), jax.random.fold_in(key_of[3], 1), 0, (LENGTH // 8) - 1).astype(jnp.int32)
    gain_attn = jnp.clip(1.0 + 0.1 * jax.random.normal(key_of[4], (D,), jnp.float32), 0.5, 1.5)
    gain_ffn = jnp.clip(1.0 + 0.1 * jax.random.normal(key_of[5], (D,), jnp.float32), 0.5, 1.5)
    w_qkv = normal_values(key_of[6], (3, D, HH), D ** -0.5, 0.125, ((2, 4),))
    a_qkv = normal_values(key_of[7], (3, D, RANK), D ** -0.5, 0.125)
    b_qkv = normal_values(key_of[8], (3, RANK, HH), (4 * RANK) ** -0.5, 0.75, ((2, 4),))
    m_qkv = jnp.clip(jnp.exp(math.log(1.6) - 0.98082923 * jax.random.uniform(key_of[9], (3, HH), jnp.float32) ** levels(key_of[9], (3, HH), ((1, 4),), -0.2, 0.2)), 0.6, 1.6)
    w_out = bell_draw_with(key_of[10], (HH, D), HH ** -0.5, 0.1875, ((0, 4),), (0, 1, 4, 2.0))
    a_out = normal_values(key_of[11], (HH, RANK), HH ** -0.5, 0.125, ((0, 4),))
    b_out = normal_values(key_of[12], (RANK, D), (4 * RANK) ** -0.5, 0.75)
    m_out = jnp.clip(jnp.exp(jax.random.uniform(key_of[13], (D,), jnp.float32, math.log(3.0), math.log(30.0))), 3.0, 30.0)
    w_gateup = normal_values(key_of[14], (2, D, FF), D ** -0.5, 0.125, ((2, 4),))
    a_gateup = normal_values(key_of[15], (2, D, RANK), D ** -0.5, 0.125)
    b_gateup = normal_values(key_of[16], (2, RANK, FF), (4 * RANK) ** -0.5, 0.75, ((2, 4),))
    m_gateup = jnp.clip(jnp.exp(math.log(3.0) - 1.7917595 * jax.random.uniform(key_of[17], (2, FF), jnp.float32) ** levels(key_of[17], (2, FF), ((1, 4),), -0.2, 0.2)), 0.5, 3.0)
    w_down = bell_draw_with(key_of[18], (FF, D), FF ** -0.5, 0.109375, ((0, 4),), (0, 1, 4, 2.0))
    a_down = normal_values(key_of[19], (FF, RANK), FF ** -0.5, 0.078125, ((0, 4),))
    b_down = normal_values(key_of[20], (RANK, D), (4 * RANK) ** -0.5, 0.75)
    m_down = jnp.clip(jnp.exp(jax.random.uniform(key_of[21], (D,), jnp.float32, math.log(0.5), math.log(4.0))), 0.5, 4.0)
    return dict(layer_in=layer_in, cotangent=cotangent, doc_lengths=doc_lengths, pad_counts=pad_counts, gain_attn=gain_attn, gain_ffn=gain_ffn, w_qkv=w_qkv, a_qkv=a_qkv, b_qkv=b_qkv, m_qkv=m_qkv, w_out=w_out, a_out=a_out, b_out=b_out, m_out=m_out, w_gateup=w_gateup, a_gateup=a_gateup, b_gateup=b_gateup, m_gateup=m_gateup, w_down=w_down, a_down=a_down, b_down=b_down, m_down=m_down)


epsilon = 1e-05
adapter_scale = 2.0
rope_base = 10000.0
maximal_precision = lax.Precision.HIGHEST

@jax.custom_vjp
def low(v):
    return lax.optimization_barrier(v.astype(jnp.bfloat16)).astype(jnp.float32)

@jax.custom_vjp
def low_back(v):
    return v

def low_keep(v):
    return (low(v), None)

def low_pass(kept, grad):
    return (grad,)

def back_keep(v):
    return (v, None)

def back_low(kept, grad):
    return (low(grad),)
low.defvjp(low_keep, low_pass)
low_back.defvjp(back_keep, back_low)

def rms_norm(values, gain):
    return values * lax.rsqrt(lax.optimization_barrier(jnp.mean(values * values, axis=-1, keepdims=True)) + epsilon) * gain

def rotary_tables(positions, head_size):
    half_size = head_size // 2
    frequency = rope_base ** (-(2.0 * jnp.arange(half_size, dtype=jnp.float32)) / head_size)
    angles = positions.astype(jnp.float32)[:, None] * frequency[None, :]
    cosine = jnp.concatenate([jnp.cos(angles), jnp.cos(angles)], axis=-1)
    sine_table = jnp.concatenate([jnp.sin(angles), jnp.sin(angles)], axis=-1)
    return (cosine, sine_table)

def rotate(values, cosine, sine_table):
    half_size = values.shape[-1] // 2
    turned = jnp.concatenate([-values[..., half_size:], values[..., :half_size]], axis=-1)
    return values * cosine[None, :, None, :] + turned * sine_table[None, :, None, :]

def dora_proj(input_rows, frozen_weight, down_adapter_matrix, up_adapter_matrix, magnitude):
    weight_heading = frozen_weight + adapter_scale * jnp.dot(down_adapter_matrix, up_adapter_matrix, precision=maximal_precision)
    lengths = jnp.sqrt(lax.optimization_barrier(jnp.sum(weight_heading * weight_heading, axis=0)))
    adapter_activation_rows = low(low_back(jnp.dot(input_rows, down_adapter_matrix, precision=maximal_precision)))
    plain_output_rows = low_back(jnp.dot(input_rows, frozen_weight, precision=maximal_precision) + adapter_scale * jnp.dot(adapter_activation_rows, up_adapter_matrix, precision=maximal_precision))
    return plain_output_rows * (magnitude / lengths)

def attend_row(queries, key_heads, value_heads, doc_row):
    total_len = queries.shape[0]
    block_len = min(total_len, 512)
    score_scale = 1.0 / math.sqrt(queries.shape[-1])
    key_pos = jnp.arange(total_len, dtype=jnp.int32)

    def one_block(block_index):
        first_pos = (block_index * block_len).astype(jnp.int32)
        query_block = lax.dynamic_slice_in_dim(queries, first_pos, block_len, 0)
        query_pos = first_pos + jnp.arange(block_len, dtype=jnp.int32)
        query_docs = lax.dynamic_slice_in_dim(doc_row, first_pos, block_len, 0)
        raw_scores = low_back(jnp.einsum('qhd,khd->hqk', query_block, key_heads, precision=maximal_precision))
        allowed = jnp.logical_and(key_pos[None, :] <= query_pos[:, None], doc_row[None, :] == query_docs[:, None])
        weights = jnp.where(allowed[None], jnp.exp(raw_scores * score_scale), 0.0)
        totals = lax.optimization_barrier(jnp.sum(weights, axis=-1))
        accumulated = low_back(jnp.einsum('hqk,khd->qhd', low(weights), value_heads, precision=maximal_precision))
        return accumulated / jnp.transpose(totals)[:, :, None]
    blocks = lax.map(jax.checkpoint(one_block), jnp.arange(total_len // block_len, dtype=jnp.int32))
    return blocks.reshape(queries.shape)

def to_wide(values):
    return values.astype(jnp.float32)

def reference(layer_in, cotangent, doc_lengths, pad_counts, gain_attn, gain_ffn, w_qkv, a_qkv, b_qkv, m_qkv, w_out, a_out, b_out, m_out, w_gateup, a_gateup, b_gateup, m_gateup, w_down, a_down, b_down, m_down):
    row_count, total_len, model_width = layer_in.shape
    positions = jnp.arange(total_len, dtype=jnp.int32)
    offsets = jnp.cumsum(doc_lengths, axis=1).astype(jnp.int32)
    doc_ids = lax.optimization_barrier(jnp.sum((offsets[:, None, :] <= positions[None, :, None]).astype(jnp.int32), axis=-1))
    cosine, sine_table = rotary_tables(positions, HEAD_DIM)
    qkv_frozen = to_wide(w_qkv)
    out_frozen = to_wide(w_out)
    gateup_frozen = to_wide(w_gateup)
    down_frozen = to_wide(w_down)
    four_d = (row_count, total_len, HEADS, HEAD_DIM)

    def forward(values, adapters):
        aq, bq, mq, ao, bo, mo, ag, bg, mg, ad, bd, md = adapters
        normed = low(rms_norm(values, gain_attn))
        projected = [dora_proj(normed, qkv_frozen[member], aq[member], bq[member], mq[member]) for member in range(3)]
        queries = low(rotate(projected[0].reshape(four_d), cosine, sine_table))
        key_heads = low(rotate(projected[1].reshape(four_d), cosine, sine_table))
        value_heads = low(projected[2].reshape(four_d))
        attended = lax.map(lambda packed: attend_row(packed[0], packed[1], packed[2], packed[3]), (queries, key_heads, value_heads, doc_ids))
        attended = low(attended.reshape(row_count, total_len, HEADS * HEAD_DIM))
        middle = values + dora_proj(attended, out_frozen, ao, bo, mo)
        normed_f = low(rms_norm(middle, gain_ffn))
        gate_act = dora_proj(normed_f, gateup_frozen[0], ag[0], bg[0], mg[0])
        up_act = dora_proj(normed_f, gateup_frozen[1], ag[1], bg[1], mg[1])
        hidden = low(jax.nn.silu(gate_act) * up_act)
        return middle + dora_proj(hidden, down_frozen, ad, bd, md)
    adapters = (to_wide(a_qkv), to_wide(b_qkv), m_qkv, to_wide(a_out), to_wide(b_out), m_out, to_wide(a_gateup), to_wide(b_gateup), m_gateup, to_wide(a_down), to_wide(b_down), m_down)
    result, pullback = jax.vjp(forward, to_wide(layer_in), adapters)
    valid_mask = (positions[None, :] < total_len - pad_counts[:, None]).astype(jnp.float32)
    grad_input, grad_adapters = pullback(to_wide(cotangent) * valid_mask[:, :, None])
    return (result.astype(jnp.bfloat16), grad_input, grad_adapters[0], grad_adapters[1], grad_adapters[2], grad_adapters[3], grad_adapters[4], grad_adapters[5], grad_adapters[6], grad_adapters[7], grad_adapters[8], grad_adapters[9], grad_adapters[10], grad_adapters[11])
```

```python
from functools import partial
import math

import jax
import jax.numpy as jnp
from jax import lax
from jax.experimental import pallas as pl
from jax.experimental.pallas import tpu as pltpu
from jax.sharding import PartitionSpec as P

HEAD_DIM = 128
LANES = 128
epsilon = 1e-05
adapter_scale = 2.0
rope_base = 10000.0
f32 = jnp.float32
bf16 = jnp.bfloat16
PIECES = (0, 2, 1, 3)
score_block = 256
NT = (((1,), (1,)), ((), ()))
NN = (((1,), (0,)), ((), ()))
TN = (((0,), (0,)), ((), ()))


def mm(a, b, dims=NN):
    return lax.dot_general(a, b, dims, preferred_element_type=f32)


def swap(values, bit):
    size = lax.axis_size("tensor")
    return lax.ppermute(values, "tensor", [(i, i ^ bit) for i in range(size)])


def gather_pieces(shard):
    far = swap(shard, 2)
    near = swap(shard, 1)
    both = swap(far, 1)
    return jnp.stack([shard, far, near, both])


def scatter_pieces(partial_sums):
    got = swap(partial_sums[2:4], 1)
    keep = partial_sums[0:2].astype(f32) + got.astype(f32)
    return keep[0] + swap(keep[1].astype(bf16), 2).astype(f32)


def tensor_sum(values):
    return values + swap(values, 1) + swap(values, 2) + swap(values, 3)


def exchange(values):
    return lax.all_to_all(values, "seq", 0, 0, tiled=True)


def seq_gather(values):
    size = lax.axis_size("seq")
    return exchange(jnp.broadcast_to(values[None], (size,) + values.shape))


def column_prep_kernel(w_ref, a_ref, b_ref, m_ref, out_ref, stat_ref, cross_ref):
    w, a, b = w_ref[0], a_ref[0], b_ref[0]
    heading = w.astype(f32) + adapter_scale * mm(a, b)
    square = jnp.sum(heading * heading, axis=0, keepdims=True)
    norm = jnp.sqrt(square)
    scale = m_ref[0] / norm
    scaled = (heading * scale).astype(bf16)
    out_ref[0] = scaled
    stat_ref[0] = jnp.concatenate([norm, scale], axis=0)
    cross_ref[0] = mm(a, scaled, TN)


def column_prep(weight, down, up, magnitude, block, interleave):
    members, width, out = weight.shape
    rank = down.shape[2]
    if interleave:
        scaled_shape = (1, width, members * out)
        scaled_map = lambda i, j: (0, 0, i * members + j)
    else:
        scaled_shape = (members, width, out)
        scaled_map = lambda i, j: (j, 0, i)
    return pl.pallas_call(
        column_prep_kernel,
        grid=(out // block, members),
        in_specs=[
            pl.BlockSpec((1, width, block), lambda i, j: (j, 0, i)),
            pl.BlockSpec((1, width, rank), lambda i, j: (j, 0, 0)),
            pl.BlockSpec((1, rank, block), lambda i, j: (j, 0, i)),
            pl.BlockSpec((1, 1, block), lambda i, j: (j, 0, i)),
        ],
        out_specs=[
            pl.BlockSpec((1, width, block), scaled_map),
            pl.BlockSpec((1, 2, block), lambda i, j: (j, 0, i)),
            pl.BlockSpec((1, rank, block), lambda i, j: (j, 0, i)),
        ],
        out_shape=[
            jax.ShapeDtypeStruct(scaled_shape, bf16),
            jax.ShapeDtypeStruct((members, 2, out), f32),
            jax.ShapeDtypeStruct((members, rank, out), f32),
        ],
        cost_estimate=pl.CostEstimate(
            flops=2 * members * width * out * 256, bytes_accessed=4 * members * width * out, transcendentals=0
        ),
        name="column_prep",
    )(weight, down, up, magnitude[:, None, :])


def row_prep_kernel(w_ref, a_ref, b_ref, out_ref, stat_ref):
    w, a, b = w_ref[...], a_ref[...], b_ref[...]
    heading = w.astype(f32) + adapter_scale * mm(a, b)
    narrow = heading.astype(bf16)
    out_ref[...] = narrow
    square = jnp.sum(heading * heading, axis=0, keepdims=True)
    stat_ref[...] = jnp.concatenate([mm(a, narrow, TN), jnp.broadcast_to(square, (8, square.shape[1]))], axis=0)


def row_prep(weight, down, up, block):
    rows, out = weight.shape
    rank = down.shape[1]
    return pl.pallas_call(
        row_prep_kernel,
        grid=(out // block,),
        in_specs=[
            pl.BlockSpec((rows, block), lambda i: (0, i)),
            pl.BlockSpec((rows, rank), lambda i: (0, 0)),
            pl.BlockSpec((rank, block), lambda i: (0, i)),
        ],
        out_specs=[
            pl.BlockSpec((rows, block), lambda i: (0, i)),
            pl.BlockSpec((rank + 8, block), lambda i: (0, i)),
        ],
        out_shape=[
            jax.ShapeDtypeStruct((rows, out), bf16),
            jax.ShapeDtypeStruct((rank + 8, out), f32),
        ],
        cost_estimate=pl.CostEstimate(flops=2 * rows * out * 256, bytes_accessed=4 * rows * out, transcendentals=0),
        name="row_prep",
    )(weight, down, up)


def turn_forward(values, cosine, signed_sine):
    return values * cosine + pltpu.roll(values, values.shape[1] // 2, 1) * signed_sine


def turn_backward(values, cosine, signed_sine):
    return values * cosine + pltpu.roll(values * signed_sine, values.shape[1] // 2, 1)


def over_blocks(total, block, body):
    if total // block <= 4:
        for i in range(total // block):
            body(i * block, (i + 1) * block)
    else:

        def step(i, carry):
            body(pl.multiple_of(i * block, block), total)
            return carry

        lax.fori_loop(0, total // block, step, 0)


def weights_t(keys, queries, kpos, qpos, qstart, scale):
    scores = mm(keys, queries, NT)
    allowed = jnp.logical_and(kpos <= qpos, kpos >= qstart)
    return jnp.where(allowed, jnp.exp(scores * scale), 0.0)


def attend_kernel(x_ref, cos_ref, sin_ref, kpos_ref, qinfo_ref, o_ref, l_ref, qs, ks, vt, os, *, scale, block):
    blocks, _, _, group, size = x_ref.shape
    total = blocks * group
    cosine, signed_sine = cos_ref[...], sin_ref[...]
    qs[...] = turn_forward(x_ref[:, 0, 0].reshape(total, size).astype(f32), cosine, signed_sine).astype(bf16)
    ks[...] = turn_forward(x_ref[:, 0, 1].reshape(total, size).astype(f32), cosine, signed_sine).astype(bf16)
    vt[...] = x_ref[:, 0, 2].reshape(total, size).astype(f32).T.astype(bf16)

    def body(first, last):
        at = pl.ds(first, block)
        weights = weights_t(
            ks[:last], qs[at, :], kpos_ref[:last], qinfo_ref[0, 0:1, at], qinfo_ref[0, 1:2, at], scale
        )
        totals = jnp.sum(weights, axis=0, keepdims=True)
        outer = mm(vt[:, :last], weights.astype(bf16))
        l_ref[0, 0:1, at] = totals
        os[at, :] = (outer / totals).T.astype(bf16)

    over_blocks(total, block, body)
    o_ref[:, 0] = os[...].reshape(blocks, group, size)


def attend(pairs, tables, kpos, qinfo):
    blocks, slots, _, group, size = pairs.shape
    total = blocks * group
    block = math.gcd(total, score_block)
    return pl.pallas_call(
        partial(attend_kernel, scale=1.0 / math.sqrt(size), block=block),
        grid=(slots,),
        in_specs=[
            pl.BlockSpec((blocks, 1, 3, group, size), lambda n: (0, n, 0, 0, 0)),
            pl.BlockSpec((total, size), lambda n: (0, 0)),
            pl.BlockSpec((total, size), lambda n: (0, 0)),
            pl.BlockSpec((total, 1), lambda n: (0, 0)),
            pl.BlockSpec((1, 2, total), lambda n: (n, 0, 0)),
        ],
        out_specs=[
            pl.BlockSpec((blocks, 1, group, size), lambda n: (0, n, 0, 0)),
            pl.BlockSpec((1, 1, total), lambda n: (n, 0, 0)),
        ],
        out_shape=[
            jax.ShapeDtypeStruct((blocks, slots, group, size), bf16),
            jax.ShapeDtypeStruct((slots, 1, total), f32),
        ],
        scratch_shapes=[
            pltpu.VMEM((total, size), bf16),
            pltpu.VMEM((total, size), bf16),
            pltpu.VMEM((size, total), bf16),
            pltpu.VMEM((total, size), bf16),
        ],
        cost_estimate=pl.CostEstimate(
            flops=slots * 4 * total * total * size,
            bytes_accessed=slots * total * size * 8,
            transcendentals=slots * total * total // 2,
        ),
        name="attend",
    )(pairs, *tables, kpos, qinfo)


def attend_back_kernel(
    x_ref, o_ref, d_ref, l_ref, cos_ref, sin_ref, kpos_ref, qinfo_ref, g_ref, s_ref,
    qs, ks, kt, vs, dk, dv, dq, *, scale, block
):
    blocks, _, _, group, size = x_ref.shape
    total = blocks * group
    cosine, signed_sine = cos_ref[...], sin_ref[...]
    plain = [x_ref[:, 0, j].reshape(total, size).astype(f32) for j in range(3)]
    qs[...] = turn_forward(plain[0], cosine, signed_sine).astype(bf16)
    turned = turn_forward(plain[1], cosine, signed_sine)
    ks[...] = turned.astype(bf16)
    kt[...] = turned.T.astype(bf16)
    vs[...] = plain[2].astype(bf16)
    dk[...] = jnp.zeros_like(dk)
    dv[...] = jnp.zeros_like(dv)

    def body(first, last):
        at = pl.ds(first, block)
        span = block // group
        rows = pl.ds(first // group, span)
        weights = weights_t(
            ks[:last], qs[at, :], kpos_ref[:last], qinfo_ref[0, 0:1, at], qinfo_ref[0, 1:2, at], scale
        )
        totals = l_ref[0, 0:1, at]
        grad_t = d_ref[rows, 0].reshape(block, size).astype(f32).T
        out_t = o_ref[rows, 0].reshape(block, size).astype(f32).T
        dlog = -jnp.sum(grad_t * out_t, axis=0, keepdims=True) / totals
        outer_t = (grad_t / totals).astype(bf16)
        dweights = mm(vs[:last], outer_t)
        dscores = (weights * (dweights + dlog)).astype(bf16)
        dk[:last] += mm(dscores, qs[at, :])
        dv[:last] += mm(weights.astype(bf16), outer_t, NT)
        dq[at, :] = mm(kt[:, :last], dscores).T

    over_blocks(total, block, body)
    grads = (
        turn_backward(dq[...] * scale, cosine, signed_sine),
        turn_backward(dk[...] * scale, cosine, signed_sine),
        dv[...],
    )
    sums = []
    for j in range(3):
        g_ref[:, 0, j] = grads[j].astype(bf16).reshape(blocks, group, size)
        sums.append(jnp.sum(grads[j] * plain[j], axis=0, keepdims=True))
    s_ref[0] = jnp.concatenate(sums, axis=0)


def attend_back(pairs, outputs, grads, totals, tables, kpos, qinfo):
    blocks, slots, _, group, size = pairs.shape
    total = blocks * group
    block = math.gcd(total, score_block)
    half = pl.BlockSpec((blocks, 1, group, size), lambda n: (0, n, 0, 0))
    whole = pl.BlockSpec((blocks, 1, 3, group, size), lambda n: (0, n, 0, 0, 0))
    return pl.pallas_call(
        partial(attend_back_kernel, scale=1.0 / math.sqrt(size), block=block),
        grid=(slots,),
        in_specs=[
            whole,
            half,
            half,
            pl.BlockSpec((1, 1, total), lambda n: (n, 0, 0)),
            pl.BlockSpec((total, size), lambda n: (0, 0)),
            pl.BlockSpec((total, size), lambda n: (0, 0)),
            pl.BlockSpec((total, 1), lambda n: (0, 0)),
            pl.BlockSpec((1, 2, total), lambda n: (n, 0, 0)),
        ],
        out_specs=[whole, pl.BlockSpec((1, 3, size), lambda n: (n, 0, 0))],
        out_shape=[
            jax.ShapeDtypeStruct(pairs.shape, bf16),
            jax.ShapeDtypeStruct((slots, 3, size), f32),
        ],
        scratch_shapes=[
            pltpu.VMEM((total, size), bf16),
            pltpu.VMEM((total, size), bf16),
            pltpu.VMEM((size, total), bf16),
            pltpu.VMEM((total, size), bf16),
            pltpu.VMEM((total, size), f32),
            pltpu.VMEM((total, size), f32),
            pltpu.VMEM((total, size), f32),
        ],
        cost_estimate=pl.CostEstimate(
            flops=slots * 10 * total * total * size,
            bytes_accessed=slots * total * size * 16,
            transcendentals=slots * total * total // 2,
        ),
        name="attend_back",
    )(pairs, outputs, grads, totals, *tables, kpos, qinfo)


def gated_kernel(x_ref, w_ref, e_ref, hidden_ref, grads_ref, sums_ref):
    both = mm(x_ref[...], w_ref[0])
    width = both.shape[1] // 2
    gate, up = both[:, :width], both[:, width:]
    dhid = e_ref[...].astype(f32)
    sig = 1.0 / (1.0 + jnp.exp(-gate))
    act = gate * sig
    hidden_ref[...] = (act * up).astype(bf16)
    dgate = dhid * up * (sig * (1.0 + gate * (1.0 - sig)))
    dup = dhid * act
    grads_ref[:, :width] = dgate.astype(bf16)
    grads_ref[:, width:] = dup.astype(bf16)
    sums_ref[...] = jnp.concatenate(
        [jnp.sum(gate * dgate, axis=0, keepdims=True), jnp.sum(up * dup, axis=0, keepdims=True)], axis=1
    )


def gated(rows, weight, dhid, block):
    count, width = rows.shape
    out = dhid.shape[1]
    return pl.pallas_call(
        gated_kernel,
        grid=(out // block,),
        in_specs=[
            pl.BlockSpec((count, width), lambda i: (0, 0)),
            pl.BlockSpec((1, width, 2 * block), lambda i: (0, 0, i)),
            pl.BlockSpec((count, block), lambda i: (0, i)),
        ],
        out_specs=[
            pl.BlockSpec((count, block), lambda i: (0, i)),
            pl.BlockSpec((count, 2 * block), lambda i: (0, i)),
            pl.BlockSpec((1, 2 * block), lambda i: (0, i)),
        ],
        out_shape=[
            jax.ShapeDtypeStruct((count, out), bf16),
            jax.ShapeDtypeStruct((count, 2 * out), bf16),
            jax.ShapeDtypeStruct((1, 2 * out), f32),
        ],
        cost_estimate=pl.CostEstimate(
            flops=4 * count * width * out,
            bytes_accessed=4 * width * out + 2 * count * (width + 4 * out),
            transcendentals=count * out,
        ),
        name="gated",
    )(rows, weight, dhid)


def norm_scale(values):
    return lax.rsqrt(jnp.mean(values * values, axis=-1, keepdims=True) + epsilon)


def norm_back(values, gain, grad):
    r = norm_scale(values)
    weighted = gain * grad
    return r * weighted - values * (r * r * r) * jnp.mean(values * weighted, axis=-1, keepdims=True)


def rotary_tables(positions, head_size):
    half_size = head_size // 2
    frequency = rope_base ** (-(2.0 * jnp.arange(half_size, dtype=f32)) / head_size)
    angles = positions.astype(f32)[:, None] * frequency[None, :]
    cosine, sine = jnp.cos(angles), jnp.sin(angles)
    return (jnp.concatenate([cosine, cosine], axis=-1), jnp.concatenate([-sine, sine], axis=-1))


def interleaved(values, block):
    lead, out = values.shape[:-2], values.shape[-1]
    parts = values.reshape(lead + (2, out // block, block))
    return jnp.swapaxes(parts, -3, -2).reshape(lead + (2 * out,))


def separated(values, block):
    lead, both = values.shape[:-1], values.shape[-1]
    parts = values.reshape(lead + (both // (2 * block), 2, block))
    return jnp.swapaxes(parts, -3, -2).reshape(lead + (2, both // 2))


def block_diagonal(values):
    members, rank, out = values.shape
    eye = jnp.eye(members, dtype=values.dtype)
    return (eye[:, None, :, None] * values[:, :, None, :]).reshape(members * rank, members * out)


def local(
    layer_in, cotangent, doc_lengths, pad_counts, gain_attn, gain_ffn, w_qkv, a_qkv, b_qkv, m_qkv, w_out, a_out,
    b_out, m_out, w_gateup, a_gateup, b_gateup, m_gateup, w_down, a_down, b_down, m_down,
):
    rows, quarter, width = layer_in.shape
    tensor, seq = lax.axis_size("tensor"), lax.axis_size("seq")
    assert tensor == len(PIECES)
    me_t, me_s = lax.axis_index("tensor"), lax.axis_index("seq")
    group = quarter * tensor
    total = group * seq
    feat = w_qkv.shape[2]
    heads = feat // HEAD_DIM
    rank = a_qkv.shape[2]
    ff = w_down.shape[0]
    tokens = group * rows
    ff_block = LANES
    pair_count = rows * heads
    slots = -(-pair_count // seq)

    piece_of = jnp.bitwise_xor(me_t, jnp.array(PIECES, jnp.int32))
    in_block = (piece_of[:, None] * quarter + jnp.arange(quarter, dtype=jnp.int32)[None, :]).reshape(group)
    positions = (jnp.arange(seq, dtype=jnp.int32)[:, None] * group + in_block[None, :]).reshape(total)
    tables = rotary_tables(positions, HEAD_DIM)
    offsets = jnp.cumsum(doc_lengths, axis=1)
    starts = jnp.max(
        jnp.where(offsets[:, :, None] <= positions[None, None, :], offsets[:, :, None], 0), axis=1
    )
    my_rows = jnp.minimum((me_s * slots + jnp.arange(slots)) // heads, rows - 1)
    row_choice = (my_rows[:, None] == jnp.arange(rows)[None, :])[:, :, None]
    my_starts = jnp.sum(jnp.where(row_choice, starts[None], 0), axis=1)
    qinfo = jnp.stack([jnp.broadcast_to(positions[None], (slots, total)), my_starts], axis=1)
    kpos = positions[:, None]

    def to_pairs(values, parts):
        laid = values.reshape(tensor, rows, quarter, parts, heads, HEAD_DIM).transpose(1, 4, 3, 0, 2, 5)
        laid = laid.reshape(pair_count, parts, group, HEAD_DIM)
        if slots * seq > pair_count:
            laid = jnp.pad(laid, ((0, slots * seq - pair_count), (0, 0), (0, 0), (0, 0)))
        return exchange(laid.reshape(seq, slots, parts, group, HEAD_DIM))

    def from_pairs(values, parts):
        laid = exchange(values).reshape(seq * slots, parts, group, HEAD_DIM)[:pair_count]
        laid = laid.reshape(rows, heads, parts, tensor, quarter, HEAD_DIM).transpose(3, 0, 4, 2, 1, 5)
        return laid.reshape(tokens, parts * heads * HEAD_DIM)

    def gathered(shard):
        return gather_pieces(shard).reshape(tokens, width)

    def scattered(partial_sums):
        return scatter_pieces(partial_sums.astype(bf16).reshape(tensor, rows, quarter, -1))

    wide_in = layer_in.astype(f32)
    normed_a = gathered((wide_in * norm_scale(wide_in) * gain_attn).astype(bf16))

    down_w, down_stat = row_prep(w_down, a_down, b_down, 256)
    qkv_w, qkv_stat, qkv_cross = column_prep(w_qkv, a_qkv, b_qkv, m_qkv, 256, False)
    out_w, out_stat = row_prep(w_out, a_out, b_out, 512)
    gu_w, gu_stat, gu_cross = column_prep(w_gateup, a_gateup, b_gateup, m_gateup, ff_block, True)
    squares = tensor_sum(jnp.stack([down_stat[rank], out_stat[rank]]))
    down_scale, out_scale = m_down / jnp.sqrt(squares[0]), m_out / jnp.sqrt(squares[1])

    owned = me_s * group + me_t * quarter + jnp.arange(quarter, dtype=jnp.int32)
    valid = (owned[None, :] < total - pad_counts[:, None]).astype(f32)
    cot = cotangent.astype(f32) * valid[:, :, None]
    du_down = gathered((cot * down_scale).astype(bf16))
    dhid = mm(du_down, down_w, NT).astype(bf16)
    dt_down = (adapter_scale * mm(du_down, b_down, NT)).astype(bf16)

    qkv_rows = jnp.concatenate([mm(normed_a, qkv_w[j]).astype(bf16) for j in range(3)], axis=1)
    pairs = to_pairs(qkv_rows, 3)
    outputs, totals = attend(pairs, tables, kpos, qinfo)
    att = from_pairs(outputs[:, :, None], 1)
    u_out = scattered(mm(att, out_w)) * out_scale
    middle = wide_in + u_out

    normed_f = gathered((middle * norm_scale(middle) * gain_ffn).astype(bf16))
    hidden, d_gu, gu_sum = gated(normed_f, gu_w, dhid, ff_block)
    grad_norm_f = scattered(mm(d_gu, gu_w[0], NT))
    d_mid = cot + norm_back(middle, gain_ffn, grad_norm_f)
    du_out = gathered((d_mid * out_scale).astype(bf16))
    d_att = mm(du_out, out_w, NT).astype(bf16)

    d_pairs, pair_sums = attend_back(
        pairs, outputs, to_pairs(d_att, 1)[:, :, 0], totals, tables, kpos, qinfo
    )
    d_qkv = from_pairs(d_pairs, 3)
    grad_norm_a = scattered(sum(mm(d_qkv[:, j * feat:(j + 1) * feat], qkv_w[j], NT) for j in range(3)))
    grad_in = d_mid + norm_back(wide_in, gain_attn, grad_norm_a)

    u_down = scattered(mm(hidden, down_w)) * down_scale
    layer_out = (middle + u_down).astype(bf16)

    row_sums = tensor_sum(
        jnp.stack([jnp.sum(u_down * cot, axis=(0, 1)), jnp.sum(u_out * d_mid, axis=(0, 1))])
    )
    down_sum, out_sum = row_sums[0], row_sums[1]
    gu_sums = separated(gu_sum[0], ff_block)
    my_heads = (me_s * slots + jnp.arange(slots)) % heads
    live = me_s * slots + jnp.arange(slots) < pair_count
    head_choice = jnp.logical_and(my_heads[:, None] == jnp.arange(heads)[None, :], live[:, None])
    qkv_sums = jnp.sum(
        jnp.where(head_choice[:, None, :, None], pair_sums[:, :, None, :], 0.0), axis=0
    ).reshape(3, feat)

    def column_grads(rows_in, grads, weight, down, up_cat, scale_cat, coef_cat, cross_cat, members):
        t = mm(rows_in, down.transpose(1, 0, 2).reshape(width, members * rank)).astype(bf16)
        grad_b = adapter_scale * (mm(t, grads, TN) * scale_cat + coef_cat * cross_cat)
        dt = mm(grads, (adapter_scale * up_cat * scale_cat).astype(bf16), NT).astype(bf16)
        grad_a = mm(dt, rows_in, TN) + adapter_scale * mm((coef_cat * up_cat).astype(bf16), weight, NT)
        return grad_a, grad_b

    qkv_cat = lambda v: block_diagonal(v)
    gu_cat = lambda v: interleaved(
        block_diagonal(v).reshape(2 * rank, 2, ff), ff_block
    )
    qkv_coef = -qkv_sums / (m_qkv * qkv_stat[:, 0])
    gu_coef = -gu_sums / (m_gateup * gu_stat[:, 0])
    qkv_flat = qkv_w.transpose(1, 0, 2).reshape(width, 3 * feat)
    grad_a_qkv, grad_b_qkv = column_grads(
        normed_a, d_qkv, qkv_flat, a_qkv, qkv_cat(b_qkv.astype(f32)), qkv_stat[:, 1].reshape(-1),
        qkv_coef.reshape(-1), qkv_cat(qkv_cross), 3,
    )
    grad_b_qkv = jnp.stack(
        [grad_b_qkv[j * rank:(j + 1) * rank, j * feat:(j + 1) * feat] for j in range(3)]
    )
    grad_a_gu, grad_b_gu = column_grads(
        normed_f, d_gu, gu_w[0], a_gateup, gu_cat(b_gateup.astype(f32)), interleaved(gu_stat[:, 1], ff_block),
        interleaved(gu_coef, ff_block), gu_cat(gu_cross), 2,
    )
    grad_b_gu = separated(grad_b_gu, ff_block)
    grad_b_gu = jnp.stack([grad_b_gu[j * rank:(j + 1) * rank, j] for j in range(2)])

    def row_grads(rows_in, grads, dt, weight, down, up, square, stat, sums):
        coef = -sums / square
        t = mm(rows_in, down).astype(bf16)
        grad_b = adapter_scale * (mm(t, grads, TN) + coef * stat[:rank])
        grad_a = mm(dt, rows_in, TN) + adapter_scale * mm((coef * up.astype(f32)).astype(bf16), weight, NT)
        return grad_a, grad_b

    grad_a_out, grad_b_out = row_grads(
        att, du_out, (adapter_scale * mm(du_out, b_out, NT)).astype(bf16), out_w, a_out, b_out, squares[1], out_stat,
        out_sum,
    )
    grad_a_down, grad_b_down = row_grads(
        hidden, du_down, dt_down, down_w, a_down, b_down, squares[0], down_stat, down_sum
    )

    def reduce_all(over_all, over_seq):
        def packed(parts):
            flat = jnp.concatenate([p.astype(bf16).reshape(-1, LANES) for p in parts])
            return flat

        everything, lone = packed(over_all), packed(over_seq)
        unit = seq * 8
        pads = [(-len(v)) % unit for v in (everything, lone)]
        everything, lone = [
            jnp.pad(v, ((0, p), (0, 0))).reshape(seq, -1, LANES) for v, p in zip((everything, lone), pads)
        ]
        cut = everything.shape[1]
        mine = jnp.sum(exchange(jnp.concatenate([everything, lone], axis=1)).astype(f32), axis=0)
        shared = tensor_sum(mine[:cut].astype(bf16).astype(f32))
        back = seq_gather(jnp.concatenate([shared.astype(bf16), mine[cut:].astype(bf16)]))
        found = []
        for parts, values in ((over_all, back[:, :cut]), (over_seq, back[:, cut:])):
            flat, at = values.reshape(-1, LANES).astype(f32), 0
            for p in parts:
                count = p.size // LANES
                found.append(flat[at:at + count].reshape(p.shape))
                at += count
        return found

    (g_a_gu, g_b_out, g_b_down, g_b_gu, g_a_out, g_a_down, s_gu, s_out, s_down) = reduce_all(
        [grad_a_gu, grad_b_out, grad_b_down], [grad_b_gu, grad_a_out, grad_a_down, gu_sums, out_sum, down_sum]
    )
    g_a_qkv, g_b_qkv, s_qkv = reduce_all([grad_a_qkv], [grad_b_qkv, qkv_sums])
    return (
        layer_out,
        grad_in,
        g_a_qkv.reshape(3, rank, width).transpose(0, 2, 1),
        g_b_qkv,
        s_qkv / m_qkv,
        g_a_out.T,
        g_b_out,
        s_out / m_out,
        g_a_gu.reshape(2, rank, width).transpose(0, 2, 1),
        g_b_gu,
        s_gu / m_gateup,
        g_a_down.T,
        g_b_down,
        s_down / m_down,
    )


def solution(mesh):
    split = P(None, ("seq", "tensor"), None)
    in_specs = (
        split, split, P(), P(), P(), P(),
        P(None, None, "tensor"), P(), P(None, None, "tensor"), P(None, "tensor"),
        P("tensor", None), P("tensor", None), P(), P(),
        P(None, None, "tensor"), P(), P(None, None, "tensor"), P(None, "tensor"),
        P("tensor", None), P("tensor", None), P(), P(),
    )
    out_specs = (
        split, split,
        P(), P(None, None, "tensor"), P(None, "tensor"),
        P("tensor", None), P(), P(),
        P(), P(None, None, "tensor"), P(None, "tensor"),
        P("tensor", None), P(), P(),
    )
    return jax.shard_map(local, mesh=mesh, in_specs=in_specs, out_specs=out_specs, check_vma=False)
```

```python
from functools import partial
import math

import jax
import jax.numpy as jnp
from jax import lax
from jax.experimental import pallas as pl
from jax.experimental.pallas import tpu as pltpu
from jax.sharding import PartitionSpec as P

HEAD_DIM = 128
LANES = 128
epsilon = 1e-05
adapter_scale = 2.0
rope_base = 10000.0
f32 = jnp.float32
bf16 = jnp.bfloat16
PIECES = (0, 2, 1, 3)
score_block = 256
GATED_BLOCKS = 2
NT = (((1,), (1,)), ((), ()))
NN = (((1,), (0,)), ((), ()))
TN = (((0,), (0,)), ((), ()))


def cost(flops, bytes_accessed, transcendentals):
    return pl.CostEstimate(flops=flops // 64, bytes_accessed=bytes_accessed // 64, transcendentals=0)


def mm(a, b, dims=NN):
    return lax.dot_general(a, b, dims, preferred_element_type=f32)


def swap(values, bit):
    size = lax.axis_size("tensor")
    return lax.ppermute(values, "tensor", [(i, i ^ bit) for i in range(size)])


def gather_start(shard):
    return shard, swap(shard, 2), swap(shard, 1)


def gather_end(shard, far, near):
    return [shard, far, near, swap(far, 1)]


def scatter_start(kept, near, send):
    got = swap(send, 1)
    return kept, got, (near.astype(f32) + got[1].astype(f32)).astype(bf16)


def scatter_end(kept, got, passed):
    return kept.astype(f32) + got[0].astype(f32) + swap(passed, 2).astype(f32)


def after(value, *others):
    return lax.optimization_barrier((value, *others))


def tensor_sum(values):
    return values + swap(values, 1) + swap(values, 2) + swap(values, 3)


def exchange(values):
    return lax.all_to_all(values, "seq", 0, 0, tiled=True)


def seq_gather(values):
    size = lax.axis_size("seq")
    return exchange(jnp.broadcast_to(values[None], (size,) + values.shape))


def column_prep_kernel(w_ref, a_ref, b_ref, m_ref, out_ref, stat_ref, cross_ref):
    members, width, block = w_ref.shape
    rank = cross_ref.shape[1]
    product = mm(a_ref[...], b_ref[0], TN)
    i = pl.program_id(0)
    for j in range(members):
        heading = w_ref[j].astype(f32) + adapter_scale * product[:, j * block:(j + 1) * block]
        norm = jnp.sqrt(jnp.sum(heading * heading, axis=0, keepdims=True))
        scale = m_ref[j] / norm
        scaled = (heading * scale).astype(bf16)
        if out_ref.shape[1] == members * block:
            out_ref[:, j * block:(j + 1) * block] = scaled
        else:
            out_ref[:, pl.ds(pl.multiple_of(j * (out_ref.shape[1] // members) + i * block, block), block)] = scaled
        stat_ref[j] = jnp.concatenate([norm, scale], axis=0)
        cross_ref[j] = mm(a_ref[j * rank:(j + 1) * rank, :], scaled)


def column_prep(weight, down, up, magnitude, block, alternate):
    members, width, out = weight.shape
    rank = down.shape[2]
    wide = members * block
    eye = jnp.eye(members, dtype=bf16)[:, None, None, :, None]
    blocks = up.reshape(members, rank, out // block, 1, block) * eye
    blocks = blocks.transpose(2, 0, 1, 3, 4).reshape(out // block, members * rank, wide)
    flat = down.transpose(0, 2, 1).reshape(members * rank, width)
    if alternate:
        scaled_spec = pl.BlockSpec((width, wide), lambda i: (0, i))
    else:
        scaled_spec = pl.BlockSpec((width, members * out), lambda i: (0, 0))
    return pl.pallas_call(
        column_prep_kernel,
        grid=(out // block,),
        in_specs=[
            pl.BlockSpec((members, width, block), lambda i: (0, 0, i)),
            pl.BlockSpec((members * rank, width), lambda i: (0, 0)),
            pl.BlockSpec((1, members * rank, wide), lambda i: (i, 0, 0)),
            pl.BlockSpec((members, 1, block), lambda i: (0, 0, i)),
        ],
        out_specs=[
            scaled_spec,
            pl.BlockSpec((members, 2, block), lambda i: (0, 0, i)),
            pl.BlockSpec((members, rank, block), lambda i: (0, 0, i)),
        ],
        out_shape=[
            jax.ShapeDtypeStruct((width, members * out), bf16),
            jax.ShapeDtypeStruct((members, 2, out), f32),
            jax.ShapeDtypeStruct((members, rank, out), f32),
        ],
        cost_estimate=cost(
            flops=4 * members * width * out * 256, bytes_accessed=4 * members * width * out, transcendentals=0
        ),
        name="column_prep",
    )(weight, flat, blocks, magnitude[:, None, :])


def row_prep_kernel(w_ref, a_ref, b_ref, out_ref, cross_ref, square_ref):
    heading = w_ref[...].astype(f32) + adapter_scale * mm(a_ref[...], b_ref[...], TN)
    narrow = heading.astype(bf16)
    out_ref[...] = narrow
    cross_ref[...] = mm(a_ref[...], narrow)
    square_ref[...] = jnp.sum(heading * heading, axis=0, keepdims=True)


def row_prep(weight, down, up, block):
    rows, out = weight.shape
    rank = down.shape[1]
    along = lambda n: pl.BlockSpec((n, block), lambda i: (0, i))
    return pl.pallas_call(
        row_prep_kernel,
        grid=(out // block,),
        in_specs=[along(rows), pl.BlockSpec((rank, rows), lambda i: (0, 0)), along(rank)],
        out_specs=[along(rows), along(rank), along(1)],
        out_shape=[
            jax.ShapeDtypeStruct((rows, out), bf16),
            jax.ShapeDtypeStruct((rank, out), f32),
            jax.ShapeDtypeStruct((1, out), f32),
        ],
        cost_estimate=cost(flops=2 * rows * out * 256, bytes_accessed=4 * rows * out, transcendentals=0),
        name="row_prep",
    )(weight, down.T, up)


def turn_forward(values, cosine, signed_sine):
    return values * cosine + pltpu.roll(values, values.shape[1] // 2, 1) * signed_sine


def turn_backward(values, cosine, signed_sine):
    return values * cosine + pltpu.roll(values * signed_sine, values.shape[1] // 2, 1)


def over_blocks(total, block, body):
    if total // block <= 4:
        for i in range(total // block):
            body(i * block, (i + 1) * block)
    else:

        def step(i, carry):
            body(pl.multiple_of(i * block, block), total)
            return carry

        lax.fori_loop(0, total // block, step, 0)


def weights_t(keys, queries, kpos, qpos, qstart, scale):
    scores = mm(keys, queries, NT)
    allowed = jnp.logical_and(kpos <= qpos, kpos >= qstart)
    return jnp.where(allowed, jnp.exp(scores * scale), 0.0)


def attend_kernel(x_ref, cos_ref, sin_ref, kpos_ref, qinfo_ref, o_ref, l_ref, qs, ks, vt, os, *, scale, block):
    blocks, _, _, group, size = x_ref.shape
    total = blocks * group
    cosine, signed_sine = cos_ref[...], sin_ref[...]
    qs[...] = turn_forward(x_ref[:, 0, 0].reshape(total, size).astype(f32), cosine, signed_sine).astype(bf16)
    ks[...] = turn_forward(x_ref[:, 0, 1].reshape(total, size).astype(f32), cosine, signed_sine).astype(bf16)
    vt[...] = x_ref[:, 0, 2].reshape(total, size).astype(f32).T.astype(bf16)

    def body(first, last):
        at = pl.ds(first, block)
        weights = weights_t(
            ks[:last], qs[at, :], kpos_ref[:last], qinfo_ref[0, 0:1, at], qinfo_ref[0, 1:2, at], scale
        )
        totals = jnp.sum(weights, axis=0, keepdims=True)
        outer = mm(vt[:, :last], weights.astype(bf16))
        l_ref[0, 0:1, at] = totals
        os[at, :] = (outer / totals).T.astype(bf16)

    over_blocks(total, block, body)
    o_ref[:, 0] = os[...].reshape(blocks, group, size)


def attend(pairs, tables, kpos, qinfo):
    blocks, slots, _, group, size = pairs.shape
    total = blocks * group
    block = math.gcd(total, score_block)
    return pl.pallas_call(
        partial(attend_kernel, scale=1.0 / math.sqrt(size), block=block),
        grid=(slots,),
        in_specs=[
            pl.BlockSpec((blocks, 1, 3, group, size), lambda n: (0, n, 0, 0, 0)),
            pl.BlockSpec((total, size), lambda n: (0, 0)),
            pl.BlockSpec((total, size), lambda n: (0, 0)),
            pl.BlockSpec((total, 1), lambda n: (0, 0)),
            pl.BlockSpec((1, 2, total), lambda n: (n, 0, 0)),
        ],
        out_specs=[
            pl.BlockSpec((blocks, 1, group, size), lambda n: (0, n, 0, 0)),
            pl.BlockSpec((1, 1, total), lambda n: (n, 0, 0)),
        ],
        out_shape=[
            jax.ShapeDtypeStruct((blocks, slots, group, size), bf16),
            jax.ShapeDtypeStruct((slots, 1, total), f32),
        ],
        scratch_shapes=[
            pltpu.VMEM((total, size), bf16),
            pltpu.VMEM((total, size), bf16),
            pltpu.VMEM((size, total), bf16),
            pltpu.VMEM((total, size), bf16),
        ],
        cost_estimate=cost(
            flops=slots * 4 * total * total * size,
            bytes_accessed=slots * total * size * 8,
            transcendentals=slots * total * total // 2,
        ),
        name="attend",
    )(pairs, *tables, kpos, qinfo)


def attend_back_kernel(
    x_ref, o_ref, d_ref, l_ref, cos_ref, sin_ref, kpos_ref, qinfo_ref, g_ref, s_ref,
    qs, ks, kt, vs, dk, dv, dq, *, scale, block
):
    blocks, _, _, group, size = x_ref.shape
    total = blocks * group
    cosine, signed_sine = cos_ref[...], sin_ref[...]
    plain = [x_ref[:, 0, j].reshape(total, size).astype(f32) for j in range(3)]
    qs[...] = turn_forward(plain[0], cosine, signed_sine).astype(bf16)
    turned = turn_forward(plain[1], cosine, signed_sine)
    ks[...] = turned.astype(bf16)
    kt[...] = turned.T.astype(bf16)
    vs[...] = plain[2].astype(bf16)
    dk[...] = jnp.zeros_like(dk)
    dv[...] = jnp.zeros_like(dv)

    def body(first, last):
        at = pl.ds(first, block)
        span = block // group
        rows = pl.ds(first // group, span)
        weights = weights_t(
            ks[:last], qs[at, :], kpos_ref[:last], qinfo_ref[0, 0:1, at], qinfo_ref[0, 1:2, at], scale
        )
        totals = l_ref[0, 0:1, at]
        grad_t = d_ref[rows, 0].reshape(block, size).astype(f32).T
        out_t = o_ref[rows, 0].reshape(block, size).astype(f32).T
        dlog = -jnp.sum(grad_t * out_t, axis=0, keepdims=True) / totals
        outer_t = (grad_t / totals).astype(bf16)
        dweights = mm(vs[:last], outer_t)
        dscores = (weights * (dweights + dlog)).astype(bf16)
        dk[:last] += mm(dscores, qs[at, :])
        dv[:last] += mm(weights.astype(bf16), outer_t, NT)
        dq[at, :] = mm(kt[:, :last], dscores).T

    over_blocks(total, block, body)
    grads = (
        turn_backward(dq[...] * scale, cosine, signed_sine),
        turn_backward(dk[...] * scale, cosine, signed_sine),
        dv[...],
    )
    sums = []
    for j in range(3):
        g_ref[:, 0, j] = grads[j].astype(bf16).reshape(blocks, group, size)
        sums.append(jnp.sum(grads[j] * plain[j], axis=0, keepdims=True))
    s_ref[0] = jnp.concatenate(sums, axis=0)


def attend_back(pairs, outputs, grads, totals, tables, kpos, qinfo):
    blocks, slots, _, group, size = pairs.shape
    total = blocks * group
    block = math.gcd(total, score_block)
    half = pl.BlockSpec((blocks, 1, group, size), lambda n: (0, n, 0, 0))
    whole = pl.BlockSpec((blocks, 1, 3, group, size), lambda n: (0, n, 0, 0, 0))
    return pl.pallas_call(
        partial(attend_back_kernel, scale=1.0 / math.sqrt(size), block=block),
        grid=(slots,),
        in_specs=[
            whole,
            half,
            half,
            pl.BlockSpec((1, 1, total), lambda n: (n, 0, 0)),
            pl.BlockSpec((total, size), lambda n: (0, 0)),
            pl.BlockSpec((total, size), lambda n: (0, 0)),
            pl.BlockSpec((total, 1), lambda n: (0, 0)),
            pl.BlockSpec((1, 2, total), lambda n: (n, 0, 0)),
        ],
        out_specs=[whole, pl.BlockSpec((1, 3, size), lambda n: (n, 0, 0))],
        out_shape=[
            jax.ShapeDtypeStruct(pairs.shape, bf16),
            jax.ShapeDtypeStruct((slots, 3, size), f32),
        ],
        scratch_shapes=[
            pltpu.VMEM((total, size), bf16),
            pltpu.VMEM((total, size), bf16),
            pltpu.VMEM((size, total), bf16),
            pltpu.VMEM((total, size), bf16),
            pltpu.VMEM((total, size), f32),
            pltpu.VMEM((total, size), f32),
            pltpu.VMEM((total, size), f32),
        ],
        cost_estimate=cost(
            flops=slots * 10 * total * total * size,
            bytes_accessed=slots * total * size * 16,
            transcendentals=slots * total * total // 2,
        ),
        name="attend_back",
    )(pairs, outputs, grads, totals, *tables, kpos, qinfo)


def to_pairs_kernel(*refs, dims):
    x_refs, w_ref, out_ref, xs = refs[:4], refs[4], refs[5], refs[6]
    count = x_refs[0].shape[0]

    @pl.when(jnp.logical_and(pl.program_id(0) == 0, pl.program_id(1) == 0))
    def _():
        for i in range(4):
            xs[i * count:(i + 1) * count] = x_refs[i][...]

    rows, heads, _, pieces, quarter, size = out_ref.shape
    product = mm(xs[...], w_ref[...], dims).astype(bf16)
    for i in range(pieces):
        for r in range(rows):
            at = (i * rows + r) * quarter
            for h in range(heads):
                out_ref[r, h, 0, i] = product[at:at + quarter, h * size:(h + 1) * size]


def project_to_pairs(pieces, weight, dims, parts, heads, size, span):
    rows, quarter, width = pieces[0].shape
    count = rows * quarter
    wide = span * size
    steps = heads // span
    if dims == NN:
        w_spec = pl.BlockSpec((width, wide), lambda j, h: (0, j * steps + h))
    else:
        w_spec = pl.BlockSpec((wide, width), lambda j, h: (j * steps + h, 0))
    return pl.pallas_call(
        partial(to_pairs_kernel, dims=dims),
        grid=(parts, steps),
        in_specs=[pl.BlockSpec(memory_space=pltpu.VMEM)] * 4 + [w_spec],
        out_specs=[
            pl.BlockSpec((rows, span, 1, 4, quarter, size), lambda j, h: (0, h, j, 0, 0, 0)),
            pl.BlockSpec((4 * count, width), lambda j, h: (0, 0)),
        ],
        out_shape=[
            jax.ShapeDtypeStruct((rows, heads, parts, 4, quarter, size), bf16),
            jax.ShapeDtypeStruct((4 * count, width), bf16),
        ],
        cost_estimate=cost(
            flops=8 * count * width * parts * heads * size,
            bytes_accessed=2 * width * (8 * count + parts * heads * size),
            transcendentals=0,
        ),
        name="project_to_pairs",
    )(*[p.reshape(count, width) for p in pieces], weight)


def split_out(product, out_refs, at):
    kept_ref, near_ref, send_ref = out_refs
    half = product.shape[0] // 4
    kept_ref[at:at + half] = product[:half]
    near_ref[at:at + half] = product[half:2 * half]
    for i in range(2):
        send_ref[i, at:at + half] = product[(i + 2) * half:(i + 3) * half]


def split_specs(count, out, block):
    one, two = pl.BlockSpec((count, block), lambda n: (0, n)), pl.BlockSpec((2, count, block), lambda n: (0, 0, n))
    shapes = [(count, out), (count, out), (2, count, out)]
    return [one, one, two], [jax.ShapeDtypeStruct(v, bf16) for v in shapes]


def by_rows(kept, near, send, quarter):
    shape = (kept.shape[0] // quarter, quarter, kept.shape[1])
    return kept.reshape(shape), near.reshape(shape), send.reshape((2,) + shape)


def join_pairs(x_ref, flat_ref):
    rows, heads, parts, pieces, quarter, size = x_ref.shape
    for i in range(pieces):
        for r in range(rows):
            at = (i * rows + r) * quarter
            for j in range(parts):
                for h in range(heads):
                    col = (j * heads + h) * size
                    flat_ref[at:at + quarter, col:col + size] = x_ref[r, h, j, i]


def from_pairs_kernel(x_ref, w_ref, flat_ref, *out_refs):
    @pl.when(pl.program_id(0) == 0)
    def _():
        join_pairs(x_ref, flat_ref)

    split_out(mm(flat_ref[...], w_ref[...]).astype(bf16), out_refs, 0)


def project_from_pairs(pairs, weight, block):
    rows, heads, parts, pieces, quarter, size = pairs.shape
    count, width = rows * quarter, parts * heads * size
    out = weight.shape[1]
    specs, shapes = split_specs(count, out, block)
    flat, *split = pl.pallas_call(
        from_pairs_kernel,
        grid=(out // block,),
        in_specs=[pl.BlockSpec(pairs.shape, lambda n: (0,) * 6), pl.BlockSpec((width, block), lambda n: (0, n))],
        out_specs=[pl.BlockSpec((4 * count, width), lambda n: (0, 0))] + specs,
        out_shape=[jax.ShapeDtypeStruct((4 * count, width), bf16)] + shapes,
        cost_estimate=cost(
            flops=8 * count * width * out, bytes_accessed=2 * (out * width + 4 * count * (2 * width + out)),
            transcendentals=0,
        ),
        name="project_from_pairs",
    )(pairs, weight)
    return flat, by_rows(*split, quarter)


def project_split_kernel(*refs, dims):
    x_refs, w_ref, out_refs = refs[:-4], refs[-4], refs[-3:]
    at = 0
    for x_ref in x_refs:
        split_out(mm(x_ref[...], w_ref[...], dims).astype(bf16), out_refs, at)
        at += x_ref.shape[0] // 4


def project_split(flats, weight, dims, block, quarter):
    width = flats[0].shape[1]
    count = sum(v.shape[0] for v in flats) // 4
    if dims == NN:
        out = weight.shape[1]
        w_spec = pl.BlockSpec((width, block), lambda n: (0, n))
    else:
        out = weight.shape[0]
        w_spec = pl.BlockSpec((block, width), lambda n: (n, 0))
    specs, shapes = split_specs(count, out, block)
    split = pl.pallas_call(
        partial(project_split_kernel, dims=dims),
        grid=(out // block,),
        in_specs=[pl.BlockSpec(v.shape, lambda n: (0, 0)) for v in flats] + [w_spec],
        out_specs=specs,
        out_shape=shapes,
        cost_estimate=cost(
            flops=8 * count * width * out, bytes_accessed=2 * (out * width + 4 * count * (width + out)), transcendentals=0
        ),
        name="project_split",
    )(*flats, weight)
    return by_rows(*split, quarter)


def cotangent_kernel(*refs):
    x_refs, w_ref, out_ref, flat_ref = refs[:4], refs[4], refs[5], refs[6]
    part = x_refs[0].shape[0]
    for i in range(4):
        flat_ref[i * part:(i + 1) * part] = x_refs[i][...]
    out_ref[...] = mm(flat_ref[...], w_ref[...], NT).astype(bf16)


def project_cotangent(pieces, weight, rows, first):
    total, quarter, width = pieces[0].shape
    part = rows * quarter
    at = first // rows
    out = weight.shape[0]
    return pl.pallas_call(
        cotangent_kernel,
        grid=(1,),
        in_specs=[pl.BlockSpec((part, width), lambda c: (at, 0))] * 4 + [pl.BlockSpec((out, width), lambda c: (0, 0))],
        out_specs=[pl.BlockSpec((4 * part, out), lambda c: (0, 0)), pl.BlockSpec((4 * part, width), lambda c: (0, 0))],
        out_shape=[jax.ShapeDtypeStruct((4 * part, out), bf16), jax.ShapeDtypeStruct((4 * part, width), bf16)],
        cost_estimate=cost(
            flops=8 * part * width * out, bytes_accessed=2 * width * (out + 8 * part), transcendentals=0
        ),
        name="project_cotangent",
    )(*[p.reshape(total * quarter, width) for p in pieces], weight)


def assemble(pairs):
    rows, heads, parts, pieces, quarter, size = pairs.shape
    tokens, width = 4 * rows * quarter, parts * heads * size
    return pl.pallas_call(
        join_pairs,
        out_shape=jax.ShapeDtypeStruct((tokens, width), bf16),
        cost_estimate=cost(flops=0, bytes_accessed=4 * tokens * width, transcendentals=0),
        name="assemble",
    )(pairs)


def runs(lengths, cut):
    at = 0
    for k, n in enumerate(lengths):
        start = 0
        while start < n:
            step = min(n - start, cut - at % cut)
            yield k, start, at, step
            start += step
            at += step


def width_of(sizes, pieces):
    return -(-sum(sizes) // (pieces * LANES)) * LANES


def part_of(ref, j, rank, lanes):
    return ref.at[j, :, lanes] if len(ref.shape) == 3 else ref.at[j * rank:(j + 1) * rank, lanes]


def pack_kernel(*refs, plan, counts, vectors):
    total = sum(counts)
    in_refs, sum_refs, out_ref, sums = refs[:total], refs[total:-2], refs[-2], refs[-1]
    rank = out_ref.shape[1]
    sums[...] = jnp.zeros_like(sums)
    row = 0
    for ref in sum_refs:
        for j in range(ref.shape[0]):
            sums[row:row + 1, :ref.shape[2]] = ref[j]
            row += 1
    base = 0
    for entries, cut in plan:
        sizes = [n for _, _, n in entries]
        for k, start, at, n in runs(sizes, cut):
            which, j, _ = entries[k]
            lanes = slice(start, start + n)
            values = sums[:, lanes] if which is None else part_of(in_refs[which], j, rank, lanes)[...]
            out_ref[at // cut, :, base + at % cut:base + at % cut + n] = values.astype(bf16)
        end = sum(sizes)
        while end < out_ref.shape[0] * cut:
            n = cut - end % cut
            out_ref[end // cut, :, base + end % cut:base + end % cut + n] = jnp.zeros((rank, n), bf16)
            end += n
        base += cut


def unpack_kernel(*refs, plan, count):
    x_ref, m_refs, out_refs = refs[0], refs[1:1 + count], refs[1 + count:]
    rank = x_ref.shape[1]
    base = 0
    for entries, cut in plan:
        for k, start, at, n in runs([n for _, _, n in entries], cut):
            values = x_ref[at // cut, :, base + at % cut:base + at % cut + n].astype(f32)
            which, j, _ = entries[k]
            if which is not None:
                part_of(out_refs[which], j, rank, slice(start, start + n))[...] = values
                continue
            row = 0
            for m_ref, out_ref in zip(m_refs, out_refs[-count:]):
                members, size = m_ref.shape
                stop = min(start + n, size)
                if start < stop:
                    out_ref[:, start:stop] = values[row:row + members, :stop - start] / m_ref[:, start:stop]
                row += members
        base += cut


def packing(over_all, over_seq, width, pieces, rank):
    plan, at = [], 0
    for arrays in (over_all, over_seq):
        entries = []
        for v in arrays:
            members = v.shape[0] if len(v.shape) == 3 else v.shape[0] // rank
            entries += [(at, j, v.shape[-1]) for j in range(members)]
            at += 1
        plan.append(entries)
    plan[1].append((None, 0, width))
    return [(entries, width_of([n for _, _, n in entries], pieces)) for entries in plan]


def pack(plan, arrays, vectors, pieces, rank, width):
    return pl.pallas_call(
        partial(pack_kernel, plan=plan, counts=[len(arrays)], vectors=len(vectors)),
        out_shape=jax.ShapeDtypeStruct((pieces, rank, sum(cut for _, cut in plan)), bf16),
        scratch_shapes=[pltpu.VMEM((rank, width), f32)],
        cost_estimate=cost(flops=0, bytes_accessed=4 * sum(v.size for v in arrays), transcendentals=0),
        name="pack",
    )(*arrays, *vectors)


def unpack(plan, values, arrays, magnitudes):
    return pl.pallas_call(
        partial(unpack_kernel, plan=plan, count=len(magnitudes)),
        out_shape=[jax.ShapeDtypeStruct(v.shape, f32) for v in (*arrays, *magnitudes)],
        cost_estimate=cost(flops=0, bytes_accessed=6 * values.size, transcendentals=0),
        name="unpack",
    )(values, *magnitudes)


def gated_kernel(*refs):
    x_refs, w_ref, e_ref, hidden_ref, grads_ref, sums_ref, xs = refs[:4], *refs[4:]
    count = x_refs[0].shape[0]

    @pl.when(pl.program_id(0) == 0)
    def _():
        for i in range(4):
            xs[i * count:(i + 1) * count] = x_refs[i][...]

    product = mm(xs[...], w_ref[...])
    block = LANES
    for k in range(product.shape[1] // (2 * block)):
        at, mine = k * 2 * block, slice(k * block, (k + 1) * block)
        gate, up = product[:, at:at + block], product[:, at + block:at + 2 * block]
        dhid = e_ref[:, mine].astype(f32)
        sig = 1.0 / (1.0 + jnp.exp(-gate))
        act = gate * sig
        hidden_ref[:, mine] = (act * up).astype(bf16)
        dgate = dhid * up * (sig * (1.0 + gate * (1.0 - sig)))
        dup = dhid * act
        grads_ref[:, at:at + block] = dgate.astype(bf16)
        grads_ref[:, at + block:at + 2 * block] = dup.astype(bf16)
        sums_ref[0, :, mine] = jnp.sum(gate * dgate, axis=0, keepdims=True)
        sums_ref[1, :, mine] = jnp.sum(up * dup, axis=0, keepdims=True)


def gated(pieces, weight, dhid):
    rows, quarter, width = pieces[0].shape
    count = rows * quarter
    out = dhid.shape[1]
    block = GATED_BLOCKS * LANES
    return pl.pallas_call(
        gated_kernel,
        grid=(-(-out // block),),
        in_specs=[pl.BlockSpec(memory_space=pltpu.VMEM)] * 4
        + [
            pl.BlockSpec((width, 2 * block), lambda i: (0, i)),
            pl.BlockSpec((4 * count, block), lambda i: (0, i)),
        ],
        out_specs=[
            pl.BlockSpec((4 * count, block), lambda i: (0, i)),
            pl.BlockSpec((4 * count, 2 * block), lambda i: (0, i)),
            pl.BlockSpec((2, 1, block), lambda i: (0, 0, i)),
            pl.BlockSpec((4 * count, width), lambda i: (0, 0)),
        ],
        out_shape=[
            jax.ShapeDtypeStruct((4 * count, out), bf16),
            jax.ShapeDtypeStruct((4 * count, 2 * out), bf16),
            jax.ShapeDtypeStruct((2, 1, out), f32),
            jax.ShapeDtypeStruct((4 * count, width), bf16),
        ],
        cost_estimate=cost(
            flops=16 * count * width * out,
            bytes_accessed=4 * width * out + 8 * count * (2 * width + 4 * out),
            transcendentals=4 * count * out,
        ),
        name="gated",
    )(*[p.reshape(count, width) for p in pieces], weight, dhid)


def chunk_lanes(refs):
    ends = [0]
    for ref in refs:
        ends.append(ends[-1] + ref.shape[0])
    return [slice(a, b) for a, b in zip(ends, ends[1:])]


def column_grads_kernel(*refs, chunks, steps):
    x_refs, d_refs, refs = refs[:chunks], refs[chunks:2 * chunks], refs[2 * chunks:]
    w_ref, a_ref, b_ref, stat_ref, m_ref, sum_ref, cross_ref, gb_ref, ga_ref, ts, dts, es = refs
    members, rank, block = b_ref.shape
    lanes = chunk_lanes(x_refs)
    i = pl.program_id(0)

    @pl.when(i == 0)
    def _():
        for c in range(chunks):
            ts[:, lanes[c]] = mm(a_ref[...], x_refs[c][...], NT).astype(bf16)
        dts[...] = jnp.zeros_like(dts)

    @pl.when(i < steps)
    def _():
        found = sum(mm(ts[:, lanes[c]], d_refs[c][...]) for c in range(chunks))
        spread, along = [], []
        for j in range(members):
            b = b_ref[j].astype(f32)
            scale = stat_ref[j, 1:2]
            coef = -sum_ref[j] / (m_ref[j] * stat_ref[j, 0:1])
            mine = found[j * rank:(j + 1) * rank, j * block:(j + 1) * block]
            gb_ref[j] = (adapter_scale * (mine * scale + coef * cross_ref[j])).astype(bf16)
            empty = jnp.zeros((rank, block), f32)
            row = lambda v: jnp.concatenate([v if k == j else empty for k in range(members)], axis=1)
            spread.append(row(adapter_scale * coef * b))
            along.append(row(adapter_scale * scale * b))
        wide = members * block
        es[:, pl.ds(pl.multiple_of(i * wide, wide), wide)] = jnp.concatenate(spread, axis=0).astype(bf16)
        up = jnp.concatenate(along, axis=0).astype(bf16)
        for c in range(chunks):
            dts[:, lanes[c]] += mm(up, d_refs[c][...], NT)

    @pl.when(i >= steps)
    def _():
        span = w_ref.shape[0]
        at = pl.ds(pl.multiple_of((i - steps) * span, span), span)
        total = mm(es[...], w_ref[...], NT)
        for c in range(chunks):
            total = total + mm(dts[:, lanes[c]].astype(bf16), x_refs[c][:, at])
        ga_ref[...] = total.astype(bf16)


def column_grads(rows, grads, weight, down, up, stat, magnitude, sums, cross, block):
    tokens, width = sum(v.shape[0] for v in rows), rows[0].shape[1]
    members, rank, out = up.shape
    chunks, steps, span = len(rows), out // block, 512
    first = lambda i: jnp.minimum(i, steps - 1)
    then = lambda i: jnp.maximum(i - steps, 0)
    part = lambda n: pl.BlockSpec((members, n, block), lambda i: (0, 0, first(i)))
    wide = members * block
    ranks = members * rank
    grad_b, grad_a = pl.pallas_call(
        partial(column_grads_kernel, chunks=chunks, steps=steps),
        grid=(steps + width // span,),
        in_specs=[pl.BlockSpec(v.shape, lambda i: (0, 0)) for v in rows]
        + [pl.BlockSpec((v.shape[0], wide), lambda i: (0, first(i))) for v in grads]
        + [
            pl.BlockSpec((span, members * out), lambda i: (then(i), 0)),
            pl.BlockSpec((ranks, width), lambda i: (0, 0)),
            part(rank), part(2), part(1), part(1), part(rank),
        ],
        out_specs=[part(rank), pl.BlockSpec((ranks, span), lambda i: (0, then(i)))],
        out_shape=[
            jax.ShapeDtypeStruct((members, rank, out), bf16),
            jax.ShapeDtypeStruct((ranks, width), bf16),
        ],
        scratch_shapes=[
            pltpu.VMEM((ranks, tokens), bf16),
            pltpu.VMEM((ranks, tokens), f32),
            pltpu.VMEM((ranks, members * out), bf16),
        ],
        cost_estimate=cost(
            flops=4 * 256 * width * members * out // 4,
            bytes_accessed=2 * (width * members * out + tokens * (width + members * out)),
            transcendentals=0,
        ),
        name="column_grads",
    )(*rows, *grads, weight, down.transpose(0, 2, 1).reshape(ranks, width), up, stat, magnitude[:, None, :], sums, cross)
    return grad_a, grad_b


def row_grads_kernel(*refs, chunks):
    h_refs, d_refs, refs = refs[:chunks], refs[chunks:2 * chunks], refs[2 * chunks:]
    w_ref, a_ref, b_ref, stat_ref, coef_ref, ga_ref, gb_ref, ts, dts, acc = refs
    lanes = chunk_lanes(h_refs)
    i = pl.program_id(0)

    @pl.when(i == 0)
    def _():
        for c in range(chunks):
            ts[:, lanes[c]] = mm(a_ref[...], h_refs[c][...], NT).astype(bf16)
        dts[...] = jnp.zeros_like(dts)
        acc[...] = jnp.zeros_like(acc)

    b = b_ref[...].astype(f32)
    coef = coef_ref[...]
    found = sum(mm(ts[:, lanes[c]], d_refs[c][...]) for c in range(chunks))
    gb_ref[...] = (adapter_scale * (found + coef * stat_ref[...])).astype(bf16)
    up = (adapter_scale * b).astype(bf16)
    for c in range(chunks):
        dts[:, lanes[c]] += mm(up, d_refs[c][...], NT)
    acc[...] += mm((adapter_scale * coef * b).astype(bf16), w_ref[...], NT)

    @pl.when(i == pl.num_programs(0) - 1)
    def _():
        total = acc[...]
        for c in range(chunks):
            total = total + mm(dts[:, lanes[c]].astype(bf16), h_refs[c][...])
        ga_ref[...] = total.astype(bf16)


def row_grads(rows, grads, weight, down, up, stat, coef, block):
    tokens, count = sum(v.shape[0] for v in rows), rows[0].shape[1]
    rank, out = up.shape
    chunks = len(rows)
    along = lambda n: pl.BlockSpec((n, block), lambda i: (0, i))
    return pl.pallas_call(
        partial(row_grads_kernel, chunks=chunks),
        grid=(out // block,),
        in_specs=[pl.BlockSpec(v.shape, lambda i: (0, 0)) for v in rows]
        + [pl.BlockSpec((v.shape[0], block), lambda i: (0, i)) for v in grads]
        + [along(count), pl.BlockSpec((rank, count), lambda i: (0, 0)), along(rank), along(rank), along(1)],
        out_specs=[pl.BlockSpec((rank, count), lambda i: (0, 0)), along(rank)],
        out_shape=[jax.ShapeDtypeStruct((rank, count), bf16), jax.ShapeDtypeStruct((rank, out), bf16)],
        scratch_shapes=[
            pltpu.VMEM((rank, tokens), bf16),
            pltpu.VMEM((rank, tokens), f32),
            pltpu.VMEM((rank, count), f32),
        ],
        cost_estimate=cost(
            flops=256 * count * out, bytes_accessed=2 * (count * out + tokens * (count + out)), transcendentals=0
        ),
        name="row_grads",
    )(*rows, *grads, weight, down.T, up, stat, coef)


def norm_scale(values):
    return lax.rsqrt(jnp.mean(values * values, axis=-1, keepdims=True) + epsilon)


def norm_back(values, gain, grad):
    r = norm_scale(values)
    weighted = gain * grad
    return r * weighted - values * (r * r * r) * jnp.mean(values * weighted, axis=-1, keepdims=True)


def rotary_tables(positions, head_size):
    half_size = head_size // 2
    frequency = rope_base ** (-(2.0 * jnp.arange(half_size, dtype=f32)) / head_size)
    angles = positions.astype(f32)[:, None] * frequency[None, :]
    cosine, sine = jnp.cos(angles), jnp.sin(angles)
    return (jnp.concatenate([cosine, cosine], axis=-1), jnp.concatenate([-sine, sine], axis=-1))


def local(
    layer_in, cotangent, doc_lengths, pad_counts, gain_attn, gain_ffn, w_qkv, a_qkv, b_qkv, m_qkv, w_out, a_out,
    b_out, m_out, w_gateup, a_gateup, b_gateup, m_gateup, w_down, a_down, b_down, m_down,
):
    rows, quarter, width = layer_in.shape
    tensor, seq = lax.axis_size("tensor"), lax.axis_size("seq")
    assert tensor == len(PIECES)
    me_t, me_s = lax.axis_index("tensor"), lax.axis_index("seq")
    group = quarter * tensor
    total = group * seq
    feat = w_qkv.shape[2]
    heads = feat // HEAD_DIM
    rank = a_qkv.shape[2]
    ff = w_down.shape[0]
    piece_of = jnp.bitwise_xor(me_t, jnp.array(PIECES, jnp.int32))
    in_block = (piece_of[:, None] * quarter + jnp.arange(quarter, dtype=jnp.int32)[None, :]).reshape(group)
    positions = (jnp.arange(seq, dtype=jnp.int32)[:, None] * group + in_block[None, :]).reshape(total)
    tables = rotary_tables(positions, HEAD_DIM)
    offsets = jnp.cumsum(doc_lengths, axis=1)
    starts = jnp.max(
        jnp.where(offsets[:, :, None] <= positions[None, None, :], offsets[:, :, None], 0), axis=1
    )
    kpos = positions[:, None]
    few = rows // 3
    cuts = [slice(rows - few, rows), slice(0, rows - few)]
    span = range(2)
    pair_counts = [(at.stop - at.start) * heads for at in cuts]
    slots = [-(-count // seq) for count in pair_counts]
    mine = [me_s * slots[c] + jnp.arange(slots[c]) for c in span]
    live = [mine[c] < pair_counts[c] for c in span]

    def pair_info(c):
        row = jnp.minimum(mine[c] // heads + cuts[c].start, cuts[c].stop - 1)
        chosen = (row[:, None] == jnp.arange(rows)[None, :])[:, :, None]
        return jnp.stack(
            [jnp.broadcast_to(positions[None], (slots[c], total)), jnp.sum(jnp.where(chosen, starts[None], 0), axis=1)],
            axis=1,
        )

    qinfo = [pair_info(c) for c in span]

    def send_pairs(values, c):
        parts = values.shape[2]
        laid = values.reshape(pair_counts[c], parts, group, HEAD_DIM)
        if slots[c] * seq > pair_counts[c]:
            laid = jnp.pad(laid, ((0, slots[c] * seq - pair_counts[c]), (0, 0), (0, 0), (0, 0)))
        return exchange(laid.reshape(seq, slots[c], parts, group, HEAD_DIM))

    def fetch_pairs(values, c):
        parts = values.shape[2]
        laid = exchange(values).reshape(seq * slots[c], parts, group, HEAD_DIM)[:pair_counts[c]]
        return laid.reshape(pair_counts[c] // heads, heads, parts, tensor, quarter, HEAD_DIM)

    def to_heads(pieces, weight):
        return project_to_pairs(pieces, weight, NN, 3, heads, HEAD_DIM, heads)

    def back_to_heads(pieces, weight):
        return project_to_pairs(pieces, weight, NT, 1, heads, HEAD_DIM, 2)

    owned = me_s * group + me_t * quarter + jnp.arange(quarter, dtype=jnp.int32)
    valid = (owned[None, :] < total - pad_counts[:, None]).astype(f32)
    cot = cotangent.astype(f32) * valid[:, :, None]
    wide_in = [layer_in[at].astype(f32) for at in cuts]

    def normed(values, gain):
        return (values * norm_scale(values) * gain).astype(bf16)

    started = [gather_start(normed(wide_in[c], gain_attn)) for c in span]
    qkv_w, qkv_stat, qkv_cross = column_prep(w_qkv, a_qkv, b_qkv, m_qkv, 256, False)
    started[0], qkv_w = after(started[0], qkv_w)
    normed_a, d_qkv, pairs, outputs, totals, att = [[None] * 2 for _ in range(6)]
    laid, normed_a[0] = to_heads(gather_end(*started[0]), qkv_w)

    laid, started[1], w_out = after(laid, started[1], w_out)
    pairs[0] = send_pairs(laid, 0)
    laid, normed_a[1] = to_heads(gather_end(*started[1]), qkv_w)
    out_w, out_cross, out_square = row_prep(w_out, a_out, b_out, 512)
    pairs[0], laid, out_square, w_down = after(pairs[0], laid, out_square, w_down)

    outputs[0], totals[0] = attend(pairs[0], tables, kpos, qinfo[0])
    outputs[0], w_down = after(outputs[0], w_down)
    fetched = fetch_pairs(outputs[0][:, :, None], 0)
    down_w, down_cross, down_square = row_prep(w_down, a_down, b_down, 256)
    fetched, laid, down_square = after(fetched, laid, down_square)

    u_out, middle, hidden, d_gu, gu_sum, normed_f, d_mid, du_out, dhid, du_down = [[None] * 2 for _ in range(10)]

    def of_cotangent(whole, c):
        return project_cotangent(whole, down_w, cuts[c].stop - cuts[c].start, cuts[c].start)

    pairs[1] = send_pairs(laid, 1)
    squares = tensor_sum(jnp.concatenate([down_square, out_square]))
    fetched, squares = after(fetched, squares)
    down_square, out_square = squares[0:1], squares[1:2]
    down_scale, out_scale = m_down / jnp.sqrt(squares[0]), m_out / jnp.sqrt(squares[1])
    att[0], split = project_from_pairs(fetched, out_w, 512)
    moving, scaled, w_gateup = after(scatter_start(*split), (cot * down_scale).astype(bf16), w_gateup)
    tail, started = scatter_end(*moving), gather_start(scaled)
    gu_w, gu_stat, gu_cross = column_prep(w_gateup, a_gateup, b_gateup, m_gateup, LANES, True)
    tail, started, gu_w = after(tail, started, gu_w)
    u_out[0] = tail * out_scale
    middle[0] = wide_in[0] + u_out[0]
    h_f, whole_cot = after(normed(middle[0], gain_ffn), gather_end(*started))
    pairs[1], h_f = after(pairs[1], h_f)
    outputs[1], totals[1] = attend(pairs[1], tables, kpos, qinfo[1])
    started, outputs[1] = after(gather_start(h_f), outputs[1])

    fetched = fetch_pairs(outputs[1][:, :, None], 1)
    dhid[0], du_down[0] = of_cotangent(whole_cot, 0)
    hidden[0], d_gu[0], gu_sum[0], normed_f[0] = gated(gather_end(*started), gu_w, dhid[0])
    d_gu[0], fetched = after(d_gu[0], fetched)

    att[1], split = project_from_pairs(fetched, out_w, 512)
    moving, d_gu[0], whole_cot = after(scatter_start(*split), d_gu[0], whole_cot)
    split = project_split([d_gu[0]], gu_w, NT, 512, quarter)
    dhid[1], du_down[1] = of_cotangent(whole_cot, 1)
    tail, split, dhid[1] = after(scatter_end(*moving), split, dhid[1])
    u_out[1] = tail * out_scale
    middle[1] = wide_in[1] + u_out[1]
    h_f, split = after(normed(middle[1], gain_ffn), split)
    shard, far, near = gather_start(h_f)
    near, split = after(near, split)
    started = (shard, far, near)
    d_mid[0] = cot[cuts[0]] + norm_back(middle[0], gain_ffn, scatter_end(*scatter_start(*split)))
    behind = gather_start((d_mid[0] * out_scale).astype(bf16))
    d_att, du_out[0] = back_to_heads(gather_end(*behind), out_w)
    whole, d_att = after(gather_end(*started), d_att)

    d_outputs = send_pairs(d_att, 0)[:, :, 0]
    hidden[1], d_gu[1], gu_sum[1], normed_f[1] = gated(whole, gu_w, dhid[1])
    d_gu[1], d_outputs = after(d_gu[1], d_outputs)
    moving, d_outputs = after(scatter_start(*project_split([d_gu[1]], gu_w, NT, 512, quarter)), d_outputs)
    d_pairs, pair_sums = [None] * 2, [None] * 2
    d_pairs[0], pair_sums[0] = attend_back(pairs[0], outputs[0], d_outputs, totals[0], tables, kpos, qinfo[0])
    fetched = fetch_pairs(d_pairs[0], 0)
    d_mid[1] = cot[cuts[1]] + norm_back(middle[1], gain_ffn, scatter_end(*moving))
    scaled, hidden = after((d_mid[1] * out_scale).astype(bf16), hidden)
    split = project_split(hidden[::-1], down_w, NN, 512, quarter)
    started, split, fetched = after(gather_start(scaled), split, fetched)
    d_att, du_out[1] = back_to_heads(gather_end(*started), out_w)

    d_att, fetched, out_sum = after(d_att, fetched, sum(jnp.sum(u_out[c] * d_mid[c], axis=(0, 1)) for c in span)[None])
    d_outputs = send_pairs(d_att, 1)[:, :, 0]
    out_sum, fetched = after(tensor_sum(out_sum), fetched)
    d_qkv[0] = assemble(fetched)
    split_in = [project_split([d_qkv[0]], qkv_w, NT, 512, quarter), None]
    d_outputs, split_in[0], out_sum, d_gu = after(d_outputs, split_in[0], out_sum, d_gu)
    d_pairs[1], pair_sums[1] = attend_back(pairs[1], outputs[1], d_outputs, totals[1], tables, kpos, qinfo[1])

    d_pairs[1], split, att, d_gu, split_in[0] = after(d_pairs[1], split, att, d_gu, split_in[0])
    fetched = fetch_pairs(d_pairs[1], 1)
    moving, d_gu = after(scatter_start(*split), d_gu)
    gu_sums = sum(gu_sum)
    grad_a_gu, grad_b_gu = column_grads(
        normed_f, d_gu, gu_w, a_gateup, b_gateup, gu_stat, m_gateup, gu_sums, gu_cross, LANES
    )
    tail, grad_a_gu, att = after(scatter_end(*moving), grad_a_gu, att)
    u_down = tail * down_scale
    layer_out = (jnp.concatenate(middle[::-1]) + u_down).astype(bf16)
    down_sum = tensor_sum(jnp.sum(u_down * cot, axis=(0, 1))[None])
    grad_a_out, grad_b_out = row_grads(att, du_out, out_w, a_out, b_out, out_cross, -out_sum / out_square, 512)
    grad_a_down, grad_b_down = row_grads(
        hidden, du_down, down_w, a_down, b_down, down_cross, -down_sum / down_square, 512
    )
    grad_norm_a = [scatter_end(*scatter_start(*split_in[0])), None]
    fetched, grad_a_out, grad_a_down, layer_out, grad_norm_a[0] = after(
        fetched, grad_a_out, grad_a_down, layer_out, grad_norm_a[0]
    )
    d_qkv[1] = assemble(fetched)

    qkv_sums = 0.0
    for c in span:
        choice = jnp.logical_and((mine[c] % heads)[:, None] == jnp.arange(heads)[None, :], live[c][:, None])
        qkv_sums = qkv_sums + jnp.sum(jnp.where(choice[:, None, :, None], pair_sums[c][:, :, None, :], 0.0), axis=0)
    qkv_sums = qkv_sums.reshape(3, 1, feat)
    grad_a_qkv, grad_b_qkv = column_grads(
        normed_a, d_qkv, qkv_w, a_qkv, b_qkv, qkv_stat, m_qkv, qkv_sums, qkv_cross, feat
    )

    over_all = [grad_a_gu, grad_b_out, grad_b_down, grad_a_qkv]
    over_seq = [grad_b_gu, grad_a_out, grad_a_down, grad_b_qkv]
    vectors = [gu_sums, out_sum[None], down_sum[None], qkv_sums]
    plan = packing(over_all, over_seq, width, seq, rank)
    cut = plan[0][1]
    packed, d_qkv[1] = after(pack(plan, over_all + over_seq, vectors, seq, rank, width), d_qkv[1])
    added = exchange(packed)
    split_in[1] = project_split([d_qkv[1]], qkv_w, NT, 512, quarter)
    grad_norm_a[1] = scatter_end(*scatter_start(*split_in[1]))
    grad_in = jnp.concatenate(
        [d_mid[c] + norm_back(wide_in[c], gain_attn, grad_norm_a[c]) for c in reversed(span)]
    )
    added = jnp.sum(added.astype(f32), axis=0).astype(bf16)
    shared = added[:, :cut]
    shared = shared.astype(f32) + swap(shared, 1).astype(f32) + swap(shared, 2).astype(f32) + swap(shared, 3).astype(f32)
    back = seq_gather(jnp.concatenate([shared.astype(bf16), added[:, cut:]], axis=1))
    g_a_gu, g_b_out, g_b_down, g_a_qkv, g_b_gu, g_a_out, g_a_down, g_b_qkv, s_gu, s_out, s_down, s_qkv = unpack(
        plan, back, over_all + over_seq, [m_gateup, m_out[None], m_down[None], m_qkv]
    )
    return (
        layer_out,
        grad_in,
        g_a_qkv.reshape(3, rank, width).transpose(0, 2, 1),
        g_b_qkv,
        s_qkv,
        g_a_out.T,
        g_b_out,
        s_out[0],
        g_a_gu.reshape(2, rank, width).transpose(0, 2, 1),
        g_b_gu,
        s_gu,
        g_a_down.T,
        g_b_down,
        s_down[0],
    )


def solution(mesh):
    split = P(None, ("seq", "tensor"), None)
    in_specs = (
        split, split, P(), P(), P(), P(),
        P(None, None, "tensor"), P(), P(None, None, "tensor"), P(None, "tensor"),
        P("tensor", None), P("tensor", None), P(), P(),
        P(None, None, "tensor"), P(), P(None, None, "tensor"), P(None, "tensor"),
        P("tensor", None), P("tensor", None), P(), P(),
    )
    out_specs = (
        split, split,
        P(), P(None, None, "tensor"), P(None, "tensor"),
        P("tensor", None), P(), P(),
        P(), P(None, None, "tensor"), P(None, "tensor"),
        P("tensor", None), P(), P(),
    )
    return jax.shard_map(local, mesh=mesh, in_specs=in_specs, out_specs=out_specs, check_vma=False)
```

```python
from functools import partial
import math

import jax
import jax.numpy as jnp
from jax import lax
from jax.experimental import pallas as pl
from jax.experimental.pallas import tpu as pltpu
from jax.sharding import PartitionSpec as P

HEAD_DIM = 128
LANES = 128
epsilon = 1e-05
adapter_scale = 2.0
rope_base = 10000.0
f32 = jnp.float32
bf16 = jnp.bfloat16
PIECES = (0, 2, 1, 3)
score_block = 256
GATED_BLOCKS = 2
NT = (((1,), (1,)), ((), ()))
NN = (((1,), (0,)), ((), ()))
TN = (((0,), (0,)), ((), ()))


def cost(flops, bytes_accessed, transcendentals):
    return pl.CostEstimate(flops=flops // 64, bytes_accessed=bytes_accessed // 64, transcendentals=0)


def mm(a, b, dims=NN):
    return lax.dot_general(a, b, dims, preferred_element_type=f32)


def swap(values, bit):
    size = lax.axis_size("tensor")
    return lax.ppermute(values, "tensor", [(i, i ^ bit) for i in range(size)])


def gather_start(shard):
    return shard, swap(shard, 2), swap(shard, 1)


def gather_end(shard, far, near):
    return [shard, far, near, swap(far, 1)]


def scatter_start(kept, near, send):
    got = swap(send, 1)
    return kept, got, (near.astype(f32) + got[1].astype(f32)).astype(bf16)


def scatter_end(kept, got, passed):
    return kept.astype(f32) + got[0].astype(f32) + swap(passed, 2).astype(f32)


def after(value, *others):
    return lax.optimization_barrier((value, *others))


def tensor_sum(values):
    return values + swap(values, 1) + swap(values, 2) + swap(values, 3)


def exchange(values):
    return lax.all_to_all(values, "seq", 0, 0, tiled=True)


def seq_gather(values):
    size = lax.axis_size("seq")
    return exchange(jnp.broadcast_to(values[None], (size,) + values.shape))


def column_prep_kernel(w_ref, a_ref, b_ref, m_ref, out_ref, stat_ref, cross_ref):
    members, width, block = w_ref.shape
    rank = cross_ref.shape[1]
    product = mm(a_ref[...], b_ref[0], TN)
    i = pl.program_id(0)
    for j in range(members):
        heading = w_ref[j].astype(f32) + adapter_scale * product[:, j * block:(j + 1) * block]
        norm = jnp.sqrt(jnp.sum(heading * heading, axis=0, keepdims=True))
        scale = m_ref[j] / norm
        scaled = (heading * scale).astype(bf16)
        if out_ref.shape[1] == members * block:
            out_ref[:, j * block:(j + 1) * block] = scaled
        else:
            out_ref[:, pl.ds(pl.multiple_of(j * (out_ref.shape[1] // members) + i * block, block), block)] = scaled
        stat_ref[j] = jnp.concatenate([norm, scale], axis=0)
        cross_ref[j] = mm(a_ref[j * rank:(j + 1) * rank, :], scaled)


def column_prep(weight, down, up, magnitude, block, alternate):
    members, width, out = weight.shape
    rank = down.shape[2]
    wide = members * block
    eye = jnp.eye(members, dtype=bf16)[:, None, None, :, None]
    blocks = up.reshape(members, rank, out // block, 1, block) * eye
    blocks = blocks.transpose(2, 0, 1, 3, 4).reshape(out // block, members * rank, wide)
    flat = down.transpose(0, 2, 1).reshape(members * rank, width)
    if alternate:
        scaled_spec = pl.BlockSpec((width, wide), lambda i: (0, i))
    else:
        scaled_spec = pl.BlockSpec((width, members * out), lambda i: (0, 0))
    return pl.pallas_call(
        column_prep_kernel,
        grid=(out // block,),
        in_specs=[
            pl.BlockSpec((members, width, block), lambda i: (0, 0, i)),
            pl.BlockSpec((members * rank, width), lambda i: (0, 0)),
            pl.BlockSpec((1, members * rank, wide), lambda i: (i, 0, 0)),
            pl.BlockSpec((members, 1, block), lambda i: (0, 0, i)),
        ],
        out_specs=[
            scaled_spec,
            pl.BlockSpec((members, 2, block), lambda i: (0, 0, i)),
            pl.BlockSpec((members, rank, block), lambda i: (0, 0, i)),
        ],
        out_shape=[
            jax.ShapeDtypeStruct((width, members * out), bf16),
            jax.ShapeDtypeStruct((members, 2, out), f32),
            jax.ShapeDtypeStruct((members, rank, out), f32),
        ],
        cost_estimate=cost(
            flops=4 * members * width * out * 256, bytes_accessed=4 * members * width * out, transcendentals=0
        ),
        name="column_prep",
    )(weight, flat, blocks, magnitude[:, None, :])


def row_prep_kernel(w_ref, a_ref, b_ref, out_ref, cross_ref, square_ref):
    heading = w_ref[...].astype(f32) + adapter_scale * mm(a_ref[...], b_ref[...], TN)
    narrow = heading.astype(bf16)
    out_ref[...] = narrow
    cross_ref[...] = mm(a_ref[...], narrow)
    square_ref[...] = jnp.sum(heading * heading, axis=0, keepdims=True)


def row_prep(weight, down, up, block):
    rows, out = weight.shape
    rank = down.shape[1]
    along = lambda n: pl.BlockSpec((n, block), lambda i: (0, i))
    return pl.pallas_call(
        row_prep_kernel,
        grid=(out // block,),
        in_specs=[along(rows), pl.BlockSpec((rank, rows), lambda i: (0, 0)), along(rank)],
        out_specs=[along(rows), along(rank), along(1)],
        out_shape=[
            jax.ShapeDtypeStruct((rows, out), bf16),
            jax.ShapeDtypeStruct((rank, out), f32),
            jax.ShapeDtypeStruct((1, out), f32),
        ],
        cost_estimate=cost(flops=2 * rows * out * 256, bytes_accessed=4 * rows * out, transcendentals=0),
        name="row_prep",
    )(weight, down.T, up)


def turn_forward(values, cosine, signed_sine):
    return values * cosine + pltpu.roll(values, values.shape[1] // 2, 1) * signed_sine


def turn_backward(values, cosine, signed_sine):
    return values * cosine + pltpu.roll(values * signed_sine, values.shape[1] // 2, 1)


def over_blocks(total, block, body):
    if total // block <= 4:
        for i in range(total // block):
            body(i * block, (i + 1) * block)
    else:

        def step(i, carry):
            body(pl.multiple_of(i * block, block), total)
            return carry

        lax.fori_loop(0, total // block, step, 0)


def weights_t(keys, queries, kpos, qpos, qstart, scale):
    scores = mm(keys, queries, NT)
    allowed = jnp.logical_and(kpos <= qpos, kpos >= qstart)
    return jnp.where(allowed, jnp.exp(scores * scale), 0.0)


def attend_kernel(x_ref, cos_ref, sin_ref, kpos_ref, qinfo_ref, o_ref, l_ref, qs, ks, vt, os, *, scale, block):
    blocks, _, _, group, size = x_ref.shape
    total = blocks * group
    cosine, signed_sine = cos_ref[...], sin_ref[...]
    qs[...] = turn_forward(x_ref[:, 0, 0].reshape(total, size).astype(f32), cosine, signed_sine).astype(bf16)
    ks[...] = turn_forward(x_ref[:, 0, 1].reshape(total, size).astype(f32), cosine, signed_sine).astype(bf16)
    vt[...] = x_ref[:, 0, 2].reshape(total, size).astype(f32).T.astype(bf16)

    def body(first, last):
        at = pl.ds(first, block)
        weights = weights_t(
            ks[:last], qs[at, :], kpos_ref[:last], qinfo_ref[0, 0:1, at], qinfo_ref[0, 1:2, at], scale
        )
        totals = jnp.sum(weights, axis=0, keepdims=True)
        outer = mm(vt[:, :last], weights.astype(bf16))
        l_ref[0, 0:1, at] = totals
        os[at, :] = (outer / totals).T.astype(bf16)

    over_blocks(total, block, body)
    o_ref[:, 0] = os[...].reshape(blocks, group, size)


def attend(pairs, tables, kpos, qinfo):
    blocks, slots, _, group, size = pairs.shape
    total = blocks * group
    block = math.gcd(total, score_block)
    return pl.pallas_call(
        partial(attend_kernel, scale=1.0 / math.sqrt(size), block=block),
        grid=(slots,),
        in_specs=[
            pl.BlockSpec((blocks, 1, 3, group, size), lambda n: (0, n, 0, 0, 0)),
            pl.BlockSpec((total, size), lambda n: (0, 0)),
            pl.BlockSpec((total, size), lambda n: (0, 0)),
            pl.BlockSpec((total, 1), lambda n: (0, 0)),
            pl.BlockSpec((1, 2, total), lambda n: (n, 0, 0)),
        ],
        out_specs=[
            pl.BlockSpec((blocks, 1, group, size), lambda n: (0, n, 0, 0)),
            pl.BlockSpec((1, 1, total), lambda n: (n, 0, 0)),
        ],
        out_shape=[
            jax.ShapeDtypeStruct((blocks, slots, group, size), bf16),
            jax.ShapeDtypeStruct((slots, 1, total), f32),
        ],
        scratch_shapes=[
            pltpu.VMEM((total, size), bf16),
            pltpu.VMEM((total, size), bf16),
            pltpu.VMEM((size, total), bf16),
            pltpu.VMEM((total, size), bf16),
        ],
        cost_estimate=cost(
            flops=slots * 4 * total * total * size,
            bytes_accessed=slots * total * size * 8,
            transcendentals=slots * total * total // 2,
        ),
        name="attend",
    )(pairs, *tables, kpos, qinfo)


def attend_back_kernel(
    x_ref, o_ref, d_ref, l_ref, cos_ref, sin_ref, kpos_ref, qinfo_ref, g_ref, s_ref,
    qs, ks, kt, vs, dk, dv, dq, *, scale, block
):
    blocks, _, _, group, size = x_ref.shape
    total = blocks * group
    cosine, signed_sine = cos_ref[...], sin_ref[...]
    plain = [x_ref[:, 0, j].reshape(total, size).astype(f32) for j in range(3)]
    qs[...] = turn_forward(plain[0], cosine, signed_sine).astype(bf16)
    turned = turn_forward(plain[1], cosine, signed_sine)
    ks[...] = turned.astype(bf16)
    kt[...] = turned.T.astype(bf16)
    vs[...] = plain[2].astype(bf16)
    dk[...] = jnp.zeros_like(dk)
    dv[...] = jnp.zeros_like(dv)

    def body(first, last):
        at = pl.ds(first, block)
        span = block // group
        rows = pl.ds(first // group, span)
        weights = weights_t(
            ks[:last], qs[at, :], kpos_ref[:last], qinfo_ref[0, 0:1, at], qinfo_ref[0, 1:2, at], scale
        )
        totals = l_ref[0, 0:1, at]
        grad_t = d_ref[rows, 0].reshape(block, size).astype(f32).T
        out_t = o_ref[rows, 0].reshape(block, size).astype(f32).T
        dlog = -jnp.sum(grad_t * out_t, axis=0, keepdims=True) / totals
        outer_t = (grad_t / totals).astype(bf16)
        dweights = mm(vs[:last], outer_t)
        dscores = (weights * (dweights + dlog)).astype(bf16)
        dk[:last] += mm(dscores, qs[at, :])
        dv[:last] += mm(weights.astype(bf16), outer_t, NT)
        dq[at, :] = mm(kt[:, :last], dscores).T

    over_blocks(total, block, body)
    grads = (
        turn_backward(dq[...] * scale, cosine, signed_sine),
        turn_backward(dk[...] * scale, cosine, signed_sine),
        dv[...],
    )
    sums = []
    for j in range(3):
        g_ref[:, 0, j] = grads[j].astype(bf16).reshape(blocks, group, size)
        sums.append(jnp.sum(grads[j] * plain[j], axis=0, keepdims=True))
    s_ref[0] = jnp.concatenate(sums, axis=0)


def attend_back(pairs, outputs, grads, totals, tables, kpos, qinfo):
    blocks, slots, _, group, size = pairs.shape
    total = blocks * group
    block = math.gcd(total, score_block)
    half = pl.BlockSpec((blocks, 1, group, size), lambda n: (0, n, 0, 0))
    whole = pl.BlockSpec((blocks, 1, 3, group, size), lambda n: (0, n, 0, 0, 0))
    return pl.pallas_call(
        partial(attend_back_kernel, scale=1.0 / math.sqrt(size), block=block),
        grid=(slots,),
        in_specs=[
            whole,
            half,
            half,
            pl.BlockSpec((1, 1, total), lambda n: (n, 0, 0)),
            pl.BlockSpec((total, size), lambda n: (0, 0)),
            pl.BlockSpec((total, size), lambda n: (0, 0)),
            pl.BlockSpec((total, 1), lambda n: (0, 0)),
            pl.BlockSpec((1, 2, total), lambda n: (n, 0, 0)),
        ],
        out_specs=[whole, pl.BlockSpec((1, 3, size), lambda n: (n, 0, 0))],
        out_shape=[
            jax.ShapeDtypeStruct(pairs.shape, bf16),
            jax.ShapeDtypeStruct((slots, 3, size), f32),
        ],
        scratch_shapes=[
            pltpu.VMEM((total, size), bf16),
            pltpu.VMEM((total, size), bf16),
            pltpu.VMEM((size, total), bf16),
            pltpu.VMEM((total, size), bf16),
            pltpu.VMEM((total, size), f32),
            pltpu.VMEM((total, size), f32),
            pltpu.VMEM((total, size), f32),
        ],
        cost_estimate=cost(
            flops=slots * 10 * total * total * size,
            bytes_accessed=slots * total * size * 16,
            transcendentals=slots * total * total // 2,
        ),
        name="attend_back",
    )(pairs, outputs, grads, totals, *tables, kpos, qinfo)


def to_pairs_kernel(*refs, dims):
    x_refs, w_ref, out_ref, xs = refs[:4], refs[4], refs[5], refs[6]
    count = x_refs[0].shape[0]

    @pl.when(jnp.logical_and(pl.program_id(0) == 0, pl.program_id(1) == 0))
    def _():
        for i in range(4):
            xs[i * count:(i + 1) * count] = x_refs[i][...]

    rows, heads, _, pieces, quarter, size = out_ref.shape
    product = mm(xs[...], w_ref[...], dims).astype(bf16)
    for i in range(pieces):
        for r in range(rows):
            at = (i * rows + r) * quarter
            for h in range(heads):
                out_ref[r, h, 0, i] = product[at:at + quarter, h * size:(h + 1) * size]


def project_to_pairs(pieces, weight, dims, parts, heads, size, span):
    rows, quarter, width = pieces[0].shape
    count = rows * quarter
    wide = span * size
    steps = heads // span
    if dims == NN:
        w_spec = pl.BlockSpec((width, wide), lambda j, h: (0, j * steps + h))
    else:
        w_spec = pl.BlockSpec((wide, width), lambda j, h: (j * steps + h, 0))
    return pl.pallas_call(
        partial(to_pairs_kernel, dims=dims),
        grid=(parts, steps),
        in_specs=[pl.BlockSpec(memory_space=pltpu.VMEM)] * 4 + [w_spec],
        out_specs=[
            pl.BlockSpec((rows, span, 1, 4, quarter, size), lambda j, h: (0, h, j, 0, 0, 0)),
            pl.BlockSpec((4 * count, width), lambda j, h: (0, 0)),
        ],
        out_shape=[
            jax.ShapeDtypeStruct((rows, heads, parts, 4, quarter, size), bf16),
            jax.ShapeDtypeStruct((4 * count, width), bf16),
        ],
        cost_estimate=cost(
            flops=8 * count * width * parts * heads * size,
            bytes_accessed=2 * width * (8 * count + parts * heads * size),
            transcendentals=0,
        ),
        name="project_to_pairs",
    )(*[p.reshape(count, width) for p in pieces], weight)


def split_out(product, out_refs, at):
    kept_ref, near_ref, send_ref = out_refs
    half = product.shape[0] // 4
    kept_ref[at:at + half] = product[:half]
    near_ref[at:at + half] = product[half:2 * half]
    for i in range(2):
        send_ref[i, at:at + half] = product[(i + 2) * half:(i + 3) * half]


def split_specs(count, out, block):
    one, two = pl.BlockSpec((count, block), lambda n: (0, n)), pl.BlockSpec((2, count, block), lambda n: (0, 0, n))
    shapes = [(count, out), (count, out), (2, count, out)]
    return [one, one, two], [jax.ShapeDtypeStruct(v, bf16) for v in shapes]


def by_rows(kept, near, send, quarter):
    shape = (kept.shape[0] // quarter, quarter, kept.shape[1])
    return kept.reshape(shape), near.reshape(shape), send.reshape((2,) + shape)


def join_pairs(x_ref, flat_ref):
    rows, heads, parts, pieces, quarter, size = x_ref.shape
    for i in range(pieces):
        for r in range(rows):
            at = (i * rows + r) * quarter
            for j in range(parts):
                for h in range(heads):
                    col = (j * heads + h) * size
                    flat_ref[at:at + quarter, col:col + size] = x_ref[r, h, j, i]


def from_pairs_kernel(x_ref, w_ref, flat_ref, *out_refs):
    @pl.when(pl.program_id(0) == 0)
    def _():
        join_pairs(x_ref, flat_ref)

    split_out(mm(flat_ref[...], w_ref[...]).astype(bf16), out_refs, 0)


def project_from_pairs(pairs, weight, block):
    rows, heads, parts, pieces, quarter, size = pairs.shape
    count, width = rows * quarter, parts * heads * size
    out = weight.shape[1]
    specs, shapes = split_specs(count, out, block)
    flat, *split = pl.pallas_call(
        from_pairs_kernel,
        grid=(out // block,),
        in_specs=[pl.BlockSpec(pairs.shape, lambda n: (0,) * 6), pl.BlockSpec((width, block), lambda n: (0, n))],
        out_specs=[pl.BlockSpec((4 * count, width), lambda n: (0, 0))] + specs,
        out_shape=[jax.ShapeDtypeStruct((4 * count, width), bf16)] + shapes,
        cost_estimate=cost(
            flops=8 * count * width * out, bytes_accessed=2 * (out * width + 4 * count * (2 * width + out)),
            transcendentals=0,
        ),
        name="project_from_pairs",
    )(pairs, weight)
    return flat, by_rows(*split, quarter)


def project_split_kernel(*refs, dims):
    x_refs, w_ref, out_refs = refs[:-4], refs[-4], refs[-3:]
    at = 0
    for x_ref in x_refs:
        split_out(mm(x_ref[...], w_ref[...], dims).astype(bf16), out_refs, at)
        at += x_ref.shape[0] // 4


def project_split(flats, weight, dims, block, quarter):
    width = flats[0].shape[1]
    count = sum(v.shape[0] for v in flats) // 4
    if dims == NN:
        out = weight.shape[1]
        w_spec = pl.BlockSpec((width, block), lambda n: (0, n))
    else:
        out = weight.shape[0]
        w_spec = pl.BlockSpec((block, width), lambda n: (n, 0))
    specs, shapes = split_specs(count, out, block)
    split = pl.pallas_call(
        partial(project_split_kernel, dims=dims),
        grid=(out // block,),
        in_specs=[pl.BlockSpec(v.shape, lambda n: (0, 0)) for v in flats] + [w_spec],
        out_specs=specs,
        out_shape=shapes,
        cost_estimate=cost(
            flops=8 * count * width * out, bytes_accessed=2 * (out * width + 4 * count * (width + out)), transcendentals=0
        ),
        name="project_split",
    )(*flats, weight)
    return by_rows(*split, quarter)


def cotangent_kernel(*refs):
    x_refs, w_ref, out_ref, flat_ref = refs[:4], refs[4], refs[5], refs[6]
    part = x_refs[0].shape[0]
    for i in range(4):
        flat_ref[i * part:(i + 1) * part] = x_refs[i][...]
    out_ref[...] = mm(flat_ref[...], w_ref[...], NT).astype(bf16)


def project_cotangent(pieces, weight, rows, first):
    total, quarter, width = pieces[0].shape
    part = rows * quarter
    at = first // rows
    out = weight.shape[0]
    return pl.pallas_call(
        cotangent_kernel,
        grid=(1,),
        in_specs=[pl.BlockSpec((part, width), lambda c: (at, 0))] * 4 + [pl.BlockSpec((out, width), lambda c: (0, 0))],
        out_specs=[pl.BlockSpec((4 * part, out), lambda c: (0, 0)), pl.BlockSpec((4 * part, width), lambda c: (0, 0))],
        out_shape=[jax.ShapeDtypeStruct((4 * part, out), bf16), jax.ShapeDtypeStruct((4 * part, width), bf16)],
        cost_estimate=cost(
            flops=8 * part * width * out, bytes_accessed=2 * width * (out + 8 * part), transcendentals=0
        ),
        name="project_cotangent",
    )(*[p.reshape(total * quarter, width) for p in pieces], weight)


def assemble(pairs):
    rows, heads, parts, pieces, quarter, size = pairs.shape
    tokens, width = 4 * rows * quarter, parts * heads * size
    return pl.pallas_call(
        join_pairs,
        out_shape=jax.ShapeDtypeStruct((tokens, width), bf16),
        cost_estimate=cost(flops=0, bytes_accessed=4 * tokens * width, transcendentals=0),
        name="assemble",
    )(pairs)


def runs(lengths, cut):
    at = 0
    for k, n in enumerate(lengths):
        start = 0
        while start < n:
            step = min(n - start, cut - at % cut)
            yield k, start, at, step
            start += step
            at += step


def width_of(sizes, pieces):
    return -(-sum(sizes) // (pieces * LANES)) * LANES


def part_of(ref, j, rank, lanes):
    return ref.at[j, :, lanes] if len(ref.shape) == 3 else ref.at[j * rank:(j + 1) * rank, lanes]


def pack_kernel(*refs, plan, counts, vectors):
    total = sum(counts)
    in_refs, sum_refs, out_ref, sums = refs[:total], refs[total:-2], refs[-2], refs[-1]
    rank = out_ref.shape[1]
    sums[...] = jnp.zeros_like(sums)
    row = 0
    for ref in sum_refs:
        for j in range(ref.shape[0]):
            sums[row:row + 1, :ref.shape[2]] = ref[j]
            row += 1
    base = 0
    for entries, cut in plan:
        sizes = [n for _, _, n in entries]
        for k, start, at, n in runs(sizes, cut):
            which, j, _ = entries[k]
            lanes = slice(start, start + n)
            values = sums[:, lanes] if which is None else part_of(in_refs[which], j, rank, lanes)[...]
            out_ref[at // cut, :, base + at % cut:base + at % cut + n] = values.astype(bf16)
        end = sum(sizes)
        while end < out_ref.shape[0] * cut:
            n = cut - end % cut
            out_ref[end // cut, :, base + end % cut:base + end % cut + n] = jnp.zeros((rank, n), bf16)
            end += n
        base += cut


def unpack_kernel(*refs, plan, count):
    x_ref, m_refs, out_refs = refs[0], refs[1:1 + count], refs[1 + count:]
    rank = x_ref.shape[1]
    base = 0
    for entries, cut in plan:
        for k, start, at, n in runs([n for _, _, n in entries], cut):
            values = x_ref[at // cut, :, base + at % cut:base + at % cut + n].astype(f32)
            which, j, _ = entries[k]
            if which is not None:
                part_of(out_refs[which], j, rank, slice(start, start + n))[...] = values
                continue
            row = 0
            for m_ref, out_ref in zip(m_refs, out_refs[-count:]):
                members, size = m_ref.shape
                stop = min(start + n, size)
                if start < stop:
                    out_ref[:, start:stop] = values[row:row + members, :stop - start] / m_ref[:, start:stop]
                row += members
        base += cut


def packing(over_all, over_seq, width, pieces, rank):
    plan, at = [], 0
    for arrays in (over_all, over_seq):
        entries = []
        for v in arrays:
            members = v.shape[0] if len(v.shape) == 3 else v.shape[0] // rank
            entries += [(at, j, v.shape[-1]) for j in range(members)]
            at += 1
        plan.append(entries)
    plan[1].append((None, 0, width))
    return [(entries, width_of([n for _, _, n in entries], pieces)) for entries in plan]


def pack(plan, arrays, vectors, pieces, rank, width):
    return pl.pallas_call(
        partial(pack_kernel, plan=plan, counts=[len(arrays)], vectors=len(vectors)),
        out_shape=jax.ShapeDtypeStruct((pieces, rank, sum(cut for _, cut in plan)), bf16),
        scratch_shapes=[pltpu.VMEM((rank, width), f32)],
        cost_estimate=cost(flops=0, bytes_accessed=4 * sum(v.size for v in arrays), transcendentals=0),
        name="pack",
    )(*arrays, *vectors)


def unpack(plan, values, arrays, magnitudes):
    return pl.pallas_call(
        partial(unpack_kernel, plan=plan, count=len(magnitudes)),
        out_shape=[jax.ShapeDtypeStruct(v.shape, f32) for v in (*arrays, *magnitudes)],
        cost_estimate=cost(flops=0, bytes_accessed=6 * values.size, transcendentals=0),
        name="unpack",
    )(values, *magnitudes)


def gated_kernel(*refs):
    x_refs, w_ref, e_ref, hidden_ref, grads_ref, sums_ref, xs = refs[:4], *refs[4:]
    count = x_refs[0].shape[0]

    @pl.when(pl.program_id(0) == 0)
    def _():
        for i in range(4):
            xs[i * count:(i + 1) * count] = x_refs[i][...]

    product = mm(xs[...], w_ref[...])
    block = LANES
    for k in range(product.shape[1] // (2 * block)):
        at, mine = k * 2 * block, slice(k * block, (k + 1) * block)
        gate, up = product[:, at:at + block], product[:, at + block:at + 2 * block]
        dhid = e_ref[:, mine].astype(f32)
        sig = 1.0 / (1.0 + jnp.exp(-gate))
        act = gate * sig
        hidden_ref[:, mine] = (act * up).astype(bf16)
        dgate = dhid * up * (sig * (1.0 + gate * (1.0 - sig)))
        dup = dhid * act
        grads_ref[:, at:at + block] = dgate.astype(bf16)
        grads_ref[:, at + block:at + 2 * block] = dup.astype(bf16)
        sums_ref[0, :, mine] = jnp.sum(gate * dgate, axis=0, keepdims=True)
        sums_ref[1, :, mine] = jnp.sum(up * dup, axis=0, keepdims=True)


def gated(pieces, weight, dhid):
    rows, quarter, width = pieces[0].shape
    count = rows * quarter
    out = dhid.shape[1]
    block = GATED_BLOCKS * LANES
    return pl.pallas_call(
        gated_kernel,
        grid=(-(-out // block),),
        in_specs=[pl.BlockSpec(memory_space=pltpu.VMEM)] * 4
        + [
            pl.BlockSpec((width, 2 * block), lambda i: (0, i)),
            pl.BlockSpec((4 * count, block), lambda i: (0, i)),
        ],
        out_specs=[
            pl.BlockSpec((4 * count, block), lambda i: (0, i)),
            pl.BlockSpec((4 * count, 2 * block), lambda i: (0, i)),
            pl.BlockSpec((2, 1, block), lambda i: (0, 0, i)),
            pl.BlockSpec((4 * count, width), lambda i: (0, 0)),
        ],
        out_shape=[
            jax.ShapeDtypeStruct((4 * count, out), bf16),
            jax.ShapeDtypeStruct((4 * count, 2 * out), bf16),
            jax.ShapeDtypeStruct((2, 1, out), f32),
            jax.ShapeDtypeStruct((4 * count, width), bf16),
        ],
        cost_estimate=cost(
            flops=16 * count * width * out,
            bytes_accessed=4 * width * out + 8 * count * (2 * width + 4 * out),
            transcendentals=4 * count * out,
        ),
        name="gated",
    )(*[p.reshape(count, width) for p in pieces], weight, dhid)


def chunk_lanes(refs):
    ends = [0]
    for ref in refs:
        ends.append(ends[-1] + ref.shape[0])
    return [slice(a, b) for a, b in zip(ends, ends[1:])]


def column_grads_kernel(*refs, chunks, steps):
    x_refs, d_refs, refs = refs[:chunks], refs[chunks:2 * chunks], refs[2 * chunks:]
    w_ref, a_ref, b_ref, stat_ref, m_ref, sum_ref, cross_ref, gb_ref, ga_ref, ts, dts, es = refs
    members, rank, block = b_ref.shape
    lanes = chunk_lanes(x_refs)
    i = pl.program_id(0)

    @pl.when(i == 0)
    def _():
        for c in range(chunks):
            ts[:, lanes[c]] = mm(a_ref[...], x_refs[c][...], NT).astype(bf16)
        dts[...] = jnp.zeros_like(dts)

    @pl.when(i < steps)
    def _():
        found = sum(mm(ts[:, lanes[c]], d_refs[c][...]) for c in range(chunks))
        spread, along = [], []
        for j in range(members):
            b = b_ref[j].astype(f32)
            scale = stat_ref[j, 1:2]
            coef = -sum_ref[j] / (m_ref[j] * stat_ref[j, 0:1])
            mine = found[j * rank:(j + 1) * rank, j * block:(j + 1) * block]
            gb_ref[j] = (adapter_scale * (mine * scale + coef * cross_ref[j])).astype(bf16)
            empty = jnp.zeros((rank, block), f32)
            row = lambda v: jnp.concatenate([v if k == j else empty for k in range(members)], axis=1)
            spread.append(row(adapter_scale * coef * b))
            along.append(row(adapter_scale * scale * b))
        wide = members * block
        es[:, pl.ds(pl.multiple_of(i * wide, wide), wide)] = jnp.concatenate(spread, axis=0).astype(bf16)
        up = jnp.concatenate(along, axis=0).astype(bf16)
        for c in range(chunks):
            dts[:, lanes[c]] += mm(up, d_refs[c][...], NT)

    @pl.when(i >= steps)
    def _():
        span = w_ref.shape[0]
        at = pl.ds(pl.multiple_of((i - steps) * span, span), span)
        total = mm(es[...], w_ref[...], NT)
        for c in range(chunks):
            total = total + mm(dts[:, lanes[c]].astype(bf16), x_refs[c][:, at])
        ga_ref[...] = total.astype(bf16)


def column_grads(rows, grads, weight, down, up, stat, magnitude, sums, cross, block):
    tokens, width = sum(v.shape[0] for v in rows), rows[0].shape[1]
    members, rank, out = up.shape
    chunks, steps, span = len(rows), out // block, 512
    first = lambda i: jnp.minimum(i, steps - 1)
    then = lambda i: jnp.maximum(i - steps, 0)
    part = lambda n: pl.BlockSpec((members, n, block), lambda i: (0, 0, first(i)))
    wide = members * block
    ranks = members * rank
    grad_b, grad_a = pl.pallas_call(
        partial(column_grads_kernel, chunks=chunks, steps=steps),
        grid=(steps + width // span,),
        in_specs=[pl.BlockSpec(v.shape, lambda i: (0, 0)) for v in rows]
        + [pl.BlockSpec((v.shape[0], wide), lambda i: (0, first(i))) for v in grads]
        + [
            pl.BlockSpec((span, members * out), lambda i: (then(i), 0)),
            pl.BlockSpec((ranks, width), lambda i: (0, 0)),
            part(rank), part(2), part(1), part(1), part(rank),
        ],
        out_specs=[part(rank), pl.BlockSpec((ranks, span), lambda i: (0, then(i)))],
        out_shape=[
            jax.ShapeDtypeStruct((members, rank, out), bf16),
            jax.ShapeDtypeStruct((ranks, width), bf16),
        ],
        scratch_shapes=[
            pltpu.VMEM((ranks, tokens), bf16),
            pltpu.VMEM((ranks, tokens), f32),
            pltpu.VMEM((ranks, members * out), bf16),
        ],
        cost_estimate=cost(
            flops=4 * 256 * width * members * out // 4,
            bytes_accessed=2 * (width * members * out + tokens * (width + members * out)),
            transcendentals=0,
        ),
        name="column_grads",
    )(*rows, *grads, weight, down.transpose(0, 2, 1).reshape(ranks, width), up, stat, magnitude[:, None, :], sums, cross)
    return grad_a, grad_b


def row_grads_kernel(*refs, chunks):
    h_refs, d_refs, refs = refs[:chunks], refs[chunks:2 * chunks], refs[2 * chunks:]
    w_ref, a_ref, b_ref, stat_ref, coef_ref, ga_ref, gb_ref, ts, dts, acc = refs
    lanes = chunk_lanes(h_refs)
    i = pl.program_id(0)

    @pl.when(i == 0)
    def _():
        for c in range(chunks):
            ts[:, lanes[c]] = mm(a_ref[...], h_refs[c][...], NT).astype(bf16)
        dts[...] = jnp.zeros_like(dts)
        acc[...] = jnp.zeros_like(acc)

    b = b_ref[...].astype(f32)
    coef = coef_ref[...]
    found = sum(mm(ts[:, lanes[c]], d_refs[c][...]) for c in range(chunks))
    gb_ref[...] = (adapter_scale * (found + coef * stat_ref[...])).astype(bf16)
    up = (adapter_scale * b).astype(bf16)
    for c in range(chunks):
        dts[:, lanes[c]] += mm(up, d_refs[c][...], NT)
    acc[...] += mm((adapter_scale * coef * b).astype(bf16), w_ref[...], NT)

    @pl.when(i == pl.num_programs(0) - 1)
    def _():
        total = acc[...]
        for c in range(chunks):
            total = total + mm(dts[:, lanes[c]].astype(bf16), h_refs[c][...])
        ga_ref[...] = total.astype(bf16)


def row_grads(rows, grads, weight, down, up, stat, coef, block):
    tokens, count = sum(v.shape[0] for v in rows), rows[0].shape[1]
    rank, out = up.shape
    chunks = len(rows)
    along = lambda n: pl.BlockSpec((n, block), lambda i: (0, i))
    return pl.pallas_call(
        partial(row_grads_kernel, chunks=chunks),
        grid=(out // block,),
        in_specs=[pl.BlockSpec(v.shape, lambda i: (0, 0)) for v in rows]
        + [pl.BlockSpec((v.shape[0], block), lambda i: (0, i)) for v in grads]
        + [along(count), pl.BlockSpec((rank, count), lambda i: (0, 0)), along(rank), along(rank), along(1)],
        out_specs=[pl.BlockSpec((rank, count), lambda i: (0, 0)), along(rank)],
        out_shape=[jax.ShapeDtypeStruct((rank, count), bf16), jax.ShapeDtypeStruct((rank, out), bf16)],
        scratch_shapes=[
            pltpu.VMEM((rank, tokens), bf16),
            pltpu.VMEM((rank, tokens), f32),
            pltpu.VMEM((rank, count), f32),
        ],
        cost_estimate=cost(
            flops=256 * count * out, bytes_accessed=2 * (count * out + tokens * (count + out)), transcendentals=0
        ),
        name="row_grads",
    )(*rows, *grads, weight, down.T, up, stat, coef)


def norm_scale(values):
    return lax.rsqrt(jnp.mean(values * values, axis=-1, keepdims=True) + epsilon)


def norm_back(values, gain, grad):
    r = norm_scale(values)
    weighted = gain * grad
    return r * weighted - values * (r * r * r) * jnp.mean(values * weighted, axis=-1, keepdims=True)


def rotary_tables(positions, head_size):
    half_size = head_size // 2
    frequency = rope_base ** (-(2.0 * jnp.arange(half_size, dtype=f32)) / head_size)
    angles = positions.astype(f32)[:, None] * frequency[None, :]
    cosine, sine = jnp.cos(angles), jnp.sin(angles)
    return (jnp.concatenate([cosine, cosine], axis=-1), jnp.concatenate([-sine, sine], axis=-1))


def local(
    layer_in, cotangent, doc_lengths, pad_counts, gain_attn, gain_ffn, w_qkv, a_qkv, b_qkv, m_qkv, w_out, a_out,
    b_out, m_out, w_gateup, a_gateup, b_gateup, m_gateup, w_down, a_down, b_down, m_down,
):
    rows, quarter, width = layer_in.shape
    tensor, seq = lax.axis_size("tensor"), lax.axis_size("seq")
    assert tensor == len(PIECES)
    me_t, me_s = lax.axis_index("tensor"), lax.axis_index("seq")
    group = quarter * tensor
    total = group * seq
    feat = w_qkv.shape[2]
    heads = feat // HEAD_DIM
    rank = a_qkv.shape[2]
    ff = w_down.shape[0]
    piece_of = jnp.bitwise_xor(me_t, jnp.array(PIECES, jnp.int32))
    in_block = (piece_of[:, None] * quarter + jnp.arange(quarter, dtype=jnp.int32)[None, :]).reshape(group)
    positions = (jnp.arange(seq, dtype=jnp.int32)[:, None] * group + in_block[None, :]).reshape(total)
    tables = rotary_tables(positions, HEAD_DIM)
    offsets = jnp.cumsum(doc_lengths, axis=1)
    starts = jnp.max(
        jnp.where(offsets[:, :, None] <= positions[None, None, :], offsets[:, :, None], 0), axis=1
    )
    kpos = positions[:, None]
    few = rows // 3
    cuts = [slice(rows - few, rows), slice(0, rows - few)]
    span = range(2)
    pair_counts = [(at.stop - at.start) * heads for at in cuts]
    slots = [-(-count // seq) for count in pair_counts]
    mine = [me_s * slots[c] + jnp.arange(slots[c]) for c in span]
    live = [mine[c] < pair_counts[c] for c in span]

    def pair_info(c):
        row = jnp.minimum(mine[c] // heads + cuts[c].start, cuts[c].stop - 1)
        chosen = (row[:, None] == jnp.arange(rows)[None, :])[:, :, None]
        return jnp.stack(
            [jnp.broadcast_to(positions[None], (slots[c], total)), jnp.sum(jnp.where(chosen, starts[None], 0), axis=1)],
            axis=1,
        )

    qinfo = [pair_info(c) for c in span]

    def send_pairs(values, c):
        parts = values.shape[2]
        laid = values.reshape(pair_counts[c], parts, group, HEAD_DIM)
        if slots[c] * seq > pair_counts[c]:
            laid = jnp.pad(laid, ((0, slots[c] * seq - pair_counts[c]), (0, 0), (0, 0), (0, 0)))
        return exchange(laid.reshape(seq, slots[c], parts, group, HEAD_DIM))

    def fetch_pairs(values, c):
        parts = values.shape[2]
        laid = exchange(values).reshape(seq * slots[c], parts, group, HEAD_DIM)[:pair_counts[c]]
        return laid.reshape(pair_counts[c] // heads, heads, parts, tensor, quarter, HEAD_DIM)

    def to_heads(pieces, weight):
        return project_to_pairs(pieces, weight, NN, 3, heads, HEAD_DIM, heads)

    def back_to_heads(pieces, weight):
        return project_to_pairs(pieces, weight, NT, 1, heads, HEAD_DIM, 2)

    owned = me_s * group + me_t * quarter + jnp.arange(quarter, dtype=jnp.int32)
    valid = (owned[None, :] < total - pad_counts[:, None]).astype(f32)
    cot = cotangent.astype(f32) * valid[:, :, None]
    wide_in = [layer_in[at].astype(f32) for at in cuts]

    def normed(values, gain):
        return (values * norm_scale(values) * gain).astype(bf16)

    started = [gather_start(normed(wide_in[c], gain_attn)) for c in span]
    qkv_w, qkv_stat, qkv_cross = column_prep(w_qkv, a_qkv, b_qkv, m_qkv, 256, False)
    started[0], qkv_w = after(started[0], qkv_w)
    normed_a, d_qkv, pairs, outputs, totals, att = [[None] * 2 for _ in range(6)]
    laid, normed_a[0] = to_heads(gather_end(*started[0]), qkv_w)

    laid, started[1], w_out, w_down = after(laid, started[1], w_out, w_down)
    pairs[0] = send_pairs(laid, 0)
    laid, normed_a[1] = to_heads(gather_end(*started[1]), qkv_w)
    down_w, down_cross, down_square = row_prep(w_down, a_down, b_down, 256)
    out_w, out_cross, out_square = row_prep(w_out, a_out, b_out, 512)
    pairs[0], laid, down_square, out_square, w_gateup = after(pairs[0], laid, down_square, out_square, w_gateup)

    u_out, middle, hidden, d_gu, gu_sum, normed_f, d_mid, du_out, dhid, du_down = [[None] * 2 for _ in range(10)]

    def of_cotangent(whole, c):
        return project_cotangent(whole, down_w, cuts[c].stop - cuts[c].start, cuts[c].start)

    pairs[1] = send_pairs(laid, 1)
    outputs[0], totals[0] = attend(pairs[0], tables, kpos, qinfo[0])
    squares = tensor_sum(jnp.concatenate([down_square, out_square]))
    down_square, out_square = squares[0:1], squares[1:2]
    down_scale, out_scale = m_down / jnp.sqrt(squares[0]), m_out / jnp.sqrt(squares[1])
    scaled, w_gateup = after((cot * down_scale).astype(bf16), w_gateup)
    gu_w, gu_stat, gu_cross = column_prep(w_gateup, a_gateup, b_gateup, m_gateup, LANES, True)
    started, gu_w = after(gather_start(scaled), gu_w)
    whole_cot = gather_end(*started)
    dhid[0], du_down[0] = of_cotangent(whole_cot, 0)
    pairs[1], outputs[0], dhid[0] = after(pairs[1], outputs[0], dhid[0])

    fetched = fetch_pairs(outputs[0][:, :, None], 0)
    outputs[1], totals[1] = attend(pairs[1], tables, kpos, qinfo[1])
    fetched, outputs[1], whole_cot = after(fetched, outputs[1], whole_cot)

    returned = fetch_pairs(outputs[1][:, :, None], 1)
    att[0], split = project_from_pairs(fetched, out_w, 512)
    moving, whole_cot = after(scatter_start(*split), whole_cot)
    dhid[1], du_down[1] = of_cotangent(whole_cot, 1)
    tail, dhid[1] = after(scatter_end(*moving), dhid[1])
    u_out[0] = tail * out_scale
    middle[0] = wide_in[0] + u_out[0]
    started = gather_start(normed(middle[0], gain_ffn))

    att[1], split = project_from_pairs(returned, out_w, 512)
    started, split = after(started, split)
    moving, whole = after(scatter_start(*split), gather_end(*started))
    hidden[0], d_gu[0], gu_sum[0], normed_f[0] = gated(whole, gu_w, dhid[0])
    tail, d_gu[0] = after(scatter_end(*moving), d_gu[0])
    u_out[1] = tail * out_scale
    middle[1] = wide_in[1] + u_out[1]
    h_f, d_gu[0] = after(normed(middle[1], gain_ffn), d_gu[0])
    started = gather_start(h_f)
    split = project_split([d_gu[0]], gu_w, NT, 512, quarter)
    whole, behind = after(gather_end(*started), scatter_start(*split))

    hidden[1], d_gu[1], gu_sum[1], normed_f[1] = gated(whole, gu_w, dhid[1])
    tail, d_gu[1] = after(scatter_end(*behind), d_gu[1])
    d_mid[0] = cot[cuts[0]] + norm_back(middle[0], gain_ffn, tail)
    scaled, d_gu[1] = after((d_mid[0] * out_scale).astype(bf16), d_gu[1])
    started, split = after(gather_start(scaled), project_split([d_gu[1]], gu_w, NT, 512, quarter))
    moving, whole = after(scatter_start(*split), gather_end(*started))

    d_att, du_out[0] = back_to_heads(whole, out_w)
    d_outputs = send_pairs(d_att, 0)[:, :, 0]
    tail, d_att = after(scatter_end(*moving), d_att)
    d_mid[1] = cot[cuts[1]] + norm_back(middle[1], gain_ffn, tail)
    scaled, d_outputs = after((d_mid[1] * out_scale).astype(bf16), d_outputs)
    d_pairs, pair_sums = [None] * 2, [None] * 2
    d_pairs[0], pair_sums[0] = attend_back(pairs[0], outputs[0], d_outputs, totals[0], tables, kpos, qinfo[0])
    d_pairs[0], scaled, hidden = after(d_pairs[0], scaled, hidden)
    fetched = fetch_pairs(d_pairs[0], 0)
    started, split = after(gather_start(scaled), project_split(hidden[::-1], down_w, NN, 512, quarter))
    d_att, du_out[1] = back_to_heads(gather_end(*started), out_w)
    d_att, fetched = after(d_att, fetched)

    d_att, att, out_sum = after(d_att, att, sum(jnp.sum(u_out[c] * d_mid[c], axis=(0, 1)) for c in span)[None])
    d_outputs = send_pairs(d_att, 1)[:, :, 0]
    out_sum = tensor_sum(out_sum)
    grad_a_out, grad_b_out = row_grads(att, du_out, out_w, a_out, b_out, out_cross, -out_sum / out_square, 512)
    d_outputs, grad_a_out, d_gu = after(d_outputs, grad_a_out, d_gu)
    d_pairs[1], pair_sums[1] = attend_back(pairs[1], outputs[1], d_outputs, totals[1], tables, kpos, qinfo[1])

    d_pairs[1], split, d_gu = after(d_pairs[1], split, d_gu)
    returned = fetch_pairs(d_pairs[1], 1)
    moving, d_gu = after(scatter_start(*split), d_gu)
    gu_sums = sum(gu_sum)
    grad_a_gu, grad_b_gu = column_grads(
        normed_f, d_gu, gu_w, a_gateup, b_gateup, gu_stat, m_gateup, gu_sums, gu_cross, LANES
    )
    tail, grad_a_gu, fetched = after(scatter_end(*moving), grad_a_gu, fetched)
    u_down = tail * down_scale
    layer_out = (jnp.concatenate(middle[::-1]) + u_down).astype(bf16)
    down_sum = tensor_sum(jnp.sum(u_down * cot, axis=(0, 1))[None])
    d_qkv[0] = assemble(fetched)
    grad_a_down, grad_b_down = row_grads(
        hidden, du_down, down_w, a_down, b_down, down_cross, -down_sum / down_square, 512
    )
    fetched, d_qkv[0], grad_a_down, layer_out = after(returned, d_qkv[0], grad_a_down, layer_out)
    d_qkv[1] = assemble(fetched)

    qkv_sums = 0.0
    for c in span:
        choice = jnp.logical_and((mine[c] % heads)[:, None] == jnp.arange(heads)[None, :], live[c][:, None])
        qkv_sums = qkv_sums + jnp.sum(jnp.where(choice[:, None, :, None], pair_sums[c][:, :, None, :], 0.0), axis=0)
    qkv_sums = qkv_sums.reshape(3, 1, feat)
    grad_a_qkv, grad_b_qkv = column_grads(
        normed_a, d_qkv, qkv_w, a_qkv, b_qkv, qkv_stat, m_qkv, qkv_sums, qkv_cross, feat
    )

    over_all = [grad_a_gu, grad_b_out, grad_b_down, grad_a_qkv]
    over_seq = [grad_b_gu, grad_a_out, grad_a_down, grad_b_qkv]
    vectors = [gu_sums, out_sum[None], down_sum[None], qkv_sums]
    plan = packing(over_all, over_seq, width, seq, rank)
    cut = plan[0][1]
    packed, d_qkv = after(pack(plan, over_all + over_seq, vectors, seq, rank, width), d_qkv)
    added, split = after(exchange(packed), project_split(d_qkv[::-1], qkv_w, NT, 512, quarter))
    moving = scatter_start(*split)
    added = jnp.sum(added.astype(f32), axis=0).astype(bf16)
    shared = added[:, :cut]
    shared = shared.astype(f32) + swap(shared, 1).astype(f32) + swap(shared, 2).astype(f32) + swap(shared, 3).astype(f32)
    joined, moving = after(jnp.concatenate([shared.astype(bf16), added[:, cut:]], axis=1), moving)
    back = seq_gather(joined)
    grad_in = jnp.concatenate(d_mid[::-1]) + norm_back(layer_in.astype(f32), gain_attn, scatter_end(*moving))
    g_a_gu, g_b_out, g_b_down, g_a_qkv, g_b_gu, g_a_out, g_a_down, g_b_qkv, s_gu, s_out, s_down, s_qkv = unpack(
        plan, back, over_all + over_seq, [m_gateup, m_out[None], m_down[None], m_qkv]
    )
    return (
        layer_out,
        grad_in,
        g_a_qkv.reshape(3, rank, width).transpose(0, 2, 1),
        g_b_qkv,
        s_qkv,
        g_a_out.T,
        g_b_out,
        s_out[0],
        g_a_gu.reshape(2, rank, width).transpose(0, 2, 1),
        g_b_gu,
        s_gu,
        g_a_down.T,
        g_b_down,
        s_down[0],
    )


def solution(mesh):
    split = P(None, ("seq", "tensor"), None)
    in_specs = (
        split, split, P(), P(), P(), P(),
        P(None, None, "tensor"), P(), P(None, None, "tensor"), P(None, "tensor"),
        P("tensor", None), P("tensor", None), P(), P(),
        P(None, None, "tensor"), P(), P(None, None, "tensor"), P(None, "tensor"),
        P("tensor", None), P("tensor", None), P(), P(),
    )
    out_specs = (
        split, split,
        P(), P(None, None, "tensor"), P(None, "tensor"),
        P("tensor", None), P(), P(),
        P(), P(None, None, "tensor"), P(None, "tensor"),
        P("tensor", None), P(), P(),
    )
    return jax.shard_map(local, mesh=mesh, in_specs=in_specs, out_specs=out_specs, check_vma=False)
```

```python
from functools import partial
import math

import jax
import jax.numpy as jnp
from jax import lax
from jax.experimental import pallas as pl
from jax.experimental.pallas import tpu as pltpu
from jax.sharding import PartitionSpec as P

HEAD_DIM = 128
LANES = 128
epsilon = 1e-05
adapter_scale = 2.0
rope_base = 10000.0
f32 = jnp.float32
bf16 = jnp.bfloat16
PIECES = (0, 2, 1, 3)
score_block = 256
GATED_BLOCKS = 2
NT = (((1,), (1,)), ((), ()))
NN = (((1,), (0,)), ((), ()))
TN = (((0,), (0,)), ((), ()))


def cost(flops, bytes_accessed, transcendentals):
    return pl.CostEstimate(flops=flops // 64, bytes_accessed=bytes_accessed // 64, transcendentals=0)


def mm(a, b, dims=NN):
    return lax.dot_general(a, b, dims, preferred_element_type=f32)


def swap(values, bit):
    size = lax.axis_size("tensor")
    return lax.ppermute(values, "tensor", [(i, i ^ bit) for i in range(size)])


def gather_start(shard):
    return shard, swap(shard, 2), swap(shard, 1)


def gather_end(shard, far, near):
    return [shard, far, near, swap(far, 1)]


def scatter_start(kept, near, send):
    got = swap(send, 1)
    return kept, got, (near.astype(f32) + got[1].astype(f32)).astype(bf16)


def scatter_end(kept, got, passed):
    return kept.astype(f32) + got[0].astype(f32) + swap(passed, 2).astype(f32)


def after(value, *others):
    return lax.optimization_barrier((value, *others))


def tensor_sum(values):
    return values + swap(values, 1) + swap(values, 2) + swap(values, 3)


def exchange(values):
    return lax.all_to_all(values, "seq", 0, 0, tiled=True)


def seq_gather(values):
    size = lax.axis_size("seq")
    return exchange(jnp.broadcast_to(values[None], (size,) + values.shape))


def column_prep_kernel(w_ref, a_ref, b_ref, m_ref, out_ref, stat_ref, cross_ref):
    members, width, block = w_ref.shape
    rank = cross_ref.shape[1]
    product = mm(a_ref[...], b_ref[0], TN)
    i = pl.program_id(0)
    for j in range(members):
        heading = w_ref[j].astype(f32) + adapter_scale * product[:, j * block:(j + 1) * block]
        norm = jnp.sqrt(jnp.sum(heading * heading, axis=0, keepdims=True))
        scale = m_ref[j] / norm
        scaled = (heading * scale).astype(bf16)
        if out_ref.shape[1] == members * block:
            out_ref[:, j * block:(j + 1) * block] = scaled
        else:
            out_ref[:, pl.ds(pl.multiple_of(j * (out_ref.shape[1] // members) + i * block, block), block)] = scaled
        stat_ref[j] = jnp.concatenate([norm, scale], axis=0)
        cross_ref[j] = mm(a_ref[j * rank:(j + 1) * rank, :], scaled)


def column_prep(weight, down, up, magnitude, block, alternate):
    members, width, out = weight.shape
    rank = down.shape[2]
    wide = members * block
    eye = jnp.eye(members, dtype=bf16)[:, None, None, :, None]
    blocks = up.reshape(members, rank, out // block, 1, block) * eye
    blocks = blocks.transpose(2, 0, 1, 3, 4).reshape(out // block, members * rank, wide)
    flat = down.transpose(0, 2, 1).reshape(members * rank, width)
    if alternate:
        scaled_spec = pl.BlockSpec((width, wide), lambda i: (0, i))
    else:
        scaled_spec = pl.BlockSpec((width, members * out), lambda i: (0, 0))
    return pl.pallas_call(
        column_prep_kernel,
        grid=(out // block,),
        in_specs=[
            pl.BlockSpec((members, width, block), lambda i: (0, 0, i)),
            pl.BlockSpec((members * rank, width), lambda i: (0, 0)),
            pl.BlockSpec((1, members * rank, wide), lambda i: (i, 0, 0)),
            pl.BlockSpec((members, 1, block), lambda i: (0, 0, i)),
        ],
        out_specs=[
            scaled_spec,
            pl.BlockSpec((members, 2, block), lambda i: (0, 0, i)),
            pl.BlockSpec((members, rank, block), lambda i: (0, 0, i)),
        ],
        out_shape=[
            jax.ShapeDtypeStruct((width, members * out), bf16),
            jax.ShapeDtypeStruct((members, 2, out), f32),
            jax.ShapeDtypeStruct((members, rank, out), f32),
        ],
        cost_estimate=cost(
            flops=4 * members * width * out * 256, bytes_accessed=4 * members * width * out, transcendentals=0
        ),
        name="column_prep",
    )(weight, flat, blocks, magnitude[:, None, :])


def row_prep_kernel(w_ref, a_ref, b_ref, out_ref, cross_ref, square_ref):
    heading = w_ref[...].astype(f32) + adapter_scale * mm(a_ref[...], b_ref[...], TN)
    narrow = heading.astype(bf16)
    out_ref[...] = narrow
    cross_ref[...] = mm(a_ref[...], narrow)
    square_ref[...] = jnp.sum(heading * heading, axis=0, keepdims=True)


def row_prep(weight, down, up, block):
    rows, out = weight.shape
    rank = down.shape[1]
    along = lambda n: pl.BlockSpec((n, block), lambda i: (0, i))
    return pl.pallas_call(
        row_prep_kernel,
        grid=(out // block,),
        in_specs=[along(rows), pl.BlockSpec((rank, rows), lambda i: (0, 0)), along(rank)],
        out_specs=[along(rows), along(rank), along(1)],
        out_shape=[
            jax.ShapeDtypeStruct((rows, out), bf16),
            jax.ShapeDtypeStruct((rank, out), f32),
            jax.ShapeDtypeStruct((1, out), f32),
        ],
        cost_estimate=cost(flops=2 * rows * out * 256, bytes_accessed=4 * rows * out, transcendentals=0),
        name="row_prep",
    )(weight, down.T, up)


def turn_forward(values, cosine, signed_sine):
    return values * cosine + pltpu.roll(values, values.shape[1] // 2, 1) * signed_sine


def turn_backward(values, cosine, signed_sine):
    return values * cosine + pltpu.roll(values * signed_sine, values.shape[1] // 2, 1)


def over_blocks(total, block, body):
    if total // block <= 4:
        for i in range(total // block):
            body(i * block, (i + 1) * block)
    else:

        def step(i, carry):
            body(pl.multiple_of(i * block, block), total)
            return carry

        lax.fori_loop(0, total // block, step, 0)


def weights_t(keys, queries, kpos, qpos, qstart, scale):
    scores = mm(keys, queries, NT)
    allowed = jnp.logical_and(kpos <= qpos, kpos >= qstart)
    return jnp.where(allowed, jnp.exp(scores * scale), 0.0)


def attend_kernel(x_ref, cos_ref, sin_ref, kpos_ref, qinfo_ref, o_ref, l_ref, qs, ks, vt, os, *, scale, block):
    blocks, _, _, group, size = x_ref.shape
    total = blocks * group
    cosine, signed_sine = cos_ref[...], sin_ref[...]
    qs[...] = turn_forward(x_ref[:, 0, 0].reshape(total, size).astype(f32), cosine, signed_sine).astype(bf16)
    ks[...] = turn_forward(x_ref[:, 0, 1].reshape(total, size).astype(f32), cosine, signed_sine).astype(bf16)
    vt[...] = x_ref[:, 0, 2].reshape(total, size).astype(f32).T.astype(bf16)

    def body(first, last):
        at = pl.ds(first, block)
        weights = weights_t(
            ks[:last], qs[at, :], kpos_ref[:last], qinfo_ref[0, 0:1, at], qinfo_ref[0, 1:2, at], scale
        )
        totals = jnp.sum(weights, axis=0, keepdims=True)
        outer = mm(vt[:, :last], weights.astype(bf16))
        l_ref[0, 0:1, at] = totals
        os[at, :] = (outer / totals).T.astype(bf16)

    over_blocks(total, block, body)
    o_ref[:, 0] = os[...].reshape(blocks, group, size)


def attend(pairs, tables, kpos, qinfo):
    blocks, slots, _, group, size = pairs.shape
    total = blocks * group
    block = math.gcd(total, score_block)
    return pl.pallas_call(
        partial(attend_kernel, scale=1.0 / math.sqrt(size), block=block),
        grid=(slots,),
        in_specs=[
            pl.BlockSpec((blocks, 1, 3, group, size), lambda n: (0, n, 0, 0, 0)),
            pl.BlockSpec((total, size), lambda n: (0, 0)),
            pl.BlockSpec((total, size), lambda n: (0, 0)),
            pl.BlockSpec((total, 1), lambda n: (0, 0)),
            pl.BlockSpec((1, 2, total), lambda n: (n, 0, 0)),
        ],
        out_specs=[
            pl.BlockSpec((blocks, 1, group, size), lambda n: (0, n, 0, 0)),
            pl.BlockSpec((1, 1, total), lambda n: (n, 0, 0)),
        ],
        out_shape=[
            jax.ShapeDtypeStruct((blocks, slots, group, size), bf16),
            jax.ShapeDtypeStruct((slots, 1, total), f32),
        ],
        scratch_shapes=[
            pltpu.VMEM((total, size), bf16),
            pltpu.VMEM((total, size), bf16),
            pltpu.VMEM((size, total), bf16),
            pltpu.VMEM((total, size), bf16),
        ],
        cost_estimate=cost(
            flops=slots * 4 * total * total * size,
            bytes_accessed=slots * total * size * 8,
            transcendentals=slots * total * total // 2,
        ),
        name="attend",
    )(pairs, *tables, kpos, qinfo)


def attend_back_kernel(
    x_ref, o_ref, d_ref, l_ref, cos_ref, sin_ref, kpos_ref, qinfo_ref, g_ref, s_ref,
    qs, ks, kt, vs, dk, dv, dq, *, scale, block
):
    blocks, _, _, group, size = x_ref.shape
    total = blocks * group
    cosine, signed_sine = cos_ref[...], sin_ref[...]
    plain = [x_ref[:, 0, j].reshape(total, size).astype(f32) for j in range(3)]
    qs[...] = turn_forward(plain[0], cosine, signed_sine).astype(bf16)
    turned = turn_forward(plain[1], cosine, signed_sine)
    ks[...] = turned.astype(bf16)
    kt[...] = turned.T.astype(bf16)
    vs[...] = plain[2].astype(bf16)
    dk[...] = jnp.zeros_like(dk)
    dv[...] = jnp.zeros_like(dv)

    def body(first, last):
        at = pl.ds(first, block)
        span = block // group
        rows = pl.ds(first // group, span)
        weights = weights_t(
            ks[:last], qs[at, :], kpos_ref[:last], qinfo_ref[0, 0:1, at], qinfo_ref[0, 1:2, at], scale
        )
        totals = l_ref[0, 0:1, at]
        grad_t = d_ref[rows, 0].reshape(block, size).astype(f32).T
        out_t = o_ref[rows, 0].reshape(block, size).astype(f32).T
        dlog = -jnp.sum(grad_t * out_t, axis=0, keepdims=True) / totals
        outer_t = (grad_t / totals).astype(bf16)
        dweights = mm(vs[:last], outer_t)
        dscores = (weights * (dweights + dlog)).astype(bf16)
        dk[:last] += mm(dscores, qs[at, :])
        dv[:last] += mm(weights.astype(bf16), outer_t, NT)
        dq[at, :] = mm(kt[:, :last], dscores).T

    over_blocks(total, block, body)
    grads = (
        turn_backward(dq[...] * scale, cosine, signed_sine),
        turn_backward(dk[...] * scale, cosine, signed_sine),
        dv[...],
    )
    sums = []
    for j in range(3):
        g_ref[:, 0, j] = grads[j].astype(bf16).reshape(blocks, group, size)
        sums.append(jnp.sum(grads[j] * plain[j], axis=0, keepdims=True))
    s_ref[0] = jnp.concatenate(sums, axis=0)


def attend_back(pairs, outputs, grads, totals, tables, kpos, qinfo):
    blocks, slots, _, group, size = pairs.shape
    total = blocks * group
    block = math.gcd(total, score_block)
    half = pl.BlockSpec((blocks, 1, group, size), lambda n: (0, n, 0, 0))
    whole = pl.BlockSpec((blocks, 1, 3, group, size), lambda n: (0, n, 0, 0, 0))
    return pl.pallas_call(
        partial(attend_back_kernel, scale=1.0 / math.sqrt(size), block=block),
        grid=(slots,),
        in_specs=[
            whole,
            half,
            half,
            pl.BlockSpec((1, 1, total), lambda n: (n, 0, 0)),
            pl.BlockSpec((total, size), lambda n: (0, 0)),
            pl.BlockSpec((total, size), lambda n: (0, 0)),
            pl.BlockSpec((total, 1), lambda n: (0, 0)),
            pl.BlockSpec((1, 2, total), lambda n: (n, 0, 0)),
        ],
        out_specs=[whole, pl.BlockSpec((1, 3, size), lambda n: (n, 0, 0))],
        out_shape=[
            jax.ShapeDtypeStruct(pairs.shape, bf16),
            jax.ShapeDtypeStruct((slots, 3, size), f32),
        ],
        scratch_shapes=[
            pltpu.VMEM((total, size), bf16),
            pltpu.VMEM((total, size), bf16),
            pltpu.VMEM((size, total), bf16),
            pltpu.VMEM((total, size), bf16),
            pltpu.VMEM((total, size), f32),
            pltpu.VMEM((total, size), f32),
            pltpu.VMEM((total, size), f32),
        ],
        cost_estimate=cost(
            flops=slots * 10 * total * total * size,
            bytes_accessed=slots * total * size * 16,
            transcendentals=slots * total * total // 2,
        ),
        name="attend_back",
    )(pairs, outputs, grads, totals, *tables, kpos, qinfo)


def to_pairs_kernel(*refs, dims):
    x_refs, w_ref, out_ref, xs = refs[:4], refs[4], refs[5], refs[6]
    count = x_refs[0].shape[0]

    @pl.when(jnp.logical_and(pl.program_id(0) == 0, pl.program_id(1) == 0))
    def _():
        for i in range(4):
            xs[i * count:(i + 1) * count] = x_refs[i][...]

    rows, heads, _, pieces, quarter, size = out_ref.shape
    product = mm(xs[...], w_ref[...], dims).astype(bf16)
    for i in range(pieces):
        for r in range(rows):
            at = (i * rows + r) * quarter
            for h in range(heads):
                out_ref[r, h, 0, i] = product[at:at + quarter, h * size:(h + 1) * size]


def project_to_pairs(pieces, weight, dims, parts, heads, size, span):
    rows, quarter, width = pieces[0].shape
    count = rows * quarter
    wide = span * size
    steps = heads // span
    if dims == NN:
        w_spec = pl.BlockSpec((width, wide), lambda j, h: (0, j * steps + h))
    else:
        w_spec = pl.BlockSpec((wide, width), lambda j, h: (j * steps + h, 0))
    return pl.pallas_call(
        partial(to_pairs_kernel, dims=dims),
        grid=(parts, steps),
        in_specs=[pl.BlockSpec(memory_space=pltpu.VMEM)] * 4 + [w_spec],
        out_specs=[
            pl.BlockSpec((rows, span, 1, 4, quarter, size), lambda j, h: (0, h, j, 0, 0, 0)),
            pl.BlockSpec((4 * count, width), lambda j, h: (0, 0)),
        ],
        out_shape=[
            jax.ShapeDtypeStruct((rows, heads, parts, 4, quarter, size), bf16),
            jax.ShapeDtypeStruct((4 * count, width), bf16),
        ],
        cost_estimate=cost(
            flops=8 * count * width * parts * heads * size,
            bytes_accessed=2 * width * (8 * count + parts * heads * size),
            transcendentals=0,
        ),
        name="project_to_pairs",
    )(*[p.reshape(count, width) for p in pieces], weight)


def split_out(product, out_refs, at):
    kept_ref, near_ref, send_ref = out_refs
    half = product.shape[0] // 4
    kept_ref[at:at + half] = product[:half]
    near_ref[at:at + half] = product[half:2 * half]
    for i in range(2):
        send_ref[i, at:at + half] = product[(i + 2) * half:(i + 3) * half]


def split_specs(count, out, block):
    one, two = pl.BlockSpec((count, block), lambda n: (0, n)), pl.BlockSpec((2, count, block), lambda n: (0, 0, n))
    shapes = [(count, out), (count, out), (2, count, out)]
    return [one, one, two], [jax.ShapeDtypeStruct(v, bf16) for v in shapes]


def by_rows(kept, near, send, quarter):
    shape = (kept.shape[0] // quarter, quarter, kept.shape[1])
    return kept.reshape(shape), near.reshape(shape), send.reshape((2,) + shape)


def join_pairs(x_ref, flat_ref):
    rows, heads, parts, pieces, quarter, size = x_ref.shape
    for i in range(pieces):
        for r in range(rows):
            at = (i * rows + r) * quarter
            for j in range(parts):
                for h in range(heads):
                    col = (j * heads + h) * size
                    flat_ref[at:at + quarter, col:col + size] = x_ref[r, h, j, i]


def from_pairs_kernel(x_ref, w_ref, flat_ref, *out_refs):
    @pl.when(pl.program_id(0) == 0)
    def _():
        join_pairs(x_ref, flat_ref)

    split_out(mm(flat_ref[...], w_ref[...]).astype(bf16), out_refs, 0)


def project_from_pairs(pairs, weight, block):
    rows, heads, parts, pieces, quarter, size = pairs.shape
    count, width = rows * quarter, parts * heads * size
    out = weight.shape[1]
    specs, shapes = split_specs(count, out, block)
    flat, *split = pl.pallas_call(
        from_pairs_kernel,
        grid=(out // block,),
        in_specs=[pl.BlockSpec(pairs.shape, lambda n: (0,) * 6), pl.BlockSpec((width, block), lambda n: (0, n))],
        out_specs=[pl.BlockSpec((4 * count, width), lambda n: (0, 0))] + specs,
        out_shape=[jax.ShapeDtypeStruct((4 * count, width), bf16)] + shapes,
        cost_estimate=cost(
            flops=8 * count * width * out, bytes_accessed=2 * (out * width + 4 * count * (2 * width + out)),
            transcendentals=0,
        ),
        name="project_from_pairs",
    )(pairs, weight)
    return flat, by_rows(*split, quarter)


def project_split_kernel(*refs, dims):
    x_refs, w_ref, out_refs = refs[:-4], refs[-4], refs[-3:]
    at = 0
    for x_ref in x_refs:
        split_out(mm(x_ref[...], w_ref[...], dims).astype(bf16), out_refs, at)
        at += x_ref.shape[0] // 4


def project_split(flats, weight, dims, block, quarter):
    width = flats[0].shape[1]
    count = sum(v.shape[0] for v in flats) // 4
    if dims == NN:
        out = weight.shape[1]
        w_spec = pl.BlockSpec((width, block), lambda n: (0, n))
    else:
        out = weight.shape[0]
        w_spec = pl.BlockSpec((block, width), lambda n: (n, 0))
    specs, shapes = split_specs(count, out, block)
    split = pl.pallas_call(
        partial(project_split_kernel, dims=dims),
        grid=(out // block,),
        in_specs=[pl.BlockSpec(v.shape, lambda n: (0, 0)) for v in flats] + [w_spec],
        out_specs=specs,
        out_shape=shapes,
        cost_estimate=cost(
            flops=8 * count * width * out, bytes_accessed=2 * (out * width + 4 * count * (width + out)), transcendentals=0
        ),
        name="project_split",
    )(*flats, weight)
    return by_rows(*split, quarter)


def cotangent_kernel(*refs):
    x_refs, w_ref, out_ref, flat_ref = refs[:4], refs[4], refs[5], refs[6]
    part = x_refs[0].shape[0]
    for i in range(4):
        flat_ref[i * part:(i + 1) * part] = x_refs[i][...]
    out_ref[...] = mm(flat_ref[...], w_ref[...], NT).astype(bf16)


def project_cotangent(pieces, weight, rows, first):
    total, quarter, width = pieces[0].shape
    part = rows * quarter
    at = first // rows
    out = weight.shape[0]
    return pl.pallas_call(
        cotangent_kernel,
        grid=(1,),
        in_specs=[pl.BlockSpec((part, width), lambda c: (at, 0))] * 4 + [pl.BlockSpec((out, width), lambda c: (0, 0))],
        out_specs=[pl.BlockSpec((4 * part, out), lambda c: (0, 0)), pl.BlockSpec((4 * part, width), lambda c: (0, 0))],
        out_shape=[jax.ShapeDtypeStruct((4 * part, out), bf16), jax.ShapeDtypeStruct((4 * part, width), bf16)],
        cost_estimate=cost(
            flops=8 * part * width * out, bytes_accessed=2 * width * (out + 8 * part), transcendentals=0
        ),
        name="project_cotangent",
    )(*[p.reshape(total * quarter, width) for p in pieces], weight)


def assemble(pairs):
    rows, heads, parts, pieces, quarter, size = pairs.shape
    tokens, width = 4 * rows * quarter, parts * heads * size
    return pl.pallas_call(
        join_pairs,
        out_shape=jax.ShapeDtypeStruct((tokens, width), bf16),
        cost_estimate=cost(flops=0, bytes_accessed=4 * tokens * width, transcendentals=0),
        name="assemble",
    )(pairs)


def runs(lengths, cut):
    at = 0
    for k, n in enumerate(lengths):
        start = 0
        while start < n:
            step = min(n - start, cut - at % cut)
            yield k, start, at, step
            start += step
            at += step


def width_of(sizes, pieces):
    return -(-sum(sizes) // (pieces * LANES)) * LANES


def part_of(ref, j, rank, lanes):
    return ref.at[j, :, lanes] if len(ref.shape) == 3 else ref.at[j * rank:(j + 1) * rank, lanes]


def cells(shapes):
    return [(v, j, c) for v, (members, size) in enumerate(shapes) for j in range(members) for c in range(size // LANES)]


def pack_kernel(*refs, plan, count):
    in_refs, sum_refs, out_ref, sums = refs[:count], refs[count:-2], refs[-2], refs[-1]
    rank = out_ref.shape[1]
    sums[...] = jnp.zeros_like(sums)
    for k, (v, j, c) in enumerate(cells([(ref.shape[0], ref.shape[2]) for ref in sum_refs])):
        at = k // rank * LANES
        sums[k % rank:k % rank + 1, at:at + LANES] = sum_refs[v][j, :, c * LANES:(c + 1) * LANES]
    base = 0
    for entries, cut in plan:
        sizes = [n for _, _, n in entries]
        for k, start, at, n in runs(sizes, cut):
            which, j, _ = entries[k]
            lanes = slice(start, start + n)
            values = sums[:, lanes] if which is None else part_of(in_refs[which], j, rank, lanes)[...]
            out_ref[at // cut, :, base + at % cut:base + at % cut + n] = values.astype(bf16)
        end = sum(sizes)
        while end < out_ref.shape[0] * cut:
            n = cut - end % cut
            out_ref[end // cut, :, base + end % cut:base + end % cut + n] = jnp.zeros((rank, n), bf16)
            end += n
        base += cut


def unpack_kernel(*refs, plan, count):
    x_ref, m_refs, out_refs = refs[0], refs[1:1 + count], refs[1 + count:]
    rank = x_ref.shape[1]
    base = 0
    for entries, cut in plan:
        for k, start, at, n in runs([n for _, _, n in entries], cut):
            values = x_ref[at // cut, :, base + at % cut:base + at % cut + n].astype(f32)
            which, j, _ = entries[k]
            if which is not None:
                part_of(out_refs[which], j, rank, slice(start, start + n))[...] = values
                continue
            for cell, (v, j, c) in enumerate(cells([ref.shape for ref in m_refs])):
                lane = cell // rank * LANES - start
                if 0 <= lane < n:
                    place = (slice(j, j + 1), slice(c * LANES, (c + 1) * LANES))
                    row = slice(cell % rank, cell % rank + 1)
                    out_refs[v - count][place] = values[row, lane:lane + LANES] / m_refs[v][place]
        base += cut


def packing(over_all, over_seq, vectors, pieces, rank):
    plan, at = [], 0
    for arrays in (over_all, over_seq):
        entries = []
        for v in arrays:
            members = v.shape[0] if len(v.shape) == 3 else v.shape[0] // rank
            entries += [(at, j, v.shape[-1]) for j in range(members)]
            at += 1
        plan.append(entries)
    blocks = len(cells([(v.shape[0], v.shape[2]) for v in vectors]))
    plan[1].append((None, 0, -(-blocks // rank) * LANES))
    return [(entries, width_of([n for _, _, n in entries], pieces)) for entries in plan]


def pack(plan, arrays, vectors, pieces, rank):
    return pl.pallas_call(
        partial(pack_kernel, plan=plan, count=len(arrays)),
        out_shape=jax.ShapeDtypeStruct((pieces, rank, sum(cut for _, cut in plan)), bf16),
        scratch_shapes=[pltpu.VMEM((rank, plan[1][0][-1][2]), f32)],
        cost_estimate=cost(flops=0, bytes_accessed=4 * sum(v.size for v in arrays), transcendentals=0),
        name="pack",
    )(*arrays, *vectors)


def unpack(plan, values, arrays, magnitudes):
    return pl.pallas_call(
        partial(unpack_kernel, plan=plan, count=len(magnitudes)),
        out_shape=[jax.ShapeDtypeStruct(v.shape, f32) for v in (*arrays, *magnitudes)],
        cost_estimate=cost(flops=0, bytes_accessed=6 * values.size, transcendentals=0),
        name="unpack",
    )(values, *magnitudes)


def gated_kernel(*refs):
    x_refs, w_ref, e_ref, hidden_ref, grads_ref, sums_ref, xs = refs[:4], *refs[4:]
    count = x_refs[0].shape[0]

    @pl.when(pl.program_id(0) == 0)
    def _():
        for i in range(4):
            xs[i * count:(i + 1) * count] = x_refs[i][...]

    product = mm(xs[...], w_ref[...])
    block = LANES
    for k in range(product.shape[1] // (2 * block)):
        at, mine = k * 2 * block, slice(k * block, (k + 1) * block)
        gate, up = product[:, at:at + block], product[:, at + block:at + 2 * block]
        dhid = e_ref[:, mine].astype(f32)
        sig = 1.0 / (1.0 + jnp.exp(-gate))
        act = gate * sig
        hidden_ref[:, mine] = (act * up).astype(bf16)
        dgate = dhid * up * (sig * (1.0 + gate * (1.0 - sig)))
        dup = dhid * act
        grads_ref[:, at:at + block] = dgate.astype(bf16)
        grads_ref[:, at + block:at + 2 * block] = dup.astype(bf16)
        sums_ref[0, :, mine] = jnp.sum(gate * dgate, axis=0, keepdims=True)
        sums_ref[1, :, mine] = jnp.sum(up * dup, axis=0, keepdims=True)


def gated(pieces, weight, dhid):
    rows, quarter, width = pieces[0].shape
    count = rows * quarter
    out = dhid.shape[1]
    block = GATED_BLOCKS * LANES
    return pl.pallas_call(
        gated_kernel,
        grid=(-(-out // block),),
        in_specs=[pl.BlockSpec(memory_space=pltpu.VMEM)] * 4
        + [
            pl.BlockSpec((width, 2 * block), lambda i: (0, i)),
            pl.BlockSpec((4 * count, block), lambda i: (0, i)),
        ],
        out_specs=[
            pl.BlockSpec((4 * count, block), lambda i: (0, i)),
            pl.BlockSpec((4 * count, 2 * block), lambda i: (0, i)),
            pl.BlockSpec((2, 1, block), lambda i: (0, 0, i)),
            pl.BlockSpec((4 * count, width), lambda i: (0, 0)),
        ],
        out_shape=[
            jax.ShapeDtypeStruct((4 * count, out), bf16),
            jax.ShapeDtypeStruct((4 * count, 2 * out), bf16),
            jax.ShapeDtypeStruct((2, 1, out), f32),
            jax.ShapeDtypeStruct((4 * count, width), bf16),
        ],
        cost_estimate=cost(
            flops=16 * count * width * out,
            bytes_accessed=4 * width * out + 8 * count * (2 * width + 4 * out),
            transcendentals=4 * count * out,
        ),
        name="gated",
    )(*[p.reshape(count, width) for p in pieces], weight, dhid)


def chunk_lanes(refs):
    ends = [0]
    for ref in refs:
        ends.append(ends[-1] + ref.shape[0])
    return [slice(a, b) for a, b in zip(ends, ends[1:])]


def column_grads_kernel(*refs, chunks, steps, joins):
    x_refs, d_refs, refs = refs[:chunks], list(refs[chunks:2 * chunks]), list(refs[2 * chunks:])
    if joins:
        pairs_ref, d_refs[-1] = d_refs[-1], refs.pop(9)

        @pl.when(pl.program_id(0) == 0)
        def _():
            join_pairs(pairs_ref, d_refs[-1])

    w_ref, a_ref, b_ref, stat_ref, m_ref, sum_ref, cross_ref, gb_ref, ga_ref, ts, dts, es = refs
    members, rank, block = b_ref.shape
    lanes = chunk_lanes(x_refs)
    i = pl.program_id(0)

    @pl.when(i == 0)
    def _():
        for c in range(chunks):
            ts[:, lanes[c]] = mm(a_ref[...], x_refs[c][...], NT).astype(bf16)
        dts[...] = jnp.zeros_like(dts)

    @pl.when(i < steps)
    def _():
        found = sum(mm(ts[:, lanes[c]], d_refs[c][...]) for c in range(chunks))
        spread, along = [], []
        for j in range(members):
            b = b_ref[j].astype(f32)
            scale = stat_ref[j, 1:2]
            coef = -sum_ref[j] / (m_ref[j] * stat_ref[j, 0:1])
            mine = found[j * rank:(j + 1) * rank, j * block:(j + 1) * block]
            gb_ref[j] = (adapter_scale * (mine * scale + coef * cross_ref[j])).astype(bf16)
            empty = jnp.zeros((rank, block), f32)
            row = lambda v: jnp.concatenate([v if k == j else empty for k in range(members)], axis=1)
            spread.append(row(adapter_scale * coef * b))
            along.append(row(adapter_scale * scale * b))
        wide = members * block
        es[:, pl.ds(pl.multiple_of(i * wide, wide), wide)] = jnp.concatenate(spread, axis=0).astype(bf16)
        up = jnp.concatenate(along, axis=0).astype(bf16)
        for c in range(chunks):
            dts[:, lanes[c]] += mm(up, d_refs[c][...], NT)

    @pl.when(i >= steps)
    def _():
        span = w_ref.shape[0]
        at = pl.ds(pl.multiple_of((i - steps) * span, span), span)
        total = mm(es[...], w_ref[...], NT)
        for c in range(chunks):
            total = total + mm(dts[:, lanes[c]].astype(bf16), x_refs[c][:, at])
        ga_ref[...] = total.astype(bf16)


def column_grads(rows, grads, weight, down, up, stat, magnitude, sums, cross, block):
    tokens, width = sum(v.shape[0] for v in rows), rows[0].shape[1]
    members, rank, out = up.shape
    chunks, steps, span = len(rows), out // block, 512
    first = lambda i: jnp.minimum(i, steps - 1)
    then = lambda i: jnp.maximum(i - steps, 0)
    part = lambda n: pl.BlockSpec((members, n, block), lambda i: (0, 0, first(i)))
    joins = len(grads[-1].shape) == 6
    joined = (rows[-1].shape[0], members * out)
    wide = members * block
    ranks = members * rank
    assert steps == 1 or not joins
    grad_b, grad_a, *flat = pl.pallas_call(
        partial(column_grads_kernel, chunks=chunks, steps=steps, joins=joins),
        grid=(steps + width // span,),
        in_specs=[pl.BlockSpec(v.shape, lambda i: (0, 0)) for v in rows]
        + [
            pl.BlockSpec(v.shape, lambda i: (0,) * 6) if len(v.shape) == 6
            else pl.BlockSpec((v.shape[0], wide), lambda i: (0, first(i)))
            for v in grads
        ]
        + [
            pl.BlockSpec((span, members * out), lambda i: (then(i), 0)),
            pl.BlockSpec((ranks, width), lambda i: (0, 0)),
            part(rank), part(2), part(1), part(1), part(rank),
        ],
        out_specs=[part(rank), pl.BlockSpec((ranks, span), lambda i: (0, then(i)))]
        + [pl.BlockSpec(joined, lambda i: (0, 0))] * joins,
        out_shape=[
            jax.ShapeDtypeStruct((members, rank, out), bf16),
            jax.ShapeDtypeStruct((ranks, width), bf16),
        ]
        + [jax.ShapeDtypeStruct(joined, bf16)] * joins,
        scratch_shapes=[
            pltpu.VMEM((ranks, tokens), bf16),
            pltpu.VMEM((ranks, tokens), f32),
            pltpu.VMEM((ranks, members * out), bf16),
        ],
        cost_estimate=cost(
            flops=4 * 256 * width * members * out // 4,
            bytes_accessed=2 * (width * members * out + tokens * (width + members * out)),
            transcendentals=0,
        ),
        name="column_grads",
    )(*rows, *grads, weight, down.transpose(0, 2, 1).reshape(ranks, width), up, stat, magnitude[:, None, :], sums, cross)
    return (grad_a, grad_b, *flat)


def row_grads_kernel(*refs, chunks):
    h_refs, d_refs, refs = refs[:chunks], refs[chunks:2 * chunks], refs[2 * chunks:]
    w_ref, a_ref, b_ref, stat_ref, coef_ref, ga_ref, gb_ref, ts, dts, acc = refs
    lanes = chunk_lanes(h_refs)
    i = pl.program_id(0)

    @pl.when(i == 0)
    def _():
        for c in range(chunks):
            ts[:, lanes[c]] = mm(a_ref[...], h_refs[c][...], NT).astype(bf16)
        dts[...] = jnp.zeros_like(dts)
        acc[...] = jnp.zeros_like(acc)

    b = b_ref[...].astype(f32)
    coef = coef_ref[...]
    found = sum(mm(ts[:, lanes[c]], d_refs[c][...]) for c in range(chunks))
    gb_ref[...] = (adapter_scale * (found + coef * stat_ref[...])).astype(bf16)
    up = (adapter_scale * b).astype(bf16)
    for c in range(chunks):
        dts[:, lanes[c]] += mm(up, d_refs[c][...], NT)
    acc[...] += mm((adapter_scale * coef * b).astype(bf16), w_ref[...], NT)

    @pl.when(i == pl.num_programs(0) - 1)
    def _():
        total = acc[...]
        for c in range(chunks):
            total = total + mm(dts[:, lanes[c]].astype(bf16), h_refs[c][...])
        ga_ref[...] = total.astype(bf16)


def row_grads(rows, grads, weight, down, up, stat, coef, block):
    tokens, count = sum(v.shape[0] for v in rows), rows[0].shape[1]
    rank, out = up.shape
    chunks = len(rows)
    along = lambda n: pl.BlockSpec((n, block), lambda i: (0, i))
    return pl.pallas_call(
        partial(row_grads_kernel, chunks=chunks),
        grid=(out // block,),
        in_specs=[pl.BlockSpec(v.shape, lambda i: (0, 0)) for v in rows]
        + [pl.BlockSpec((v.shape[0], block), lambda i: (0, i)) for v in grads]
        + [along(count), pl.BlockSpec((rank, count), lambda i: (0, 0)), along(rank), along(rank), along(1)],
        out_specs=[pl.BlockSpec((rank, count), lambda i: (0, 0)), along(rank)],
        out_shape=[jax.ShapeDtypeStruct((rank, count), bf16), jax.ShapeDtypeStruct((rank, out), bf16)],
        scratch_shapes=[
            pltpu.VMEM((rank, tokens), bf16),
            pltpu.VMEM((rank, tokens), f32),
            pltpu.VMEM((rank, count), f32),
        ],
        cost_estimate=cost(
            flops=256 * count * out, bytes_accessed=2 * (count * out + tokens * (count + out)), transcendentals=0
        ),
        name="row_grads",
    )(*rows, *grads, weight, down.T, up, stat, coef)


def norm_scale(values):
    return lax.rsqrt(jnp.mean(values * values, axis=-1, keepdims=True) + epsilon)


def norm_back(values, gain, grad):
    r = norm_scale(values)
    weighted = gain * grad
    return r * weighted - values * (r * r * r) * jnp.mean(values * weighted, axis=-1, keepdims=True)


def rotary_tables(positions, head_size):
    half_size = head_size // 2
    frequency = rope_base ** (-(2.0 * jnp.arange(half_size, dtype=f32)) / head_size)
    angles = positions.astype(f32)[:, None] * frequency[None, :]
    cosine, sine = jnp.cos(angles), jnp.sin(angles)
    return (jnp.concatenate([cosine, cosine], axis=-1), jnp.concatenate([-sine, sine], axis=-1))


def local(
    layer_in, cotangent, doc_lengths, pad_counts, gain_attn, gain_ffn, w_qkv, a_qkv, b_qkv, m_qkv, w_out, a_out,
    b_out, m_out, w_gateup, a_gateup, b_gateup, m_gateup, w_down, a_down, b_down, m_down,
):
    rows, quarter, width = layer_in.shape
    tensor, seq = lax.axis_size("tensor"), lax.axis_size("seq")
    assert tensor == len(PIECES)
    me_t, me_s = lax.axis_index("tensor"), lax.axis_index("seq")
    group = quarter * tensor
    total = group * seq
    feat = w_qkv.shape[2]
    heads = feat // HEAD_DIM
    rank = a_qkv.shape[2]
    ff = w_down.shape[0]
    piece_of = jnp.bitwise_xor(me_t, jnp.array(PIECES, jnp.int32))
    in_block = (piece_of[:, None] * quarter + jnp.arange(quarter, dtype=jnp.int32)[None, :]).reshape(group)
    positions = (jnp.arange(seq, dtype=jnp.int32)[:, None] * group + in_block[None, :]).reshape(total)
    tables = rotary_tables(positions, HEAD_DIM)
    offsets = jnp.cumsum(doc_lengths, axis=1)
    starts = jnp.max(
        jnp.where(offsets[:, :, None] <= positions[None, None, :], offsets[:, :, None], 0), axis=1
    )
    kpos = positions[:, None]
    few = rows // 3
    cuts = [slice(rows - few, rows), slice(0, rows - few)]
    span = range(2)
    pair_counts = [(at.stop - at.start) * heads for at in cuts]
    slots = [-(-count // seq) for count in pair_counts]
    mine = [me_s * slots[c] + jnp.arange(slots[c]) for c in span]
    live = [mine[c] < pair_counts[c] for c in span]

    def pair_info(c):
        row = jnp.minimum(mine[c] // heads + cuts[c].start, cuts[c].stop - 1)
        chosen = (row[:, None] == jnp.arange(rows)[None, :])[:, :, None]
        return jnp.stack(
            [jnp.broadcast_to(positions[None], (slots[c], total)), jnp.sum(jnp.where(chosen, starts[None], 0), axis=1)],
            axis=1,
        )

    qinfo = [pair_info(c) for c in span]

    def send_pairs(values, c):
        parts = values.shape[2]
        laid = values.reshape(pair_counts[c], parts, group, HEAD_DIM)
        if slots[c] * seq > pair_counts[c]:
            laid = jnp.pad(laid, ((0, slots[c] * seq - pair_counts[c]), (0, 0), (0, 0), (0, 0)))
        return exchange(laid.reshape(seq, slots[c], parts, group, HEAD_DIM))

    def fetch_pairs(values, c):
        parts = values.shape[2]
        laid = exchange(values).reshape(seq * slots[c], parts, group, HEAD_DIM)[:pair_counts[c]]
        return laid.reshape(pair_counts[c] // heads, heads, parts, tensor, quarter, HEAD_DIM)

    def to_heads(pieces, weight):
        return project_to_pairs(pieces, weight, NN, 3, heads, HEAD_DIM, heads)

    def back_to_heads(pieces, weight):
        return project_to_pairs(pieces, weight, NT, 1, heads, HEAD_DIM, 2)

    owned = me_s * group + me_t * quarter + jnp.arange(quarter, dtype=jnp.int32)
    valid = (owned[None, :] < total - pad_counts[:, None]).astype(f32)
    cot = cotangent.astype(f32) * valid[:, :, None]
    wide_in = [layer_in[at].astype(f32) for at in cuts]

    def normed(values, gain):
        return (values * norm_scale(values) * gain).astype(bf16)

    started = [gather_start(normed(wide_in[c], gain_attn)) for c in span]
    qkv_w, qkv_stat, qkv_cross = column_prep(w_qkv, a_qkv, b_qkv, m_qkv, 256, False)
    started[0], qkv_w = after(started[0], qkv_w)
    normed_a, d_qkv, pairs, outputs, totals, att = [[None] * 2 for _ in range(6)]
    laid, normed_a[0] = to_heads(gather_end(*started[0]), qkv_w)

    laid, started[1], w_down = after(laid, started[1], w_down)
    pairs[0] = send_pairs(laid, 0)
    laid, normed_a[1] = to_heads(gather_end(*started[1]), qkv_w)
    down_w, down_cross, down_square = row_prep(w_down, a_down, b_down, 256)
    pairs[0], laid, down_square, w_out, w_gateup = after(pairs[0], laid, down_square, w_out, w_gateup)

    u_out, middle, hidden, d_gu, gu_sum, normed_f, d_mid, du_out, dhid, du_down = [[None] * 2 for _ in range(10)]

    def of_cotangent(whole, c):
        return project_cotangent(whole, down_w, cuts[c].stop - cuts[c].start, cuts[c].start)

    pairs[1] = send_pairs(laid, 1)
    outputs[0], totals[0] = attend(pairs[0], tables, kpos, qinfo[0])
    down_square = tensor_sum(down_square)
    down_scale = m_down / jnp.sqrt(down_square[0])
    scaled, w_gateup, w_out = after((cot * down_scale).astype(bf16), w_gateup, w_out)
    out_w, out_cross, out_square = row_prep(w_out, a_out, b_out, 512)
    gu_w, gu_stat, gu_cross = column_prep(w_gateup, a_gateup, b_gateup, m_gateup, LANES, True)
    started, gu_w, out_w = after(gather_start(scaled), gu_w, out_w)
    whole_cot = gather_end(*started)
    pairs[1], outputs[0], whole_cot, out_square = after(pairs[1], outputs[0], whole_cot, out_square)

    fetched = fetch_pairs(outputs[0][:, :, None], 0)
    outputs[1], totals[1] = attend(pairs[1], tables, kpos, qinfo[1])
    out_square = tensor_sum(out_square)
    out_scale = m_out / jnp.sqrt(out_square[0])
    fetched, outputs[1], whole_cot, out_scale = after(fetched, outputs[1], whole_cot, out_scale)

    returned = fetch_pairs(outputs[1][:, :, None], 1)
    att[0], split = project_from_pairs(fetched, out_w, 512)
    moving, whole_cot = after(scatter_start(*split), whole_cot)
    for c in span:
        dhid[c], du_down[c] = of_cotangent(whole_cot, c)
    tail, dhid = after(scatter_end(*moving), dhid)
    u_out[0] = tail * out_scale
    middle[0] = wide_in[0] + u_out[0]
    started = gather_start(normed(middle[0], gain_ffn))

    att[1], split = project_from_pairs(returned, out_w, 512)
    started, split = after(started, split)
    moving, whole = after(scatter_start(*split), gather_end(*started))
    hidden[0], d_gu[0], gu_sum[0], normed_f[0] = gated(whole, gu_w, dhid[0])
    tail, d_gu[0] = after(scatter_end(*moving), d_gu[0])
    u_out[1] = tail * out_scale
    middle[1] = wide_in[1] + u_out[1]
    h_f, d_gu[0] = after(normed(middle[1], gain_ffn), d_gu[0])
    started = gather_start(h_f)
    split = project_split([d_gu[0]], gu_w, NT, 512, quarter)
    whole, behind = after(gather_end(*started), scatter_start(*split))

    hidden[1], d_gu[1], gu_sum[1], normed_f[1] = gated(whole, gu_w, dhid[1])
    tail, d_gu[1] = after(scatter_end(*behind), d_gu[1])
    d_mid[0] = cot[cuts[0]] + norm_back(middle[0], gain_ffn, tail)
    scaled, d_gu[1] = after((d_mid[0] * out_scale).astype(bf16), d_gu[1])
    started, split = after(gather_start(scaled), project_split([d_gu[1]], gu_w, NT, 512, quarter))
    moving, whole = after(scatter_start(*split), gather_end(*started))

    d_att, du_out[0] = back_to_heads(whole, out_w)
    d_outputs = send_pairs(d_att, 0)[:, :, 0]
    tail, d_att = after(scatter_end(*moving), d_att)
    d_mid[1] = cot[cuts[1]] + norm_back(middle[1], gain_ffn, tail)
    scaled, d_outputs = after((d_mid[1] * out_scale).astype(bf16), d_outputs)
    d_pairs, pair_sums = [None] * 2, [None] * 2
    d_pairs[0], pair_sums[0] = attend_back(pairs[0], outputs[0], d_outputs, totals[0], tables, kpos, qinfo[0])
    d_pairs[0], scaled, hidden = after(d_pairs[0], scaled, hidden)
    fetched = fetch_pairs(d_pairs[0], 0)
    started, split = after(gather_start(scaled), project_split(hidden[::-1], down_w, NN, 512, quarter))
    d_att, du_out[1] = back_to_heads(gather_end(*started), out_w)
    d_att, fetched = after(d_att, fetched)

    d_att, att, out_sum = after(d_att, att, sum(jnp.sum(u_out[c] * d_mid[c], axis=(0, 1)) for c in span)[None])
    d_outputs = send_pairs(d_att, 1)[:, :, 0]
    out_sum = tensor_sum(out_sum)
    grad_a_out, grad_b_out = row_grads(att, du_out, out_w, a_out, b_out, out_cross, -out_sum / out_square, 512)
    d_outputs, grad_a_out, d_gu = after(d_outputs, grad_a_out, d_gu)
    d_pairs[1], pair_sums[1] = attend_back(pairs[1], outputs[1], d_outputs, totals[1], tables, kpos, qinfo[1])

    d_pairs[1], split, d_gu = after(d_pairs[1], split, d_gu)
    returned = fetch_pairs(d_pairs[1], 1)
    moving, d_gu = after(scatter_start(*split), d_gu)
    gu_sums = sum(gu_sum)
    grad_a_gu, grad_b_gu = column_grads(
        normed_f, d_gu, gu_w, a_gateup, b_gateup, gu_stat, m_gateup, gu_sums, gu_cross, LANES
    )
    tail, grad_a_gu, fetched = after(scatter_end(*moving), grad_a_gu, fetched)
    u_down = tail * down_scale
    layer_out = (jnp.concatenate(middle[::-1]) + u_down).astype(bf16)
    down_sum = tensor_sum(jnp.sum(u_down * cot, axis=(0, 1))[None])
    d_qkv[0] = assemble(fetched)
    grad_a_down, grad_b_down = row_grads(
        hidden, du_down, down_w, a_down, b_down, down_cross, -down_sum / down_square, 512
    )
    fetched, d_qkv[0], grad_a_down, layer_out = after(returned, d_qkv[0], grad_a_down, layer_out)

    qkv_sums = 0.0
    for c in span:
        choice = jnp.logical_and((mine[c] % heads)[:, None] == jnp.arange(heads)[None, :], live[c][:, None])
        qkv_sums = qkv_sums + jnp.sum(jnp.where(choice[:, None, :, None], pair_sums[c][:, :, None, :], 0.0), axis=0)
    qkv_sums = qkv_sums.reshape(3, 1, feat)
    grad_a_qkv, grad_b_qkv, d_qkv[1] = column_grads(
        normed_a, [d_qkv[0], fetched], qkv_w, a_qkv, b_qkv, qkv_stat, m_qkv, qkv_sums, qkv_cross, feat
    )

    over_all = [grad_a_gu, grad_b_out, grad_b_down, grad_a_qkv]
    over_seq = [grad_b_gu, grad_a_out, grad_a_down, grad_b_qkv]
    vectors = [gu_sums, out_sum[None], down_sum[None], qkv_sums]
    plan = packing(over_all, over_seq, vectors, seq, rank)
    cut = plan[0][1]
    packed, d_qkv = after(pack(plan, over_all + over_seq, vectors, seq, rank), d_qkv)
    added, split = after(exchange(packed), project_split(d_qkv[::-1], qkv_w, NT, 512, quarter))
    moving = scatter_start(*split)
    added = jnp.sum(added.astype(f32), axis=0).astype(bf16)
    shared = added[:, :cut]
    shared = shared.astype(f32) + swap(shared, 1).astype(f32) + swap(shared, 2).astype(f32) + swap(shared, 3).astype(f32)
    joined, moving = after(jnp.concatenate([shared.astype(bf16), added[:, cut:]], axis=1), moving)
    back = seq_gather(joined)
    grad_in = jnp.concatenate(d_mid[::-1]) + norm_back(layer_in.astype(f32), gain_attn, scatter_end(*moving))
    g_a_gu, g_b_out, g_b_down, g_a_qkv, g_b_gu, g_a_out, g_a_down, g_b_qkv, s_gu, s_out, s_down, s_qkv = unpack(
        plan, back, over_all + over_seq, [m_gateup, m_out[None], m_down[None], m_qkv]
    )
    return (
        layer_out,
        grad_in,
        g_a_qkv.reshape(3, rank, width).transpose(0, 2, 1),
        g_b_qkv,
        s_qkv,
        g_a_out.T,
        g_b_out,
        s_out[0],
        g_a_gu.reshape(2, rank, width).transpose(0, 2, 1),
        g_b_gu,
        s_gu,
        g_a_down.T,
        g_b_down,
        s_down[0],
    )


def solution(mesh):
    split = P(None, ("seq", "tensor"), None)
    in_specs = (
        split, split, P(), P(), P(), P(),
        P(None, None, "tensor"), P(), P(None, None, "tensor"), P(None, "tensor"),
        P("tensor", None), P("tensor", None), P(), P(),
        P(None, None, "tensor"), P(), P(None, None, "tensor"), P(None, "tensor"),
        P("tensor", None), P("tensor", None), P(), P(),
    )
    out_specs = (
        split, split,
        P(), P(None, None, "tensor"), P(None, "tensor"),
        P("tensor", None), P(), P(),
        P(), P(None, None, "tensor"), P(None, "tensor"),
        P("tensor", None), P(), P(),
    )
    return jax.shard_map(local, mesh=mesh, in_specs=in_specs, out_specs=out_specs, check_vma=False)
```

```python
from functools import partial
import math

import jax
import jax.numpy as jnp
from jax import lax
from jax.experimental import pallas as pl
from jax.experimental.pallas import tpu as pltpu
from jax.sharding import PartitionSpec as P

HEAD_DIM = 128
LANES = 128
epsilon = 1e-05
adapter_scale = 2.0
rope_base = 10000.0
f32 = jnp.float32
bf16 = jnp.bfloat16
PIECES = (0, 2, 1, 3)
score_block = 256
GATED_BLOCKS = 3
LOG2_E = math.log2(math.e)
NT = (((1,), (1,)), ((), ()))
NN = (((1,), (0,)), ((), ()))
TN = (((0,), (0,)), ((), ()))


def cost(flops, bytes_accessed, transcendentals):
    return pl.CostEstimate(flops=flops // 64, bytes_accessed=bytes_accessed // 64, transcendentals=0)


def mm(a, b, dims=NN):
    return lax.dot_general(a, b, dims, preferred_element_type=f32)


def swap(values, bit):
    size = lax.axis_size("tensor")
    return lax.ppermute(values, "tensor", [(i, i ^ bit) for i in range(size)])


def gather_start(shard):
    return shard, swap(shard, 2), swap(shard, 1)


def gather_end(shard, far, near):
    return [shard, far, near, swap(far, 1)]


def scatter_start(kept, near, send):
    got = swap(send, 1)
    return kept, got, (near.astype(f32) + got[1].astype(f32)).astype(bf16)


def scatter_end(kept, got, passed):
    return kept.astype(f32) + got[0].astype(f32) + swap(passed, 2).astype(f32)


def after(value, *others):
    return lax.optimization_barrier((value, *others))


def tensor_sum(values):
    return values + swap(values, 1) + swap(values, 2) + swap(values, 3)


def exchange(values):
    return lax.all_to_all(values, "seq", 0, 0, tiled=True)


def seq_gather(values):
    size = lax.axis_size("seq")
    return exchange(jnp.broadcast_to(values[None], (size,) + values.shape))


def column_prep_kernel(w_ref, a_ref, b_ref, m_ref, out_ref, stat_ref, cross_ref):
    members, width, block = w_ref.shape
    rank = cross_ref.shape[1]
    product = mm(a_ref[...], b_ref[0], TN)
    i = pl.program_id(0)
    for j in range(members):
        heading = w_ref[j].astype(f32) + adapter_scale * product[:, j * block:(j + 1) * block]
        norm = jnp.sqrt(jnp.sum(heading * heading, axis=0, keepdims=True))
        scale = m_ref[j] / norm
        scaled = (heading * scale).astype(bf16)
        if out_ref.shape[1] == members * block:
            out_ref[:, j * block:(j + 1) * block] = scaled
        else:
            out_ref[:, pl.ds(pl.multiple_of(j * (out_ref.shape[1] // members) + i * block, block), block)] = scaled
        stat_ref[j] = jnp.concatenate([norm, scale], axis=0)
        cross_ref[j] = mm(a_ref[j * rank:(j + 1) * rank, :], scaled)


def column_prep(weight, down, up, magnitude, block, alternate):
    members, width, out = weight.shape
    rank = down.shape[2]
    wide = members * block
    eye = jnp.eye(members, dtype=bf16)[:, None, None, :, None]
    blocks = up.reshape(members, rank, out // block, 1, block) * eye
    blocks = blocks.transpose(2, 0, 1, 3, 4).reshape(out // block, members * rank, wide)
    flat = down.transpose(0, 2, 1).reshape(members * rank, width)
    if alternate:
        scaled_spec = pl.BlockSpec((width, wide), lambda i: (0, i))
    else:
        scaled_spec = pl.BlockSpec((width, members * out), lambda i: (0, 0))
    return pl.pallas_call(
        column_prep_kernel,
        grid=(out // block,),
        in_specs=[
            pl.BlockSpec((members, width, block), lambda i: (0, 0, i)),
            pl.BlockSpec((members * rank, width), lambda i: (0, 0)),
            pl.BlockSpec((1, members * rank, wide), lambda i: (i, 0, 0)),
            pl.BlockSpec((members, 1, block), lambda i: (0, 0, i)),
        ],
        out_specs=[
            scaled_spec,
            pl.BlockSpec((members, 2, block), lambda i: (0, 0, i)),
            pl.BlockSpec((members, rank, block), lambda i: (0, 0, i)),
        ],
        out_shape=[
            jax.ShapeDtypeStruct((width, members * out), bf16),
            jax.ShapeDtypeStruct((members, 2, out), f32),
            jax.ShapeDtypeStruct((members, rank, out), f32),
        ],
        cost_estimate=cost(
            flops=4 * members * width * out * 256, bytes_accessed=4 * members * width * out, transcendentals=0
        ),
        name="column_prep",
    )(weight, flat, blocks, magnitude[:, None, :])


def row_prep_kernel(w_ref, a_ref, b_ref, out_ref, cross_ref, square_ref):
    heading = w_ref[...].astype(f32) + adapter_scale * mm(a_ref[...], b_ref[...], TN)
    narrow = heading.astype(bf16)
    out_ref[...] = narrow
    cross_ref[...] = mm(a_ref[...], narrow)
    square_ref[...] = jnp.sum(heading * heading, axis=0, keepdims=True)


def row_prep(weight, down, up, block):
    rows, out = weight.shape
    rank = down.shape[1]
    along = lambda n: pl.BlockSpec((n, block), lambda i: (0, i))
    return pl.pallas_call(
        row_prep_kernel,
        grid=(out // block,),
        in_specs=[along(rows), pl.BlockSpec((rank, rows), lambda i: (0, 0)), along(rank)],
        out_specs=[along(rows), along(rank), along(1)],
        out_shape=[
            jax.ShapeDtypeStruct((rows, out), bf16),
            jax.ShapeDtypeStruct((rank, out), f32),
            jax.ShapeDtypeStruct((1, out), f32),
        ],
        cost_estimate=cost(flops=2 * rows * out * 256, bytes_accessed=4 * rows * out, transcendentals=0),
        name="row_prep",
    )(weight, down.T, up)


def turn_forward(values, cosine, signed_sine):
    return values * cosine + pltpu.roll(values, values.shape[1] // 2, 1) * signed_sine


def turn_backward(values, cosine, signed_sine):
    return values * cosine + pltpu.roll(values * signed_sine, values.shape[1] // 2, 1)


def over_blocks(total, block, body):
    if total // block <= 4:
        for i in range(total // block):
            body(i * block, (i + 1) * block)
    else:

        def step(i, carry):
            body(pl.multiple_of(i * block, block), total)
            return carry

        lax.fori_loop(0, total // block, step, 0)


def weights_t(keys, queries, kpos, qpos, qstart, scale):
    scores = mm(keys, queries, NT)
    allowed = jnp.logical_and(kpos <= qpos, kpos >= qstart)
    return jnp.where(allowed, jnp.exp2(scores * (scale * LOG2_E)), 0.0)


def attend_kernel(x_ref, cos_ref, sin_ref, kpos_ref, qinfo_ref, o_ref, l_ref, qs, ks, vt, os, *, scale, block):
    blocks, _, _, group, size = x_ref.shape
    total = blocks * group
    cosine, signed_sine = cos_ref[...], sin_ref[...]
    qs[...] = turn_forward(x_ref[:, 0, 0].reshape(total, size).astype(f32), cosine, signed_sine).astype(bf16)
    ks[...] = turn_forward(x_ref[:, 0, 1].reshape(total, size).astype(f32), cosine, signed_sine).astype(bf16)
    vt[...] = x_ref[:, 0, 2].reshape(total, size).astype(f32).T.astype(bf16)

    def body(first, last):
        at = pl.ds(first, block)
        weights = weights_t(
            ks[:last], qs[at, :], kpos_ref[:last], qinfo_ref[0, 0:1, at], qinfo_ref[0, 1:2, at], scale
        )
        totals = jnp.sum(weights, axis=0, keepdims=True)
        outer = mm(vt[:, :last], weights.astype(bf16))
        l_ref[0, 0:1, at] = totals
        os[at, :] = (outer / totals).T.astype(bf16)

    over_blocks(total, block, body)
    o_ref[:, 0] = os[...].reshape(blocks, group, size)


def attend(pairs, tables, kpos, qinfo):
    blocks, slots, _, group, size = pairs.shape
    total = blocks * group
    block = math.gcd(total, score_block)
    return pl.pallas_call(
        partial(attend_kernel, scale=1.0 / math.sqrt(size), block=block),
        grid=(slots,),
        in_specs=[
            pl.BlockSpec((blocks, 1, 3, group, size), lambda n: (0, n, 0, 0, 0)),
            pl.BlockSpec((total, size), lambda n: (0, 0)),
            pl.BlockSpec((total, size), lambda n: (0, 0)),
            pl.BlockSpec((total, 1), lambda n: (0, 0)),
            pl.BlockSpec((1, 2, total), lambda n: (n, 0, 0)),
        ],
        out_specs=[
            pl.BlockSpec((blocks, 1, group, size), lambda n: (0, n, 0, 0)),
            pl.BlockSpec((1, 1, total), lambda n: (n, 0, 0)),
        ],
        out_shape=[
            jax.ShapeDtypeStruct((blocks, slots, group, size), bf16),
            jax.ShapeDtypeStruct((slots, 1, total), f32),
        ],
        scratch_shapes=[
            pltpu.VMEM((total, size), bf16),
            pltpu.VMEM((total, size), bf16),
            pltpu.VMEM((size, total), bf16),
            pltpu.VMEM((total, size), bf16),
        ],
        cost_estimate=cost(
            flops=slots * 4 * total * total * size,
            bytes_accessed=slots * total * size * 8,
            transcendentals=slots * total * total // 2,
        ),
        name="attend",
    )(pairs, *tables, kpos, qinfo)


def attend_back_kernel(
    x_ref, o_ref, d_ref, l_ref, cos_ref, sin_ref, kpos_ref, qinfo_ref, g_ref, s_ref,
    qs, ks, kt, vs, dk, dv, dq, *, scale, block
):
    blocks, _, _, group, size = x_ref.shape
    total = blocks * group
    cosine, signed_sine = cos_ref[...], sin_ref[...]
    plain = [x_ref[:, 0, j].reshape(total, size).astype(f32) for j in range(3)]
    qs[...] = turn_forward(plain[0], cosine, signed_sine).astype(bf16)
    turned = turn_forward(plain[1], cosine, signed_sine)
    ks[...] = turned.astype(bf16)
    kt[...] = turned.T.astype(bf16)
    vs[...] = plain[2].astype(bf16)
    dk[...] = jnp.zeros_like(dk)
    dv[...] = jnp.zeros_like(dv)

    def body(first, last):
        at = pl.ds(first, block)
        span = block // group
        rows = pl.ds(first // group, span)
        weights = weights_t(
            ks[:last], qs[at, :], kpos_ref[:last], qinfo_ref[0, 0:1, at], qinfo_ref[0, 1:2, at], scale
        )
        totals = l_ref[0, 0:1, at]
        grad_t = d_ref[rows, 0].reshape(block, size).astype(f32).T
        out_t = o_ref[rows, 0].reshape(block, size).astype(f32).T
        dlog = -jnp.sum(grad_t * out_t, axis=0, keepdims=True) / totals
        outer_t = (grad_t / totals).astype(bf16)
        dweights = mm(vs[:last], outer_t)
        dscores = (weights * (dweights + dlog)).astype(bf16)
        dk[:last] += mm(dscores, qs[at, :])
        dv[:last] += mm(weights.astype(bf16), outer_t, NT)
        dq[at, :] = mm(kt[:, :last], dscores).T

    over_blocks(total, block, body)
    grads = (
        turn_backward(dq[...] * scale, cosine, signed_sine),
        turn_backward(dk[...] * scale, cosine, signed_sine),
        dv[...],
    )
    sums = []
    for j in range(3):
        g_ref[:, 0, j] = grads[j].astype(bf16).reshape(blocks, group, size)
        sums.append(jnp.sum(grads[j] * plain[j], axis=0, keepdims=True))
    s_ref[0] = jnp.concatenate(sums, axis=0)


def attend_back(pairs, outputs, grads, totals, tables, kpos, qinfo):
    blocks, slots, _, group, size = pairs.shape
    total = blocks * group
    block = math.gcd(total, score_block)
    half = pl.BlockSpec((blocks, 1, group, size), lambda n: (0, n, 0, 0))
    whole = pl.BlockSpec((blocks, 1, 3, group, size), lambda n: (0, n, 0, 0, 0))
    return pl.pallas_call(
        partial(attend_back_kernel, scale=1.0 / math.sqrt(size), block=block),
        grid=(slots,),
        in_specs=[
            whole,
            half,
            half,
            pl.BlockSpec((1, 1, total), lambda n: (n, 0, 0)),
            pl.BlockSpec((total, size), lambda n: (0, 0)),
            pl.BlockSpec((total, size), lambda n: (0, 0)),
            pl.BlockSpec((total, 1), lambda n: (0, 0)),
            pl.BlockSpec((1, 2, total), lambda n: (n, 0, 0)),
        ],
        out_specs=[whole, pl.BlockSpec((1, 3, size), lambda n: (n, 0, 0))],
        out_shape=[
            jax.ShapeDtypeStruct(pairs.shape, bf16),
            jax.ShapeDtypeStruct((slots, 3, size), f32),
        ],
        scratch_shapes=[
            pltpu.VMEM((total, size), bf16),
            pltpu.VMEM((total, size), bf16),
            pltpu.VMEM((size, total), bf16),
            pltpu.VMEM((total, size), bf16),
            pltpu.VMEM((total, size), f32),
            pltpu.VMEM((total, size), f32),
            pltpu.VMEM((total, size), f32),
        ],
        cost_estimate=cost(
            flops=slots * 10 * total * total * size,
            bytes_accessed=slots * total * size * 16,
            transcendentals=slots * total * total // 2,
        ),
        name="attend_back",
    )(pairs, outputs, grads, totals, *tables, kpos, qinfo)


def to_pairs_kernel(*refs, dims):
    x_refs, w_ref, out_ref, xs = refs[:4], refs[4], refs[5], refs[6]
    count = x_refs[0].shape[0]

    @pl.when(jnp.logical_and(pl.program_id(0) == 0, pl.program_id(1) == 0))
    def _():
        for i in range(4):
            xs[i * count:(i + 1) * count] = x_refs[i][...]

    rows, heads, _, pieces, quarter, size = out_ref.shape
    product = mm(xs[...], w_ref[...], dims).astype(bf16)
    for i in range(pieces):
        for r in range(rows):
            at = (i * rows + r) * quarter
            for h in range(heads):
                out_ref[r, h, 0, i] = product[at:at + quarter, h * size:(h + 1) * size]


def project_to_pairs(pieces, weight, dims, parts, heads, size, span):
    rows, quarter, width = pieces[0].shape
    count = rows * quarter
    wide = span * size
    steps = heads // span
    if dims == NN:
        w_spec = pl.BlockSpec((width, wide), lambda j, h: (0, j * steps + h))
    else:
        w_spec = pl.BlockSpec((wide, width), lambda j, h: (j * steps + h, 0))
    return pl.pallas_call(
        partial(to_pairs_kernel, dims=dims),
        grid=(parts, steps),
        in_specs=[pl.BlockSpec(memory_space=pltpu.VMEM)] * 4 + [w_spec],
        out_specs=[
            pl.BlockSpec((rows, span, 1, 4, quarter, size), lambda j, h: (0, h, j, 0, 0, 0)),
            pl.BlockSpec((4 * count, width), lambda j, h: (0, 0)),
        ],
        out_shape=[
            jax.ShapeDtypeStruct((rows, heads, parts, 4, quarter, size), bf16),
            jax.ShapeDtypeStruct((4 * count, width), bf16),
        ],
        cost_estimate=cost(
            flops=8 * count * width * parts * heads * size,
            bytes_accessed=2 * width * (8 * count + parts * heads * size),
            transcendentals=0,
        ),
        name="project_to_pairs",
    )(*[p.reshape(count, width) for p in pieces], weight)


def split_out(product, out_refs, at):
    kept_ref, near_ref, send_ref = out_refs
    half = product.shape[0] // 4
    kept_ref[at:at + half] = product[:half]
    near_ref[at:at + half] = product[half:2 * half]
    for i in range(2):
        send_ref[i, at:at + half] = product[(i + 2) * half:(i + 3) * half]


def split_specs(count, out, block):
    one, two = pl.BlockSpec((count, block), lambda n: (0, n)), pl.BlockSpec((2, count, block), lambda n: (0, 0, n))
    shapes = [(count, out), (count, out), (2, count, out)]
    return [one, one, two], [jax.ShapeDtypeStruct(v, bf16) for v in shapes]


def by_rows(kept, near, send, quarter):
    shape = (kept.shape[0] // quarter, quarter, kept.shape[1])
    return kept.reshape(shape), near.reshape(shape), send.reshape((2,) + shape)


def join_pairs(x_ref, flat_ref):
    rows, heads, parts, pieces, quarter, size = x_ref.shape
    for i in range(pieces):
        for r in range(rows):
            at = (i * rows + r) * quarter
            for j in range(parts):
                for h in range(heads):
                    col = (j * heads + h) * size
                    flat_ref[at:at + quarter, col:col + size] = x_ref[r, h, j, i]


def from_pairs_kernel(x_ref, w_ref, flat_ref, *out_refs):
    @pl.when(pl.program_id(0) == 0)
    def _():
        join_pairs(x_ref, flat_ref)

    split_out(mm(flat_ref[...], w_ref[...]).astype(bf16), out_refs, 0)


def project_from_pairs(pairs, weight, block):
    rows, heads, parts, pieces, quarter, size = pairs.shape
    count, width = rows * quarter, parts * heads * size
    out = weight.shape[1]
    specs, shapes = split_specs(count, out, block)
    flat, *split = pl.pallas_call(
        from_pairs_kernel,
        grid=(out // block,),
        in_specs=[pl.BlockSpec(pairs.shape, lambda n: (0,) * 6), pl.BlockSpec((width, block), lambda n: (0, n))],
        out_specs=[pl.BlockSpec((4 * count, width), lambda n: (0, 0))] + specs,
        out_shape=[jax.ShapeDtypeStruct((4 * count, width), bf16)] + shapes,
        cost_estimate=cost(
            flops=8 * count * width * out, bytes_accessed=2 * (out * width + 4 * count * (2 * width + out)),
            transcendentals=0,
        ),
        name="project_from_pairs",
    )(pairs, weight)
    return flat, by_rows(*split, quarter)


def project_split_kernel(*refs, dims):
    x_refs, w_ref, out_refs = refs[:-4], refs[-4], refs[-3:]
    at = 0
    for x_ref in x_refs:
        split_out(mm(x_ref[...], w_ref[...], dims).astype(bf16), out_refs, at)
        at += x_ref.shape[0] // 4


def project_split(flats, weight, dims, block, quarter):
    width = flats[0].shape[1]
    count = sum(v.shape[0] for v in flats) // 4
    if dims == NN:
        out = weight.shape[1]
        w_spec = pl.BlockSpec((width, block), lambda n: (0, n))
    else:
        out = weight.shape[0]
        w_spec = pl.BlockSpec((block, width), lambda n: (n, 0))
    specs, shapes = split_specs(count, out, block)
    split = pl.pallas_call(
        partial(project_split_kernel, dims=dims),
        grid=(out // block,),
        in_specs=[pl.BlockSpec(v.shape, lambda n: (0, 0)) for v in flats] + [w_spec],
        out_specs=specs,
        out_shape=shapes,
        cost_estimate=cost(
            flops=8 * count * width * out, bytes_accessed=2 * (out * width + 4 * count * (width + out)), transcendentals=0
        ),
        name="project_split",
    )(*flats, weight)
    return by_rows(*split, quarter)


def cotangent_kernel(*refs):
    x_refs, w_ref, out_ref, flat_ref = refs[:4], refs[4], refs[5], refs[6]
    part = x_refs[0].shape[0]
    for i in range(4):
        flat_ref[i * part:(i + 1) * part] = x_refs[i][...]
    out_ref[...] = mm(flat_ref[...], w_ref[...], NT).astype(bf16)


def project_cotangent(pieces, weight, rows, first):
    total, quarter, width = pieces[0].shape
    part = rows * quarter
    at = first // rows
    out = weight.shape[0]
    return pl.pallas_call(
        cotangent_kernel,
        grid=(1,),
        in_specs=[pl.BlockSpec((part, width), lambda c: (at, 0))] * 4 + [pl.BlockSpec((out, width), lambda c: (0, 0))],
        out_specs=[pl.BlockSpec((4 * part, out), lambda c: (0, 0)), pl.BlockSpec((4 * part, width), lambda c: (0, 0))],
        out_shape=[jax.ShapeDtypeStruct((4 * part, out), bf16), jax.ShapeDtypeStruct((4 * part, width), bf16)],
        cost_estimate=cost(
            flops=8 * part * width * out, bytes_accessed=2 * width * (out + 8 * part), transcendentals=0
        ),
        name="project_cotangent",
    )(*[p.reshape(total * quarter, width) for p in pieces], weight)


def assemble(pairs):
    rows, heads, parts, pieces, quarter, size = pairs.shape
    tokens, width = 4 * rows * quarter, parts * heads * size
    return pl.pallas_call(
        join_pairs,
        out_shape=jax.ShapeDtypeStruct((tokens, width), bf16),
        cost_estimate=cost(flops=0, bytes_accessed=4 * tokens * width, transcendentals=0),
        name="assemble",
    )(pairs)


def runs(lengths, cut):
    at = 0
    for k, n in enumerate(lengths):
        start = 0
        while start < n:
            step = min(n - start, cut - at % cut)
            yield k, start, at, step
            start += step
            at += step


def width_of(sizes, pieces):
    return -(-sum(sizes) // (pieces * LANES)) * LANES


def part_of(ref, j, rank, lanes):
    return ref.at[j, :, lanes] if len(ref.shape) == 3 else ref.at[j * rank:(j + 1) * rank, lanes]


def cells(shapes):
    return [(v, j, c) for v, (members, size) in enumerate(shapes) for j in range(members) for c in range(size // LANES)]


def pack_kernel(*refs, plan, count):
    in_refs, sum_refs, out_ref, sums = refs[:count], refs[count:-2], refs[-2], refs[-1]
    rank = out_ref.shape[1]
    sums[...] = jnp.zeros_like(sums)
    for k, (v, j, c) in enumerate(cells([(ref.shape[0], ref.shape[2]) for ref in sum_refs])):
        at = k // rank * LANES
        sums[k % rank:k % rank + 1, at:at + LANES] = sum_refs[v][j, :, c * LANES:(c + 1) * LANES]
    base = 0
    for entries, cut in plan:
        sizes = [n for _, _, n in entries]
        for k, start, at, n in runs(sizes, cut):
            which, j, _ = entries[k]
            lanes = slice(start, start + n)
            values = sums[:, lanes] if which is None else part_of(in_refs[which], j, rank, lanes)[...]
            out_ref[at // cut, :, base + at % cut:base + at % cut + n] = values.astype(bf16)
        end = sum(sizes)
        while end < out_ref.shape[0] * cut:
            n = cut - end % cut
            out_ref[end // cut, :, base + end % cut:base + end % cut + n] = jnp.zeros((rank, n), bf16)
            end += n
        base += cut


def unpack_kernel(*refs, plan, count):
    x_ref, m_refs, out_refs = refs[0], refs[1:1 + count], refs[1 + count:]
    rank = x_ref.shape[1]
    base = 0
    for entries, cut in plan:
        for k, start, at, n in runs([n for _, _, n in entries], cut):
            values = x_ref[at // cut, :, base + at % cut:base + at % cut + n].astype(f32)
            which, j, _ = entries[k]
            if which is not None:
                part_of(out_refs[which], j, rank, slice(start, start + n))[...] = values
                continue
            for cell, (v, j, c) in enumerate(cells([ref.shape for ref in m_refs])):
                lane = cell // rank * LANES - start
                if 0 <= lane < n:
                    place = (slice(j, j + 1), slice(c * LANES, (c + 1) * LANES))
                    row = slice(cell % rank, cell % rank + 1)
                    out_refs[v - count][place] = values[row, lane:lane + LANES] / m_refs[v][place]
        base += cut


def packing(over_all, over_seq, vectors, pieces, rank):
    plan, at = [], 0
    for arrays in (over_all, over_seq):
        entries = []
        for v in arrays:
            members = v.shape[0] if len(v.shape) == 3 else v.shape[0] // rank
            entries += [(at, j, v.shape[-1]) for j in range(members)]
            at += 1
        plan.append(entries)
    blocks = len(cells([(v.shape[0], v.shape[2]) for v in vectors]))
    plan[1].append((None, 0, -(-blocks // rank) * LANES))
    return [(entries, width_of([n for _, _, n in entries], pieces)) for entries in plan]


def pack(plan, arrays, vectors, pieces, rank):
    return pl.pallas_call(
        partial(pack_kernel, plan=plan, count=len(arrays)),
        out_shape=jax.ShapeDtypeStruct((pieces, rank, sum(cut for _, cut in plan)), bf16),
        scratch_shapes=[pltpu.VMEM((rank, plan[1][0][-1][2]), f32)],
        cost_estimate=cost(flops=0, bytes_accessed=4 * sum(v.size for v in arrays), transcendentals=0),
        name="pack",
    )(*arrays, *vectors)


def unpack(plan, values, arrays, magnitudes):
    return pl.pallas_call(
        partial(unpack_kernel, plan=plan, count=len(magnitudes)),
        out_shape=[jax.ShapeDtypeStruct(v.shape, f32) for v in (*arrays, *magnitudes)],
        cost_estimate=cost(flops=0, bytes_accessed=6 * values.size, transcendentals=0),
        name="unpack",
    )(values, *magnitudes)


def gated_kernel(*refs):
    x_refs, w_ref, e_ref, hidden_ref, grads_ref, sums_ref, xs = refs[:4], *refs[4:]
    count = x_refs[0].shape[0]

    @pl.when(pl.program_id(0) == 0)
    def _():
        for i in range(4):
            xs[i * count:(i + 1) * count] = x_refs[i][...]

    product = mm(xs[...], w_ref[...])
    block = LANES
    for k in range(product.shape[1] // (2 * block)):
        at, mine = k * 2 * block, slice(k * block, (k + 1) * block)
        gate, up = product[:, at:at + block], product[:, at + block:at + 2 * block]
        dhid = e_ref[:, mine].astype(f32)
        sig = 1.0 / (1.0 + jnp.exp(-gate))
        act = gate * sig
        hidden_ref[:, mine] = (act * up).astype(bf16)
        dgate = dhid * up * (sig * (1.0 + gate * (1.0 - sig)))
        dup = dhid * act
        grads_ref[:, at:at + block] = dgate.astype(bf16)
        grads_ref[:, at + block:at + 2 * block] = dup.astype(bf16)
        sums_ref[0, :, mine] = jnp.sum(gate * dgate, axis=0, keepdims=True)
        sums_ref[1, :, mine] = jnp.sum(up * dup, axis=0, keepdims=True)


def gated(pieces, weight, dhid):
    rows, quarter, width = pieces[0].shape
    count = rows * quarter
    out = dhid.shape[1]
    block = GATED_BLOCKS * LANES
    return pl.pallas_call(
        gated_kernel,
        grid=(-(-out // block),),
        in_specs=[pl.BlockSpec(memory_space=pltpu.VMEM)] * 4
        + [
            pl.BlockSpec((width, 2 * block), lambda i: (0, i)),
            pl.BlockSpec((4 * count, block), lambda i: (0, i)),
        ],
        out_specs=[
            pl.BlockSpec((4 * count, block), lambda i: (0, i)),
            pl.BlockSpec((4 * count, 2 * block), lambda i: (0, i)),
            pl.BlockSpec((2, 1, block), lambda i: (0, 0, i)),
            pl.BlockSpec((4 * count, width), lambda i: (0, 0)),
        ],
        out_shape=[
            jax.ShapeDtypeStruct((4 * count, out), bf16),
            jax.ShapeDtypeStruct((4 * count, 2 * out), bf16),
            jax.ShapeDtypeStruct((2, 1, out), f32),
            jax.ShapeDtypeStruct((4 * count, width), bf16),
        ],
        cost_estimate=cost(
            flops=16 * count * width * out,
            bytes_accessed=4 * width * out + 8 * count * (2 * width + 4 * out),
            transcendentals=4 * count * out,
        ),
        name="gated",
    )(*[p.reshape(count, width) for p in pieces], weight, dhid)


def chunk_lanes(refs):
    ends = [0]
    for ref in refs:
        ends.append(ends[-1] + ref.shape[0])
    return [slice(a, b) for a, b in zip(ends, ends[1:])]


def column_grads_kernel(*refs, chunks, steps, joins):
    x_refs, d_refs, refs = refs[:chunks], list(refs[chunks:2 * chunks]), list(refs[2 * chunks:])
    if joins:
        pairs_ref, d_refs[-1] = d_refs[-1], refs.pop(9)

        @pl.when(pl.program_id(0) == 0)
        def _():
            join_pairs(pairs_ref, d_refs[-1])

    w_ref, a_ref, b_ref, stat_ref, m_ref, sum_ref, cross_ref, gb_ref, ga_ref, ts, dts, es = refs
    members, rank, block = b_ref.shape
    lanes = chunk_lanes(x_refs)
    i = pl.program_id(0)

    @pl.when(i == 0)
    def _():
        for c in range(chunks):
            ts[:, lanes[c]] = mm(a_ref[...], x_refs[c][...], NT).astype(bf16)
        dts[...] = jnp.zeros_like(dts)

    @pl.when(i < steps)
    def _():
        found = sum(mm(ts[:, lanes[c]], d_refs[c][...]) for c in range(chunks))
        spread, along = [], []
        for j in range(members):
            b = b_ref[j].astype(f32)
            scale = stat_ref[j, 1:2]
            coef = -sum_ref[j] / (m_ref[j] * stat_ref[j, 0:1])
            mine = found[j * rank:(j + 1) * rank, j * block:(j + 1) * block]
            gb_ref[j] = (adapter_scale * (mine * scale + coef * cross_ref[j])).astype(bf16)
            empty = jnp.zeros((rank, block), f32)
            row = lambda v: jnp.concatenate([v if k == j else empty for k in range(members)], axis=1)
            spread.append(row(adapter_scale * coef * b))
            along.append(row(adapter_scale * scale * b))
        wide = members * block
        es[:, pl.ds(pl.multiple_of(i * wide, wide), wide)] = jnp.concatenate(spread, axis=0).astype(bf16)
        up = jnp.concatenate(along, axis=0).astype(bf16)
        for c in range(chunks):
            dts[:, lanes[c]] += mm(up, d_refs[c][...], NT)

    @pl.when(i >= steps)
    def _():
        span = w_ref.shape[0]
        at = pl.ds(pl.multiple_of((i - steps) * span, span), span)
        total = mm(es[...], w_ref[...], NT)
        for c in range(chunks):
            total = total + mm(dts[:, lanes[c]].astype(bf16), x_refs[c][:, at])
        ga_ref[...] = total.astype(bf16)


def column_grads(rows, grads, weight, down, up, stat, magnitude, sums, cross, block):
    tokens, width = sum(v.shape[0] for v in rows), rows[0].shape[1]
    members, rank, out = up.shape
    chunks, steps, span = len(rows), out // block, 512
    first = lambda i: jnp.minimum(i, steps - 1)
    then = lambda i: jnp.maximum(i - steps, 0)
    part = lambda n: pl.BlockSpec((members, n, block), lambda i: (0, 0, first(i)))
    joins = len(grads[-1].shape) == 6
    joined = (rows[-1].shape[0], members * out)
    wide = members * block
    ranks = members * rank
    assert steps == 1 or not joins
    grad_b, grad_a, *flat = pl.pallas_call(
        partial(column_grads_kernel, chunks=chunks, steps=steps, joins=joins),
        grid=(steps + width // span,),
        in_specs=[pl.BlockSpec(v.shape, lambda i: (0, 0)) for v in rows]
        + [
            pl.BlockSpec(v.shape, lambda i: (0,) * 6) if len(v.shape) == 6
            else pl.BlockSpec((v.shape[0], wide), lambda i: (0, first(i)))
            for v in grads
        ]
        + [
            pl.BlockSpec((span, members * out), lambda i: (then(i), 0)),
            pl.BlockSpec((ranks, width), lambda i: (0, 0)),
            part(rank), part(2), part(1), part(1), part(rank),
        ],
        out_specs=[part(rank), pl.BlockSpec((ranks, span), lambda i: (0, then(i)))]
        + [pl.BlockSpec(joined, lambda i: (0, 0))] * joins,
        out_shape=[
            jax.ShapeDtypeStruct((members, rank, out), bf16),
            jax.ShapeDtypeStruct((ranks, width), bf16),
        ]
        + [jax.ShapeDtypeStruct(joined, bf16)] * joins,
        scratch_shapes=[
            pltpu.VMEM((ranks, tokens), bf16),
            pltpu.VMEM((ranks, tokens), f32),
            pltpu.VMEM((ranks, members * out), bf16),
        ],
        cost_estimate=cost(
            flops=4 * 256 * width * members * out // 4,
            bytes_accessed=2 * (width * members * out + tokens * (width + members * out)),
            transcendentals=0,
        ),
        name="column_grads",
    )(*rows, *grads, weight, down.transpose(0, 2, 1).reshape(ranks, width), up, stat, magnitude[:, None, :], sums, cross)
    return (grad_a, grad_b, *flat)


def row_grads_kernel(*refs, chunks):
    h_refs, d_refs, refs = refs[:chunks], refs[chunks:2 * chunks], refs[2 * chunks:]
    w_ref, a_ref, b_ref, stat_ref, coef_ref, ga_ref, gb_ref, ts, dts, acc = refs
    lanes = chunk_lanes(h_refs)
    i = pl.program_id(0)

    @pl.when(i == 0)
    def _():
        for c in range(chunks):
            ts[:, lanes[c]] = mm(a_ref[...], h_refs[c][...], NT).astype(bf16)
        dts[...] = jnp.zeros_like(dts)
        acc[...] = jnp.zeros_like(acc)

    b = b_ref[...].astype(f32)
    coef = coef_ref[...]
    found = sum(mm(ts[:, lanes[c]], d_refs[c][...]) for c in range(chunks))
    gb_ref[...] = (adapter_scale * (found + coef * stat_ref[...])).astype(bf16)
    up = (adapter_scale * b).astype(bf16)
    for c in range(chunks):
        dts[:, lanes[c]] += mm(up, d_refs[c][...], NT)
    acc[...] += mm((adapter_scale * coef * b).astype(bf16), w_ref[...], NT)

    @pl.when(i == pl.num_programs(0) - 1)
    def _():
        total = acc[...]
        for c in range(chunks):
            total = total + mm(dts[:, lanes[c]].astype(bf16), h_refs[c][...])
        ga_ref[...] = total.astype(bf16)


def row_grads(rows, grads, weight, down, up, stat, coef, block):
    tokens, count = sum(v.shape[0] for v in rows), rows[0].shape[1]
    rank, out = up.shape
    chunks = len(rows)
    along = lambda n: pl.BlockSpec((n, block), lambda i: (0, i))
    return pl.pallas_call(
        partial(row_grads_kernel, chunks=chunks),
        grid=(out // block,),
        in_specs=[pl.BlockSpec(v.shape, lambda i: (0, 0)) for v in rows]
        + [pl.BlockSpec((v.shape[0], block), lambda i: (0, i)) for v in grads]
        + [along(count), pl.BlockSpec((rank, count), lambda i: (0, 0)), along(rank), along(rank), along(1)],
        out_specs=[pl.BlockSpec((rank, count), lambda i: (0, 0)), along(rank)],
        out_shape=[jax.ShapeDtypeStruct((rank, count), bf16), jax.ShapeDtypeStruct((rank, out), bf16)],
        scratch_shapes=[
            pltpu.VMEM((rank, tokens), bf16),
            pltpu.VMEM((rank, tokens), f32),
            pltpu.VMEM((rank, count), f32),
        ],
        cost_estimate=cost(
            flops=256 * count * out, bytes_accessed=2 * (count * out + tokens * (count + out)), transcendentals=0
        ),
        name="row_grads",
    )(*rows, *grads, weight, down.T, up, stat, coef)


def norm_scale(values):
    return lax.rsqrt(jnp.mean(values * values, axis=-1, keepdims=True) + epsilon)


def norm_back(values, gain, grad):
    r = norm_scale(values)
    weighted = gain * grad
    return r * weighted - values * (r * r * r) * jnp.mean(values * weighted, axis=-1, keepdims=True)


def rotary_tables(positions, head_size):
    half_size = head_size // 2
    frequency = rope_base ** (-(2.0 * jnp.arange(half_size, dtype=f32)) / head_size)
    angles = positions.astype(f32)[:, None] * frequency[None, :]
    cosine, sine = jnp.cos(angles), jnp.sin(angles)
    return (jnp.concatenate([cosine, cosine], axis=-1), jnp.concatenate([-sine, sine], axis=-1))


def local(
    layer_in, cotangent, doc_lengths, pad_counts, gain_attn, gain_ffn, w_qkv, a_qkv, b_qkv, m_qkv, w_out, a_out,
    b_out, m_out, w_gateup, a_gateup, b_gateup, m_gateup, w_down, a_down, b_down, m_down,
):
    rows, quarter, width = layer_in.shape
    tensor, seq = lax.axis_size("tensor"), lax.axis_size("seq")
    assert tensor == len(PIECES)
    me_t, me_s = lax.axis_index("tensor"), lax.axis_index("seq")
    group = quarter * tensor
    total = group * seq
    feat = w_qkv.shape[2]
    heads = feat // HEAD_DIM
    rank = a_qkv.shape[2]
    ff = w_down.shape[0]
    piece_of = jnp.bitwise_xor(me_t, jnp.array(PIECES, jnp.int32))
    in_block = (piece_of[:, None] * quarter + jnp.arange(quarter, dtype=jnp.int32)[None, :]).reshape(group)
    positions = (jnp.arange(seq, dtype=jnp.int32)[:, None] * group + in_block[None, :]).reshape(total)
    tables = rotary_tables(positions, HEAD_DIM)
    offsets = jnp.cumsum(doc_lengths, axis=1)
    starts = jnp.max(
        jnp.where(offsets[:, :, None] <= positions[None, None, :], offsets[:, :, None], 0), axis=1
    )
    kpos = positions[:, None]
    few = rows // 3
    cuts = [slice(rows - few, rows), slice(0, rows - few)]
    span = range(2)
    pair_counts = [(at.stop - at.start) * heads for at in cuts]
    slots = [-(-count // seq) for count in pair_counts]
    mine = [me_s * slots[c] + jnp.arange(slots[c]) for c in span]
    live = [mine[c] < pair_counts[c] for c in span]

    def pair_info(c):
        row = jnp.minimum(mine[c] // heads + cuts[c].start, cuts[c].stop - 1)
        chosen = (row[:, None] == jnp.arange(rows)[None, :])[:, :, None]
        return jnp.stack(
            [jnp.broadcast_to(positions[None], (slots[c], total)), jnp.sum(jnp.where(chosen, starts[None], 0), axis=1)],
            axis=1,
        )

    qinfo = [pair_info(c) for c in span]

    def send_pairs(values, c):
        parts = values.shape[2]
        laid = values.reshape(pair_counts[c], parts, group, HEAD_DIM)
        if slots[c] * seq > pair_counts[c]:
            laid = jnp.pad(laid, ((0, slots[c] * seq - pair_counts[c]), (0, 0), (0, 0), (0, 0)))
        return exchange(laid.reshape(seq, slots[c], parts, group, HEAD_DIM))

    def fetch_pairs(values, c):
        parts = values.shape[2]
        laid = exchange(values).reshape(seq * slots[c], parts, group, HEAD_DIM)[:pair_counts[c]]
        return laid.reshape(pair_counts[c] // heads, heads, parts, tensor, quarter, HEAD_DIM)

    def to_heads(pieces, weight):
        return project_to_pairs(pieces, weight, NN, 3, heads, HEAD_DIM, heads)

    def back_to_heads(pieces, weight):
        return project_to_pairs(pieces, weight, NT, 1, heads, HEAD_DIM, 2)

    owned = me_s * group + me_t * quarter + jnp.arange(quarter, dtype=jnp.int32)
    valid = (owned[None, :] < total - pad_counts[:, None]).astype(f32)
    cot = cotangent.astype(f32) * valid[:, :, None]
    wide_in = [layer_in[at].astype(f32) for at in cuts]

    def normed(values, gain):
        return (values * norm_scale(values) * gain).astype(bf16)

    started = [gather_start(normed(wide_in[c], gain_attn)) for c in span]
    qkv_w, qkv_stat, qkv_cross = column_prep(w_qkv, a_qkv, b_qkv, m_qkv, 256, False)
    started[0], qkv_w = after(started[0], qkv_w)
    normed_a, d_qkv, pairs, outputs, totals, att = [[None] * 2 for _ in range(6)]
    laid, normed_a[0] = to_heads(gather_end(*started[0]), qkv_w)

    laid, started[1], w_down = after(laid, started[1], w_down)
    pairs[0] = send_pairs(laid, 0)
    laid, normed_a[1] = to_heads(gather_end(*started[1]), qkv_w)
    down_w, down_cross, down_square = row_prep(w_down, a_down, b_down, 256)
    pairs[0], laid, down_square, w_out, w_gateup = after(pairs[0], laid, down_square, w_out, w_gateup)

    u_out, middle, hidden, d_gu, gu_sum, normed_f, d_mid, du_out, dhid, du_down = [[None] * 2 for _ in range(10)]

    def of_cotangent(whole, c):
        return project_cotangent(whole, down_w, cuts[c].stop - cuts[c].start, cuts[c].start)

    pairs[1] = send_pairs(laid, 1)
    outputs[0], totals[0] = attend(pairs[0], tables, kpos, qinfo[0])
    down_square = tensor_sum(down_square)
    down_scale = m_down / jnp.sqrt(down_square[0])
    scaled, w_gateup, w_out = after((cot * down_scale).astype(bf16), w_gateup, w_out)
    out_w, out_cross, out_square = row_prep(w_out, a_out, b_out, 512)
    gu_w, gu_stat, gu_cross = column_prep(w_gateup, a_gateup, b_gateup, m_gateup, LANES, True)
    started, gu_w, out_w = after(gather_start(scaled), gu_w, out_w)
    whole_cot = gather_end(*started)
    pairs[1], outputs[0], whole_cot, out_square = after(pairs[1], outputs[0], whole_cot, out_square)

    fetched = fetch_pairs(outputs[0][:, :, None], 0)
    outputs[1], totals[1] = attend(pairs[1], tables, kpos, qinfo[1])
    out_square = tensor_sum(out_square)
    out_scale = m_out / jnp.sqrt(out_square[0])
    fetched, outputs[1], whole_cot, out_scale = after(fetched, outputs[1], whole_cot, out_scale)

    returned = fetch_pairs(outputs[1][:, :, None], 1)
    att[0], split = project_from_pairs(fetched, out_w, 1024)
    moving, whole_cot = after(scatter_start(*split), whole_cot)
    for c in span:
        dhid[c], du_down[c] = of_cotangent(whole_cot, c)
    tail, dhid = after(scatter_end(*moving), dhid)
    u_out[0] = tail * out_scale
    middle[0] = wide_in[0] + u_out[0]
    started = gather_start(normed(middle[0], gain_ffn))

    att[1], split = project_from_pairs(returned, out_w, 1024)
    started, split = after(started, split)
    moving, whole = after(scatter_start(*split), gather_end(*started))
    hidden[0], d_gu[0], gu_sum[0], normed_f[0] = gated(whole, gu_w, dhid[0])
    tail, d_gu[0] = after(scatter_end(*moving), d_gu[0])
    u_out[1] = tail * out_scale
    middle[1] = wide_in[1] + u_out[1]
    h_f, d_gu[0] = after(normed(middle[1], gain_ffn), d_gu[0])
    started = gather_start(h_f)
    split = project_split([d_gu[0]], gu_w, NT, 1024, quarter)
    whole, behind = after(gather_end(*started), scatter_start(*split))

    hidden[1], d_gu[1], gu_sum[1], normed_f[1] = gated(whole, gu_w, dhid[1])
    tail, d_gu[1] = after(scatter_end(*behind), d_gu[1])
    d_mid[0] = cot[cuts[0]] + norm_back(middle[0], gain_ffn, tail)
    scaled, d_gu[1] = after((d_mid[0] * out_scale).astype(bf16), d_gu[1])
    started, split = after(gather_start(scaled), project_split([d_gu[1]], gu_w, NT, 512, quarter))
    moving, whole = after(scatter_start(*split), gather_end(*started))

    d_att, du_out[0] = back_to_heads(whole, out_w)
    d_outputs = send_pairs(d_att, 0)[:, :, 0]
    tail, d_att = after(scatter_end(*moving), d_att)
    d_mid[1] = cot[cuts[1]] + norm_back(middle[1], gain_ffn, tail)
    scaled, d_outputs = after((d_mid[1] * out_scale).astype(bf16), d_outputs)
    d_pairs, pair_sums = [None] * 2, [None] * 2
    d_pairs[0], pair_sums[0] = attend_back(pairs[0], outputs[0], d_outputs, totals[0], tables, kpos, qinfo[0])
    d_pairs[0], scaled, hidden = after(d_pairs[0], scaled, hidden)
    fetched = fetch_pairs(d_pairs[0], 0)
    started, split = after(gather_start(scaled), project_split(hidden[::-1], down_w, NN, 512, quarter))
    d_att, du_out[1] = back_to_heads(gather_end(*started), out_w)
    d_att, fetched = after(d_att, fetched)

    d_att, att, out_sum = after(d_att, att, sum(jnp.sum(u_out[c] * d_mid[c], axis=(0, 1)) for c in span)[None])
    d_outputs = send_pairs(d_att, 1)[:, :, 0]
    out_sum = tensor_sum(out_sum)
    grad_a_out, grad_b_out = row_grads(att, du_out, out_w, a_out, b_out, out_cross, -out_sum / out_square, 512)
    d_outputs, grad_a_out, d_gu = after(d_outputs, grad_a_out, d_gu)
    d_pairs[1], pair_sums[1] = attend_back(pairs[1], outputs[1], d_outputs, totals[1], tables, kpos, qinfo[1])

    d_pairs[1], split, d_gu = after(d_pairs[1], split, d_gu)
    returned = fetch_pairs(d_pairs[1], 1)
    moving, d_gu = after(scatter_start(*split), d_gu)
    gu_sums = sum(gu_sum)
    grad_a_gu, grad_b_gu = column_grads(
        normed_f, d_gu, gu_w, a_gateup, b_gateup, gu_stat, m_gateup, gu_sums, gu_cross, LANES
    )
    tail, grad_a_gu, fetched = after(scatter_end(*moving), grad_a_gu, fetched)
    u_down = tail * down_scale
    layer_out = (jnp.concatenate(middle[::-1]) + u_down).astype(bf16)
    down_sum = tensor_sum(jnp.sum(u_down * cot, axis=(0, 1))[None])
    d_qkv[0] = assemble(fetched)
    grad_a_down, grad_b_down = row_grads(
        hidden, du_down, down_w, a_down, b_down, down_cross, -down_sum / down_square, 512
    )
    fetched, d_qkv[0], grad_a_down, layer_out = after(returned, d_qkv[0], grad_a_down, layer_out)

    qkv_sums = 0.0
    for c in span:
        choice = jnp.logical_and((mine[c] % heads)[:, None] == jnp.arange(heads)[None, :], live[c][:, None])
        qkv_sums = qkv_sums + jnp.sum(jnp.where(choice[:, None, :, None], pair_sums[c][:, :, None, :], 0.0), axis=0)
    qkv_sums = qkv_sums.reshape(3, 1, feat)
    grad_a_qkv, grad_b_qkv, d_qkv[1] = column_grads(
        normed_a, [d_qkv[0], fetched], qkv_w, a_qkv, b_qkv, qkv_stat, m_qkv, qkv_sums, qkv_cross, feat
    )

    over_all = [grad_a_gu, grad_b_out, grad_b_down, grad_a_qkv]
    over_seq = [grad_b_gu, grad_a_out, grad_a_down, grad_b_qkv]
    vectors = [gu_sums, out_sum[None], down_sum[None], qkv_sums]
    plan = packing(over_all, over_seq, vectors, seq, rank)
    cut = plan[0][1]
    packed, d_qkv = after(pack(plan, over_all + over_seq, vectors, seq, rank), d_qkv)
    added, split = after(exchange(packed), project_split(d_qkv[::-1], qkv_w, NT, 512, quarter))
    moving = scatter_start(*split)
    added = jnp.sum(added.astype(f32), axis=0).astype(bf16)
    shared = added[:, :cut]
    shared = shared.astype(f32) + swap(shared, 1).astype(f32) + swap(shared, 2).astype(f32) + swap(shared, 3).astype(f32)
    joined, moving = after(jnp.concatenate([shared.astype(bf16), added[:, cut:]], axis=1), moving)
    back = seq_gather(joined)
    grad_in = jnp.concatenate(d_mid[::-1]) + norm_back(layer_in.astype(f32), gain_attn, scatter_end(*moving))
    g_a_gu, g_b_out, g_b_down, g_a_qkv, g_b_gu, g_a_out, g_a_down, g_b_qkv, s_gu, s_out, s_down, s_qkv = unpack(
        plan, back, over_all + over_seq, [m_gateup, m_out[None], m_down[None], m_qkv]
    )
    return (
        layer_out,
        grad_in,
        g_a_qkv.reshape(3, rank, width).transpose(0, 2, 1),
        g_b_qkv,
        s_qkv,
        g_a_out.T,
        g_b_out,
        s_out[0],
        g_a_gu.reshape(2, rank, width).transpose(0, 2, 1),
        g_b_gu,
        s_gu,
        g_a_down.T,
        g_b_down,
        s_down[0],
    )


def solution(mesh):
    split = P(None, ("seq", "tensor"), None)
    in_specs = (
        split, split, P(), P(), P(), P(),
        P(None, None, "tensor"), P(), P(None, None, "tensor"), P(None, "tensor"),
        P("tensor", None), P("tensor", None), P(), P(),
        P(None, None, "tensor"), P(), P(None, None, "tensor"), P(None, "tensor"),
        P("tensor", None), P("tensor", None), P(), P(),
    )
    out_specs = (
        split, split,
        P(), P(None, None, "tensor"), P(None, "tensor"),
        P("tensor", None), P(), P(),
        P(), P(None, None, "tensor"), P(None, "tensor"),
        P("tensor", None), P(), P(),
    )
    return jax.shard_map(local, mesh=mesh, in_specs=in_specs, out_specs=out_specs, check_vma=False)
```

```python
from functools import partial
import math

import jax
import jax.numpy as jnp
from jax import lax
from jax.experimental import pallas as pl
from jax.experimental.pallas import tpu as pltpu
from jax.sharding import PartitionSpec as P

HEAD_DIM = 128
LANES = 128
epsilon = 1e-05
adapter_scale = 2.0
rope_base = 10000.0
f32 = jnp.float32
bf16 = jnp.bfloat16
PIECES = (0, 2, 1, 3)
score_block = 256
GATED_BLOCKS = 3
LOG2_E = math.log2(math.e)
NT = (((1,), (1,)), ((), ()))
NN = (((1,), (0,)), ((), ()))
TN = (((0,), (0,)), ((), ()))


def cost(flops, bytes_accessed, transcendentals):
    return pl.CostEstimate(flops=flops // 64, bytes_accessed=bytes_accessed // 64, transcendentals=0)


def mm(a, b, dims=NN):
    return lax.dot_general(a, b, dims, preferred_element_type=f32)


def swap(values, bit):
    size = lax.axis_size("tensor")
    return lax.ppermute(values, "tensor", [(i, i ^ bit) for i in range(size)])


def gather_start(shard):
    return shard, swap(shard, 2), swap(shard, 1)


def gather_end(shard, far, near):
    return [shard, far, near, swap(far, 1)]


def scatter_start(kept, near, send):
    got = swap(send, 1)
    return kept, got, (near.astype(f32) + got[1].astype(f32)).astype(bf16)


def scatter_end(kept, got, passed):
    return kept.astype(f32) + got[0].astype(f32) + swap(passed, 2).astype(f32)


def after(value, *others):
    return lax.optimization_barrier((value, *others))


def tensor_sum(values):
    return values + swap(values, 1) + swap(values, 2) + swap(values, 3)


def exchange(values):
    return lax.all_to_all(values, "seq", 0, 0, tiled=True)


def seq_gather(values):
    size = lax.axis_size("seq")
    return exchange(jnp.broadcast_to(values[None], (size,) + values.shape))


def column_prep_kernel(w_ref, a_ref, b_ref, m_ref, out_ref, stat_ref, cross_ref):
    members, width, block = w_ref.shape
    rank = cross_ref.shape[1]
    product = mm(a_ref[...], b_ref[0], TN)
    i = pl.program_id(0)
    for j in range(members):
        heading = w_ref[j].astype(f32) + adapter_scale * product[:, j * block:(j + 1) * block]
        norm = jnp.sqrt(jnp.sum(heading * heading, axis=0, keepdims=True))
        scale = m_ref[j] / norm
        scaled = (heading * scale).astype(bf16)
        if out_ref.shape[1] == members * block:
            out_ref[:, j * block:(j + 1) * block] = scaled
        else:
            out_ref[:, pl.ds(pl.multiple_of(j * (out_ref.shape[1] // members) + i * block, block), block)] = scaled
        stat_ref[j] = jnp.concatenate([norm, scale], axis=0)
        cross_ref[j] = mm(a_ref[j * rank:(j + 1) * rank, :], scaled)


def column_prep(weight, down, up, magnitude, block, alternate):
    members, width, out = weight.shape
    rank = down.shape[2]
    wide = members * block
    eye = jnp.eye(members, dtype=bf16)[:, None, None, :, None]
    blocks = up.reshape(members, rank, out // block, 1, block) * eye
    blocks = blocks.transpose(2, 0, 1, 3, 4).reshape(out // block, members * rank, wide)
    flat = down.transpose(0, 2, 1).reshape(members * rank, width)
    if alternate:
        scaled_spec = pl.BlockSpec((width, wide), lambda i: (0, i))
    else:
        scaled_spec = pl.BlockSpec((width, members * out), lambda i: (0, 0))
    return pl.pallas_call(
        column_prep_kernel,
        grid=(out // block,),
        in_specs=[
            pl.BlockSpec((members, width, block), lambda i: (0, 0, i)),
            pl.BlockSpec((members * rank, width), lambda i: (0, 0)),
            pl.BlockSpec((1, members * rank, wide), lambda i: (i, 0, 0)),
            pl.BlockSpec((members, 1, block), lambda i: (0, 0, i)),
        ],
        out_specs=[
            scaled_spec,
            pl.BlockSpec((members, 2, block), lambda i: (0, 0, i)),
            pl.BlockSpec((members, rank, block), lambda i: (0, 0, i)),
        ],
        out_shape=[
            jax.ShapeDtypeStruct((width, members * out), bf16),
            jax.ShapeDtypeStruct((members, 2, out), f32),
            jax.ShapeDtypeStruct((members, rank, out), f32),
        ],
        cost_estimate=cost(
            flops=4 * members * width * out * 256, bytes_accessed=4 * members * width * out, transcendentals=0
        ),
        name="column_prep",
    )(weight, flat, blocks, magnitude[:, None, :])


def row_prep_kernel(w_ref, a_ref, b_ref, out_ref, cross_ref, square_ref):
    heading = w_ref[...].astype(f32) + adapter_scale * mm(a_ref[...], b_ref[...], TN)
    narrow = heading.astype(bf16)
    out_ref[...] = narrow
    cross_ref[...] = mm(a_ref[...], narrow)
    square_ref[...] = jnp.sum(heading * heading, axis=0, keepdims=True)


def row_prep(weight, down, up, block):
    rows, out = weight.shape
    rank = down.shape[1]
    along = lambda n: pl.BlockSpec((n, block), lambda i: (0, i))
    return pl.pallas_call(
        row_prep_kernel,
        grid=(out // block,),
        in_specs=[along(rows), pl.BlockSpec((rank, rows), lambda i: (0, 0)), along(rank)],
        out_specs=[along(rows), along(rank), along(1)],
        out_shape=[
            jax.ShapeDtypeStruct((rows, out), bf16),
            jax.ShapeDtypeStruct((rank, out), f32),
            jax.ShapeDtypeStruct((1, out), f32),
        ],
        cost_estimate=cost(flops=2 * rows * out * 256, bytes_accessed=4 * rows * out, transcendentals=0),
        name="row_prep",
    )(weight, down.T, up)


def turn_forward(values, cosine, signed_sine):
    return values * cosine + pltpu.roll(values, values.shape[1] // 2, 1) * signed_sine


def turn_backward(values, cosine, signed_sine):
    return values * cosine + pltpu.roll(values * signed_sine, values.shape[1] // 2, 1)


def over_blocks(total, block, body):
    if total // block <= 4:
        for i in range(total // block):
            body(i * block, (i + 1) * block)
    else:

        def step(i, carry):
            body(pl.multiple_of(i * block, block), total)
            return carry

        lax.fori_loop(0, total // block, step, 0)


def weights_t(keys, queries, kpos, qpos, qstart, scale):
    scores = mm(keys, queries, NT)
    allowed = jnp.logical_and(kpos <= qpos, kpos >= qstart)
    return jnp.where(allowed, jnp.exp2(scores * (scale * LOG2_E)), 0.0)


def attend_kernel(x_ref, cos_ref, sin_ref, kpos_ref, qinfo_ref, o_ref, l_ref, qs, ks, vt, os, *, scale, block):
    blocks, _, _, group, size = x_ref.shape
    total = blocks * group
    cosine, signed_sine = cos_ref[...], sin_ref[...]
    qs[...] = turn_forward(x_ref[:, 0, 0].reshape(total, size).astype(f32), cosine, signed_sine).astype(bf16)
    ks[...] = turn_forward(x_ref[:, 0, 1].reshape(total, size).astype(f32), cosine, signed_sine).astype(bf16)
    vt[...] = x_ref[:, 0, 2].reshape(total, size).astype(f32).T.astype(bf16)

    def body(first, last):
        at = pl.ds(first, block)
        weights = weights_t(
            ks[:last], qs[at, :], kpos_ref[:last], qinfo_ref[0, 0:1, at], qinfo_ref[0, 1:2, at], scale
        )
        totals = jnp.sum(weights, axis=0, keepdims=True)
        outer = mm(vt[:, :last], weights.astype(bf16))
        l_ref[0, 0:1, at] = totals
        os[at, :] = (outer / totals).T.astype(bf16)

    over_blocks(total, block, body)
    o_ref[:, 0] = os[...].reshape(blocks, group, size)


def attend(pairs, tables, kpos, qinfo):
    blocks, slots, _, group, size = pairs.shape
    total = blocks * group
    block = math.gcd(total, score_block)
    return pl.pallas_call(
        partial(attend_kernel, scale=1.0 / math.sqrt(size), block=block),
        grid=(slots,),
        in_specs=[
            pl.BlockSpec((blocks, 1, 3, group, size), lambda n: (0, n, 0, 0, 0)),
            pl.BlockSpec((total, size), lambda n: (0, 0)),
            pl.BlockSpec((total, size), lambda n: (0, 0)),
            pl.BlockSpec((total, 1), lambda n: (0, 0)),
            pl.BlockSpec((1, 2, total), lambda n: (n, 0, 0)),
        ],
        out_specs=[
            pl.BlockSpec((blocks, 1, group, size), lambda n: (0, n, 0, 0)),
            pl.BlockSpec((1, 1, total), lambda n: (n, 0, 0)),
        ],
        out_shape=[
            jax.ShapeDtypeStruct((blocks, slots, group, size), bf16),
            jax.ShapeDtypeStruct((slots, 1, total), f32),
        ],
        scratch_shapes=[
            pltpu.VMEM((total, size), bf16),
            pltpu.VMEM((total, size), bf16),
            pltpu.VMEM((size, total), bf16),
            pltpu.VMEM((total, size), bf16),
        ],
        cost_estimate=cost(
            flops=slots * 4 * total * total * size,
            bytes_accessed=slots * total * size * 8,
            transcendentals=slots * total * total // 2,
        ),
        name="attend",
    )(pairs, *tables, kpos, qinfo)


def attend_back_kernel(
    x_ref, o_ref, d_ref, l_ref, cos_ref, sin_ref, kpos_ref, qinfo_ref, g_ref, s_ref,
    qs, ks, kt, vs, dk, dv, dq, *, scale, block
):
    blocks, _, _, group, size = x_ref.shape
    total = blocks * group
    cosine, signed_sine = cos_ref[...], sin_ref[...]
    plain = [x_ref[:, 0, j].reshape(total, size).astype(f32) for j in range(3)]
    qs[...] = turn_forward(plain[0], cosine, signed_sine).astype(bf16)
    turned = turn_forward(plain[1], cosine, signed_sine)
    ks[...] = turned.astype(bf16)
    kt[...] = turned.T.astype(bf16)
    vs[...] = plain[2].astype(bf16)
    dk[...] = jnp.zeros_like(dk)
    dv[...] = jnp.zeros_like(dv)

    def body(first, last):
        at = pl.ds(first, block)
        span = block // group
        rows = pl.ds(first // group, span)
        weights = weights_t(
            ks[:last], qs[at, :], kpos_ref[:last], qinfo_ref[0, 0:1, at], qinfo_ref[0, 1:2, at], scale
        )
        totals = l_ref[0, 0:1, at]
        grad_t = d_ref[rows, 0].reshape(block, size).astype(f32).T
        out_t = o_ref[rows, 0].reshape(block, size).astype(f32).T
        dlog = -jnp.sum(grad_t * out_t, axis=0, keepdims=True) / totals
        outer_t = (grad_t / totals).astype(bf16)
        dweights = mm(vs[:last], outer_t)
        dscores = (weights * (dweights + dlog)).astype(bf16)
        dk[:last] += mm(dscores, qs[at, :])
        dv[:last] += mm(weights.astype(bf16), outer_t, NT)
        dq[at, :] = mm(kt[:, :last], dscores).T

    over_blocks(total, block, body)
    grads = (
        turn_backward(dq[...] * scale, cosine, signed_sine),
        turn_backward(dk[...] * scale, cosine, signed_sine),
        dv[...],
    )
    sums = []
    for j in range(3):
        g_ref[:, 0, j] = grads[j].astype(bf16).reshape(blocks, group, size)
        sums.append(jnp.sum(grads[j] * plain[j], axis=0, keepdims=True))
    s_ref[0] = jnp.concatenate(sums, axis=0)


def attend_back(pairs, outputs, grads, totals, tables, kpos, qinfo):
    blocks, slots, _, group, size = pairs.shape
    total = blocks * group
    block = math.gcd(total, score_block)
    half = pl.BlockSpec((blocks, 1, group, size), lambda n: (0, n, 0, 0))
    whole = pl.BlockSpec((blocks, 1, 3, group, size), lambda n: (0, n, 0, 0, 0))
    return pl.pallas_call(
        partial(attend_back_kernel, scale=1.0 / math.sqrt(size), block=block),
        grid=(slots,),
        in_specs=[
            whole,
            half,
            half,
            pl.BlockSpec((1, 1, total), lambda n: (n, 0, 0)),
            pl.BlockSpec((total, size), lambda n: (0, 0)),
            pl.BlockSpec((total, size), lambda n: (0, 0)),
            pl.BlockSpec((total, 1), lambda n: (0, 0)),
            pl.BlockSpec((1, 2, total), lambda n: (n, 0, 0)),
        ],
        out_specs=[whole, pl.BlockSpec((1, 3, size), lambda n: (n, 0, 0))],
        out_shape=[
            jax.ShapeDtypeStruct(pairs.shape, bf16),
            jax.ShapeDtypeStruct((slots, 3, size), f32),
        ],
        scratch_shapes=[
            pltpu.VMEM((total, size), bf16),
            pltpu.VMEM((total, size), bf16),
            pltpu.VMEM((size, total), bf16),
            pltpu.VMEM((total, size), bf16),
            pltpu.VMEM((total, size), f32),
            pltpu.VMEM((total, size), f32),
            pltpu.VMEM((total, size), f32),
        ],
        cost_estimate=cost(
            flops=slots * 10 * total * total * size,
            bytes_accessed=slots * total * size * 16,
            transcendentals=slots * total * total // 2,
        ),
        name="attend_back",
    )(pairs, outputs, grads, totals, *tables, kpos, qinfo)


def to_pairs_kernel(*refs, dims):
    x_refs, w_ref, out_ref, xs = refs[:4], refs[4], refs[5], refs[6]
    count = x_refs[0].shape[0]

    @pl.when(jnp.logical_and(pl.program_id(0) == 0, pl.program_id(1) == 0))
    def _():
        for i in range(4):
            xs[i * count:(i + 1) * count] = x_refs[i][...]

    rows, heads, _, pieces, quarter, size = out_ref.shape
    product = mm(xs[...], w_ref[...], dims).astype(bf16)
    for i in range(pieces):
        for r in range(rows):
            at = (i * rows + r) * quarter
            for h in range(heads):
                out_ref[r, h, 0, i] = product[at:at + quarter, h * size:(h + 1) * size]


def project_to_pairs(pieces, weight, dims, parts, heads, size, span):
    rows, quarter, width = pieces[0].shape
    count = rows * quarter
    wide = span * size
    steps = heads // span
    if dims == NN:
        w_spec = pl.BlockSpec((width, wide), lambda j, h: (0, j * steps + h))
    else:
        w_spec = pl.BlockSpec((wide, width), lambda j, h: (j * steps + h, 0))
    return pl.pallas_call(
        partial(to_pairs_kernel, dims=dims),
        grid=(parts, steps),
        in_specs=[pl.BlockSpec(memory_space=pltpu.VMEM)] * 4 + [w_spec],
        out_specs=[
            pl.BlockSpec((rows, span, 1, 4, quarter, size), lambda j, h: (0, h, j, 0, 0, 0)),
            pl.BlockSpec((4 * count, width), lambda j, h: (0, 0)),
        ],
        out_shape=[
            jax.ShapeDtypeStruct((rows, heads, parts, 4, quarter, size), bf16),
            jax.ShapeDtypeStruct((4 * count, width), bf16),
        ],
        cost_estimate=cost(
            flops=8 * count * width * parts * heads * size,
            bytes_accessed=2 * width * (8 * count + parts * heads * size),
            transcendentals=0,
        ),
        name="project_to_pairs",
    )(*[p.reshape(count, width) for p in pieces], weight)


def split_out(product, out_refs, at):
    kept_ref, near_ref, send_ref = out_refs
    half = product.shape[0] // 4
    kept_ref[at:at + half] = product[:half]
    near_ref[at:at + half] = product[half:2 * half]
    for i in range(2):
        send_ref[i, at:at + half] = product[(i + 2) * half:(i + 3) * half]


def split_specs(count, out, block):
    one, two = pl.BlockSpec((count, block), lambda n: (0, n)), pl.BlockSpec((2, count, block), lambda n: (0, 0, n))
    shapes = [(count, out), (count, out), (2, count, out)]
    return [one, one, two], [jax.ShapeDtypeStruct(v, bf16) for v in shapes]


def by_rows(kept, near, send, quarter):
    shape = (kept.shape[0] // quarter, quarter, kept.shape[1])
    return kept.reshape(shape), near.reshape(shape), send.reshape((2,) + shape)


def join_pairs(x_ref, flat_ref):
    rows, heads, parts, pieces, quarter, size = x_ref.shape
    for i in range(pieces):
        for r in range(rows):
            at = (i * rows + r) * quarter
            for j in range(parts):
                for h in range(heads):
                    col = (j * heads + h) * size
                    flat_ref[at:at + quarter, col:col + size] = x_ref[r, h, j, i]


def from_pairs_kernel(x_ref, w_ref, flat_ref, *out_refs):
    @pl.when(pl.program_id(0) == 0)
    def _():
        join_pairs(x_ref, flat_ref)

    split_out(mm(flat_ref[...], w_ref[...]).astype(bf16), out_refs, 0)


def project_from_pairs(pairs, weight, block):
    rows, heads, parts, pieces, quarter, size = pairs.shape
    count, width = rows * quarter, parts * heads * size
    out = weight.shape[1]
    specs, shapes = split_specs(count, out, block)
    flat, *split = pl.pallas_call(
        from_pairs_kernel,
        grid=(out // block,),
        in_specs=[pl.BlockSpec(pairs.shape, lambda n: (0,) * 6), pl.BlockSpec((width, block), lambda n: (0, n))],
        out_specs=[pl.BlockSpec((4 * count, width), lambda n: (0, 0))] + specs,
        out_shape=[jax.ShapeDtypeStruct((4 * count, width), bf16)] + shapes,
        cost_estimate=cost(
            flops=8 * count * width * out, bytes_accessed=2 * (out * width + 4 * count * (2 * width + out)),
            transcendentals=0,
        ),
        name="project_from_pairs",
    )(pairs, weight)
    return flat, by_rows(*split, quarter)


def project_split_kernel(*refs, dims):
    x_refs, w_ref, out_refs = refs[:-4], refs[-4], refs[-3:]
    at = 0
    for x_ref in x_refs:
        split_out(mm(x_ref[...], w_ref[...], dims).astype(bf16), out_refs, at)
        at += x_ref.shape[0] // 4


def project_split(flats, weight, dims, block, quarter):
    width = flats[0].shape[1]
    count = sum(v.shape[0] for v in flats) // 4
    if dims == NN:
        out = weight.shape[1]
        w_spec = pl.BlockSpec((width, block), lambda n: (0, n))
    else:
        out = weight.shape[0]
        w_spec = pl.BlockSpec((block, width), lambda n: (n, 0))
    specs, shapes = split_specs(count, out, block)
    split = pl.pallas_call(
        partial(project_split_kernel, dims=dims),
        grid=(out // block,),
        in_specs=[pl.BlockSpec(v.shape, lambda n: (0, 0)) for v in flats] + [w_spec],
        out_specs=specs,
        out_shape=shapes,
        cost_estimate=cost(
            flops=8 * count * width * out, bytes_accessed=2 * (out * width + 4 * count * (width + out)), transcendentals=0
        ),
        name="project_split",
    )(*flats, weight)
    return by_rows(*split, quarter)


def cotangent_kernel(*refs):
    x_refs, w_ref, out_ref, flat_ref = refs[:4], refs[4], refs[5], refs[6]
    part = x_refs[0].shape[0]
    for i in range(4):
        flat_ref[i * part:(i + 1) * part] = x_refs[i][...]
    out_ref[...] = mm(flat_ref[...], w_ref[...], NT).astype(bf16)


def project_cotangent(pieces, weight, rows, first):
    total, quarter, width = pieces[0].shape
    part = rows * quarter
    at = first // rows
    out = weight.shape[0]
    return pl.pallas_call(
        cotangent_kernel,
        grid=(1,),
        in_specs=[pl.BlockSpec((part, width), lambda c: (at, 0))] * 4 + [pl.BlockSpec((out, width), lambda c: (0, 0))],
        out_specs=[pl.BlockSpec((4 * part, out), lambda c: (0, 0)), pl.BlockSpec((4 * part, width), lambda c: (0, 0))],
        out_shape=[jax.ShapeDtypeStruct((4 * part, out), bf16), jax.ShapeDtypeStruct((4 * part, width), bf16)],
        cost_estimate=cost(
            flops=8 * part * width * out, bytes_accessed=2 * width * (out + 8 * part), transcendentals=0
        ),
        name="project_cotangent",
    )(*[p.reshape(total * quarter, width) for p in pieces], weight)


def assemble(pairs):
    rows, heads, parts, pieces, quarter, size = pairs.shape
    tokens, width = 4 * rows * quarter, parts * heads * size
    return pl.pallas_call(
        join_pairs,
        out_shape=jax.ShapeDtypeStruct((tokens, width), bf16),
        cost_estimate=cost(flops=0, bytes_accessed=4 * tokens * width, transcendentals=0),
        name="assemble",
    )(pairs)


def runs(lengths, cut):
    at = 0
    for k, n in enumerate(lengths):
        start = 0
        while start < n:
            step = min(n - start, cut - at % cut)
            yield k, start, at, step
            start += step
            at += step


def width_of(sizes, pieces):
    return -(-sum(sizes) // (pieces * LANES)) * LANES


def part_of(ref, j, rank, lanes):
    return ref.at[j, :, lanes] if len(ref.shape) == 3 else ref.at[j * rank:(j + 1) * rank, lanes]


def cells(shapes):
    return [(v, j, c) for v, (members, size) in enumerate(shapes) for j in range(members) for c in range(size // LANES)]


def pack_kernel(*refs, plan, count):
    in_refs, sum_refs, out_ref, sums = refs[:count], refs[count:-2], refs[-2], refs[-1]
    rank = out_ref.shape[1]
    sums[...] = jnp.zeros_like(sums)
    for k, (v, j, c) in enumerate(cells([(ref.shape[0], ref.shape[2]) for ref in sum_refs])):
        at = k // rank * LANES
        sums[k % rank:k % rank + 1, at:at + LANES] = sum_refs[v][j, :, c * LANES:(c + 1) * LANES]
    base = 0
    for entries, cut in plan:
        sizes = [n for _, _, n in entries]
        for k, start, at, n in runs(sizes, cut):
            which, j, _ = entries[k]
            lanes = slice(start, start + n)
            values = sums[:, lanes] if which is None else part_of(in_refs[which], j, rank, lanes)[...]
            out_ref[at // cut, :, base + at % cut:base + at % cut + n] = values.astype(bf16)
        end = sum(sizes)
        while end < out_ref.shape[0] * cut:
            n = cut - end % cut
            out_ref[end // cut, :, base + end % cut:base + end % cut + n] = jnp.zeros((rank, n), bf16)
            end += n
        base += cut


def unpack_kernel(*refs, plan, count):
    x_ref, m_refs, out_refs = refs[0], refs[1:1 + count], refs[1 + count:]
    rank = x_ref.shape[1]
    base = 0
    for entries, cut in plan:
        for k, start, at, n in runs([n for _, _, n in entries], cut):
            values = x_ref[at // cut, :, base + at % cut:base + at % cut + n].astype(f32)
            which, j, _ = entries[k]
            if which is not None:
                part_of(out_refs[which], j, rank, slice(start, start + n))[...] = values
                continue
            for cell, (v, j, c) in enumerate(cells([ref.shape for ref in m_refs])):
                lane = cell // rank * LANES - start
                if 0 <= lane < n:
                    place = (slice(j, j + 1), slice(c * LANES, (c + 1) * LANES))
                    row = slice(cell % rank, cell % rank + 1)
                    out_refs[v - count][place] = values[row, lane:lane + LANES] / m_refs[v][place]
        base += cut


def packing(over_all, over_seq, vectors, pieces, rank):
    plan, at = [], 0
    for arrays in (over_all, over_seq):
        entries = []
        for v in arrays:
            members = v.shape[0] if len(v.shape) == 3 else v.shape[0] // rank
            entries += [(at, j, v.shape[-1]) for j in range(members)]
            at += 1
        plan.append(entries)
    blocks = len(cells([(v.shape[0], v.shape[2]) for v in vectors]))
    plan[1].append((None, 0, -(-blocks // rank) * LANES))
    return [(entries, width_of([n for _, _, n in entries], pieces)) for entries in plan]


def pack(plan, arrays, vectors, pieces, rank):
    return pl.pallas_call(
        partial(pack_kernel, plan=plan, count=len(arrays)),
        out_shape=jax.ShapeDtypeStruct((pieces, rank, sum(cut for _, cut in plan)), bf16),
        scratch_shapes=[pltpu.VMEM((rank, plan[1][0][-1][2]), f32)],
        cost_estimate=cost(flops=0, bytes_accessed=4 * sum(v.size for v in arrays), transcendentals=0),
        name="pack",
    )(*arrays, *vectors)


def unpack(plan, values, arrays, magnitudes):
    return pl.pallas_call(
        partial(unpack_kernel, plan=plan, count=len(magnitudes)),
        out_shape=[jax.ShapeDtypeStruct(v.shape, f32) for v in (*arrays, *magnitudes)],
        cost_estimate=cost(flops=0, bytes_accessed=6 * values.size, transcendentals=0),
        name="unpack",
    )(values, *magnitudes)


def gated_kernel(*refs):
    x_refs, w_ref, e_ref, hidden_ref, grads_ref, sums_ref, xs = refs[:4], *refs[4:]
    count = x_refs[0].shape[0]

    @pl.when(pl.program_id(0) == 0)
    def _():
        for i in range(4):
            xs[i * count:(i + 1) * count] = x_refs[i][...]

    product = mm(xs[...], w_ref[...])
    block = LANES
    for k in range(product.shape[1] // (2 * block)):
        at, mine = k * 2 * block, slice(k * block, (k + 1) * block)
        gate, up = product[:, at:at + block], product[:, at + block:at + 2 * block]
        dhid = e_ref[:, mine].astype(f32)
        sig = 1.0 / (1.0 + jnp.exp(-gate))
        act = gate * sig
        hidden_ref[:, mine] = (act * up).astype(bf16)
        dgate = dhid * up * (sig * (1.0 + gate * (1.0 - sig)))
        dup = dhid * act
        grads_ref[:, at:at + block] = dgate.astype(bf16)
        grads_ref[:, at + block:at + 2 * block] = dup.astype(bf16)
        sums_ref[0, :, mine] = jnp.sum(gate * dgate, axis=0, keepdims=True)
        sums_ref[1, :, mine] = jnp.sum(up * dup, axis=0, keepdims=True)


def gated(pieces, weight, dhid):
    rows, quarter, width = pieces[0].shape
    count = rows * quarter
    out = dhid.shape[1]
    block = GATED_BLOCKS * LANES
    return pl.pallas_call(
        gated_kernel,
        grid=(-(-out // block),),
        in_specs=[pl.BlockSpec(memory_space=pltpu.VMEM)] * 4
        + [
            pl.BlockSpec((width, 2 * block), lambda i: (0, i)),
            pl.BlockSpec((4 * count, block), lambda i: (0, i)),
        ],
        out_specs=[
            pl.BlockSpec((4 * count, block), lambda i: (0, i)),
            pl.BlockSpec((4 * count, 2 * block), lambda i: (0, i)),
            pl.BlockSpec((2, 1, block), lambda i: (0, 0, i)),
            pl.BlockSpec((4 * count, width), lambda i: (0, 0)),
        ],
        out_shape=[
            jax.ShapeDtypeStruct((4 * count, out), bf16),
            jax.ShapeDtypeStruct((4 * count, 2 * out), bf16),
            jax.ShapeDtypeStruct((2, 1, out), f32),
            jax.ShapeDtypeStruct((4 * count, width), bf16),
        ],
        cost_estimate=cost(
            flops=16 * count * width * out,
            bytes_accessed=4 * width * out + 8 * count * (2 * width + 4 * out),
            transcendentals=4 * count * out,
        ),
        name="gated",
    )(*[p.reshape(count, width) for p in pieces], weight, dhid)


def chunk_lanes(refs):
    ends = [0]
    for ref in refs:
        ends.append(ends[-1] + ref.shape[0])
    return [slice(a, b) for a, b in zip(ends, ends[1:])]


def column_grads_kernel(*refs, chunks, steps, joins):
    x_refs, d_refs, refs = refs[:chunks], list(refs[chunks:2 * chunks]), list(refs[2 * chunks:])
    if joins:
        pairs_ref, d_refs[-1] = d_refs[-1], refs.pop(9)

        @pl.when(pl.program_id(0) == 0)
        def _():
            join_pairs(pairs_ref, d_refs[-1])

    w_ref, a_ref, b_ref, stat_ref, m_ref, sum_ref, cross_ref, gb_ref, ga_ref, ts, dts, es = refs
    members, rank, block = b_ref.shape
    lanes = chunk_lanes(x_refs)
    i = pl.program_id(0)

    @pl.when(i == 0)
    def _():
        for c in range(chunks):
            ts[:, lanes[c]] = mm(a_ref[...], x_refs[c][...], NT).astype(bf16)
        dts[...] = jnp.zeros_like(dts)

    @pl.when(i < steps)
    def _():
        found = sum(mm(ts[:, lanes[c]], d_refs[c][...]) for c in range(chunks))
        spread, along = [], []
        for j in range(members):
            b = b_ref[j].astype(f32)
            scale = stat_ref[j, 1:2]
            coef = -sum_ref[j] / (m_ref[j] * stat_ref[j, 0:1])
            mine = found[j * rank:(j + 1) * rank, j * block:(j + 1) * block]
            gb_ref[j] = (adapter_scale * (mine * scale + coef * cross_ref[j])).astype(bf16)
            empty = jnp.zeros((rank, block), f32)
            row = lambda v: jnp.concatenate([v if k == j else empty for k in range(members)], axis=1)
            spread.append(row(adapter_scale * coef * b))
            along.append(row(adapter_scale * scale * b))
        wide = members * block
        es[:, pl.ds(pl.multiple_of(i * wide, wide), wide)] = jnp.concatenate(spread, axis=0).astype(bf16)
        up = jnp.concatenate(along, axis=0).astype(bf16)
        for c in range(chunks):
            dts[:, lanes[c]] += mm(up, d_refs[c][...], NT)

    @pl.when(i >= steps)
    def _():
        span = w_ref.shape[0]
        at = pl.ds(pl.multiple_of((i - steps) * span, span), span)
        total = mm(es[...], w_ref[...], NT)
        for c in range(chunks):
            total = total + mm(dts[:, lanes[c]].astype(bf16), x_refs[c][:, at])
        ga_ref[...] = total.astype(bf16)


def column_grads(rows, grads, weight, down, up, stat, magnitude, sums, cross, block):
    tokens, width = sum(v.shape[0] for v in rows), rows[0].shape[1]
    members, rank, out = up.shape
    chunks, steps, span = len(rows), out // block, 1024
    first = lambda i: jnp.minimum(i, steps - 1)
    then = lambda i: jnp.maximum(i - steps, 0)
    part = lambda n: pl.BlockSpec((members, n, block), lambda i: (0, 0, first(i)))
    joins = len(grads[-1].shape) == 6
    joined = (rows[-1].shape[0], members * out)
    wide = members * block
    ranks = members * rank
    assert steps == 1 or not joins
    grad_b, grad_a, *flat = pl.pallas_call(
        partial(column_grads_kernel, chunks=chunks, steps=steps, joins=joins),
        grid=(steps + width // span,),
        in_specs=[pl.BlockSpec(v.shape, lambda i: (0, 0)) for v in rows]
        + [
            pl.BlockSpec(v.shape, lambda i: (0,) * 6) if len(v.shape) == 6
            else pl.BlockSpec((v.shape[0], wide), lambda i: (0, first(i)))
            for v in grads
        ]
        + [
            pl.BlockSpec((span, members * out), lambda i: (then(i), 0)),
            pl.BlockSpec((ranks, width), lambda i: (0, 0)),
            part(rank), part(2), part(1), part(1), part(rank),
        ],
        out_specs=[part(rank), pl.BlockSpec((ranks, span), lambda i: (0, then(i)))]
        + [pl.BlockSpec(joined, lambda i: (0, 0))] * joins,
        out_shape=[
            jax.ShapeDtypeStruct((members, rank, out), bf16),
            jax.ShapeDtypeStruct((ranks, width), bf16),
        ]
        + [jax.ShapeDtypeStruct(joined, bf16)] * joins,
        scratch_shapes=[
            pltpu.VMEM((ranks, tokens), bf16),
            pltpu.VMEM((ranks, tokens), f32),
            pltpu.VMEM((ranks, members * out), bf16),
        ],
        cost_estimate=cost(
            flops=4 * 256 * width * members * out // 4,
            bytes_accessed=2 * (width * members * out + tokens * (width + members * out)),
            transcendentals=0,
        ),
        name="column_grads",
    )(*rows, *grads, weight, down.transpose(0, 2, 1).reshape(ranks, width), up, stat, magnitude[:, None, :], sums, cross)
    return (grad_a, grad_b, *flat)


def row_grads_kernel(*refs, chunks):
    h_refs, d_refs, refs = refs[:chunks], refs[chunks:2 * chunks], refs[2 * chunks:]
    w_ref, a_ref, b_ref, stat_ref, coef_ref, ga_ref, gb_ref, ts, dts, acc = refs
    lanes = chunk_lanes(h_refs)
    i = pl.program_id(0)

    @pl.when(i == 0)
    def _():
        for c in range(chunks):
            ts[:, lanes[c]] = mm(a_ref[...], h_refs[c][...], NT).astype(bf16)
        dts[...] = jnp.zeros_like(dts)
        acc[...] = jnp.zeros_like(acc)

    b = b_ref[...].astype(f32)
    coef = coef_ref[...]
    found = sum(mm(ts[:, lanes[c]], d_refs[c][...]) for c in range(chunks))
    gb_ref[...] = (adapter_scale * (found + coef * stat_ref[...])).astype(bf16)
    up = (adapter_scale * b).astype(bf16)
    for c in range(chunks):
        dts[:, lanes[c]] += mm(up, d_refs[c][...], NT)
    acc[...] += mm((adapter_scale * coef * b).astype(bf16), w_ref[...], NT)

    @pl.when(i == pl.num_programs(0) - 1)
    def _():
        total = acc[...]
        for c in range(chunks):
            total = total + mm(dts[:, lanes[c]].astype(bf16), h_refs[c][...])
        ga_ref[...] = total.astype(bf16)


def row_grads(rows, grads, weight, down, up, stat, coef, block):
    tokens, count = sum(v.shape[0] for v in rows), rows[0].shape[1]
    rank, out = up.shape
    chunks = len(rows)
    along = lambda n: pl.BlockSpec((n, block), lambda i: (0, i))
    return pl.pallas_call(
        partial(row_grads_kernel, chunks=chunks),
        grid=(out // block,),
        in_specs=[pl.BlockSpec(v.shape, lambda i: (0, 0)) for v in rows]
        + [pl.BlockSpec((v.shape[0], block), lambda i: (0, i)) for v in grads]
        + [along(count), pl.BlockSpec((rank, count), lambda i: (0, 0)), along(rank), along(rank), along(1)],
        out_specs=[pl.BlockSpec((rank, count), lambda i: (0, 0)), along(rank)],
        out_shape=[jax.ShapeDtypeStruct((rank, count), bf16), jax.ShapeDtypeStruct((rank, out), bf16)],
        scratch_shapes=[
            pltpu.VMEM((rank, tokens), bf16),
            pltpu.VMEM((rank, tokens), f32),
            pltpu.VMEM((rank, count), f32),
        ],
        cost_estimate=cost(
            flops=256 * count * out, bytes_accessed=2 * (count * out + tokens * (count + out)), transcendentals=0
        ),
        name="row_grads",
    )(*rows, *grads, weight, down.T, up, stat, coef)


def norm_scale(values):
    return lax.rsqrt(jnp.mean(values * values, axis=-1, keepdims=True) + epsilon)


def norm_back(values, gain, grad):
    r = norm_scale(values)
    weighted = gain * grad
    return r * weighted - values * (r * r * r) * jnp.mean(values * weighted, axis=-1, keepdims=True)


def rotary_tables(positions, head_size):
    half_size = head_size // 2
    frequency = rope_base ** (-(2.0 * jnp.arange(half_size, dtype=f32)) / head_size)
    angles = positions.astype(f32)[:, None] * frequency[None, :]
    cosine, sine = jnp.cos(angles), jnp.sin(angles)
    return (jnp.concatenate([cosine, cosine], axis=-1), jnp.concatenate([-sine, sine], axis=-1))


def local(
    layer_in, cotangent, doc_lengths, pad_counts, gain_attn, gain_ffn, w_qkv, a_qkv, b_qkv, m_qkv, w_out, a_out,
    b_out, m_out, w_gateup, a_gateup, b_gateup, m_gateup, w_down, a_down, b_down, m_down,
):
    rows, quarter, width = layer_in.shape
    tensor, seq = lax.axis_size("tensor"), lax.axis_size("seq")
    assert tensor == len(PIECES)
    me_t, me_s = lax.axis_index("tensor"), lax.axis_index("seq")
    group = quarter * tensor
    total = group * seq
    feat = w_qkv.shape[2]
    heads = feat // HEAD_DIM
    rank = a_qkv.shape[2]
    ff = w_down.shape[0]
    piece_of = jnp.bitwise_xor(me_t, jnp.array(PIECES, jnp.int32))
    in_block = (piece_of[:, None] * quarter + jnp.arange(quarter, dtype=jnp.int32)[None, :]).reshape(group)
    positions = (jnp.arange(seq, dtype=jnp.int32)[:, None] * group + in_block[None, :]).reshape(total)
    tables = rotary_tables(positions, HEAD_DIM)
    offsets = jnp.cumsum(doc_lengths, axis=1)
    starts = jnp.max(
        jnp.where(offsets[:, :, None] <= positions[None, None, :], offsets[:, :, None], 0), axis=1
    )
    kpos = positions[:, None]
    few = rows // 3
    cuts = [slice(rows - few, rows), slice(0, rows - few)]
    span = range(2)
    pair_counts = [(at.stop - at.start) * heads for at in cuts]
    slots = [-(-count // seq) for count in pair_counts]
    mine = [me_s * slots[c] + jnp.arange(slots[c]) for c in span]
    live = [mine[c] < pair_counts[c] for c in span]

    def pair_info(c):
        row = jnp.minimum(mine[c] // heads + cuts[c].start, cuts[c].stop - 1)
        chosen = (row[:, None] == jnp.arange(rows)[None, :])[:, :, None]
        return jnp.stack(
            [jnp.broadcast_to(positions[None], (slots[c], total)), jnp.sum(jnp.where(chosen, starts[None], 0), axis=1)],
            axis=1,
        )

    qinfo = [pair_info(c) for c in span]

    def send_pairs(values, c):
        parts = values.shape[2]
        laid = values.reshape(pair_counts[c], parts, group, HEAD_DIM)
        if slots[c] * seq > pair_counts[c]:
            laid = jnp.pad(laid, ((0, slots[c] * seq - pair_counts[c]), (0, 0), (0, 0), (0, 0)))
        return exchange(laid.reshape(seq, slots[c], parts, group, HEAD_DIM))

    def fetch_pairs(values, c):
        parts = values.shape[2]
        laid = exchange(values).reshape(seq * slots[c], parts, group, HEAD_DIM)[:pair_counts[c]]
        return laid.reshape(pair_counts[c] // heads, heads, parts, tensor, quarter, HEAD_DIM)

    def to_heads(pieces, weight):
        return project_to_pairs(pieces, weight, NN, 3, heads, HEAD_DIM, heads)

    def back_to_heads(pieces, weight):
        return project_to_pairs(pieces, weight, NT, 1, heads, HEAD_DIM, 2)

    owned = me_s * group + me_t * quarter + jnp.arange(quarter, dtype=jnp.int32)
    valid = (owned[None, :] < total - pad_counts[:, None]).astype(f32)
    cot = cotangent.astype(f32) * valid[:, :, None]
    wide_in = [layer_in[at].astype(f32) for at in cuts]

    def normed(values, gain):
        return (values * norm_scale(values) * gain).astype(bf16)

    started = [gather_start(normed(wide_in[c], gain_attn)) for c in span]
    qkv_w, qkv_stat, qkv_cross = column_prep(w_qkv, a_qkv, b_qkv, m_qkv, 256, False)
    started[0], qkv_w = after(started[0], qkv_w)
    normed_a, d_qkv, pairs, outputs, totals, att = [[None] * 2 for _ in range(6)]
    laid, normed_a[0] = to_heads(gather_end(*started[0]), qkv_w)

    laid, started[1], w_down = after(laid, started[1], w_down)
    pairs[0] = send_pairs(laid, 0)
    laid, normed_a[1] = to_heads(gather_end(*started[1]), qkv_w)
    down_w, down_cross, down_square = row_prep(w_down, a_down, b_down, 256)
    pairs[0], laid, down_square, w_out, w_gateup = after(pairs[0], laid, down_square, w_out, w_gateup)

    u_out, middle, hidden, d_gu, gu_sum, normed_f, d_mid, du_out, dhid, du_down = [[None] * 2 for _ in range(10)]

    def of_cotangent(whole, c):
        return project_cotangent(whole, down_w, cuts[c].stop - cuts[c].start, cuts[c].start)

    pairs[1] = send_pairs(laid, 1)
    outputs[0], totals[0] = attend(pairs[0], tables, kpos, qinfo[0])
    down_square = tensor_sum(down_square)
    down_scale = m_down / jnp.sqrt(down_square[0])
    scaled, w_gateup, w_out = after((cot * down_scale).astype(bf16), w_gateup, w_out)
    out_w, out_cross, out_square = row_prep(w_out, a_out, b_out, 512)
    gu_w, gu_stat, gu_cross = column_prep(w_gateup, a_gateup, b_gateup, m_gateup, LANES, True)
    started, gu_w, out_w = after(gather_start(scaled), gu_w, out_w)
    whole_cot = gather_end(*started)
    pairs[1], outputs[0], whole_cot, out_square = after(pairs[1], outputs[0], whole_cot, out_square)

    fetched = fetch_pairs(outputs[0][:, :, None], 0)
    outputs[1], totals[1] = attend(pairs[1], tables, kpos, qinfo[1])
    out_square = tensor_sum(out_square)
    out_scale = m_out / jnp.sqrt(out_square[0])
    fetched, outputs[1], whole_cot, out_scale = after(fetched, outputs[1], whole_cot, out_scale)

    returned = fetch_pairs(outputs[1][:, :, None], 1)
    att[0], split = project_from_pairs(fetched, out_w, 1024)
    moving, whole_cot = after(scatter_start(*split), whole_cot)
    for c in span:
        dhid[c], du_down[c] = of_cotangent(whole_cot, c)
    tail, dhid = after(scatter_end(*moving), dhid)
    u_out[0] = tail * out_scale
    middle[0] = wide_in[0] + u_out[0]
    started = gather_start(normed(middle[0], gain_ffn))

    att[1], split = project_from_pairs(returned, out_w, 1024)
    started, split = after(started, split)
    moving, whole = after(scatter_start(*split), gather_end(*started))
    hidden[0], d_gu[0], gu_sum[0], normed_f[0] = gated(whole, gu_w, dhid[0])
    tail, d_gu[0] = after(scatter_end(*moving), d_gu[0])
    u_out[1] = tail * out_scale
    middle[1] = wide_in[1] + u_out[1]
    h_f, d_gu[0] = after(normed(middle[1], gain_ffn), d_gu[0])
    started = gather_start(h_f)
    split = project_split([d_gu[0]], gu_w, NT, 1024, quarter)
    whole, behind = after(gather_end(*started), scatter_start(*split))

    hidden[1], d_gu[1], gu_sum[1], normed_f[1] = gated(whole, gu_w, dhid[1])
    tail, d_gu[1] = after(scatter_end(*behind), d_gu[1])
    d_mid[0] = cot[cuts[0]] + norm_back(middle[0], gain_ffn, tail)
    scaled, d_gu[1] = after((d_mid[0] * out_scale).astype(bf16), d_gu[1])
    started, split = after(gather_start(scaled), project_split([d_gu[1]], gu_w, NT, 512, quarter))
    moving, whole = after(scatter_start(*split), gather_end(*started))

    d_att, du_out[0] = back_to_heads(whole, out_w)
    d_outputs = send_pairs(d_att, 0)[:, :, 0]
    tail, d_att = after(scatter_end(*moving), d_att)
    d_mid[1] = cot[cuts[1]] + norm_back(middle[1], gain_ffn, tail)
    scaled, d_outputs = after((d_mid[1] * out_scale).astype(bf16), d_outputs)
    d_pairs, pair_sums = [None] * 2, [None] * 2
    d_pairs[0], pair_sums[0] = attend_back(pairs[0], outputs[0], d_outputs, totals[0], tables, kpos, qinfo[0])
    d_pairs[0], scaled, hidden = after(d_pairs[0], scaled, hidden)
    fetched = fetch_pairs(d_pairs[0], 0)
    started, split = after(gather_start(scaled), project_split(hidden[::-1], down_w, NN, 512, quarter))
    d_att, du_out[1] = back_to_heads(gather_end(*started), out_w)
    d_att, fetched = after(d_att, fetched)

    d_att, att, out_sum = after(d_att, att, sum(jnp.sum(u_out[c] * d_mid[c], axis=(0, 1)) for c in span)[None])
    d_outputs = send_pairs(d_att, 1)[:, :, 0]
    out_sum = tensor_sum(out_sum)
    grad_a_out, grad_b_out = row_grads(att, du_out, out_w, a_out, b_out, out_cross, -out_sum / out_square, 512)
    d_outputs, grad_a_out, d_gu = after(d_outputs, grad_a_out, d_gu)
    d_pairs[1], pair_sums[1] = attend_back(pairs[1], outputs[1], d_outputs, totals[1], tables, kpos, qinfo[1])

    d_pairs[1], split, d_gu = after(d_pairs[1], split, d_gu)
    returned = fetch_pairs(d_pairs[1], 1)
    moving, d_gu = after(scatter_start(*split), d_gu)
    gu_sums = sum(gu_sum)
    grad_a_gu, grad_b_gu = column_grads(
        normed_f, d_gu, gu_w, a_gateup, b_gateup, gu_stat, m_gateup, gu_sums, gu_cross, LANES
    )
    tail, grad_a_gu, fetched = after(scatter_end(*moving), grad_a_gu, fetched)
    u_down = tail * down_scale
    layer_out = (jnp.concatenate(middle[::-1]) + u_down).astype(bf16)
    down_sum = tensor_sum(jnp.sum(u_down * cot, axis=(0, 1))[None])
    d_qkv[0] = assemble(fetched)
    grad_a_down, grad_b_down = row_grads(
        hidden, du_down, down_w, a_down, b_down, down_cross, -down_sum / down_square, 512
    )
    fetched, d_qkv[0], grad_a_down, layer_out = after(returned, d_qkv[0], grad_a_down, layer_out)

    qkv_sums = 0.0
    for c in span:
        choice = jnp.logical_and((mine[c] % heads)[:, None] == jnp.arange(heads)[None, :], live[c][:, None])
        qkv_sums = qkv_sums + jnp.sum(jnp.where(choice[:, None, :, None], pair_sums[c][:, :, None, :], 0.0), axis=0)
    qkv_sums = qkv_sums.reshape(3, 1, feat)
    grad_a_qkv, grad_b_qkv, d_qkv[1] = column_grads(
        normed_a, [d_qkv[0], fetched], qkv_w, a_qkv, b_qkv, qkv_stat, m_qkv, qkv_sums, qkv_cross, feat
    )

    over_all = [grad_a_gu, grad_b_out, grad_b_down, grad_a_qkv]
    over_seq = [grad_b_gu, grad_a_out, grad_a_down, grad_b_qkv]
    vectors = [gu_sums, out_sum[None], down_sum[None], qkv_sums]
    plan = packing(over_all, over_seq, vectors, seq, rank)
    cut = plan[0][1]
    packed, d_qkv = after(pack(plan, over_all + over_seq, vectors, seq, rank), d_qkv)
    added, split = after(exchange(packed), project_split(d_qkv[::-1], qkv_w, NT, 512, quarter))
    moving = scatter_start(*split)
    added = jnp.sum(added.astype(f32), axis=0).astype(bf16)
    shared = added[:, :cut]
    shared = shared.astype(f32) + swap(shared, 1).astype(f32) + swap(shared, 2).astype(f32) + swap(shared, 3).astype(f32)
    joined, moving = after(jnp.concatenate([shared.astype(bf16), added[:, cut:]], axis=1), moving)
    back = seq_gather(joined)
    grad_in = jnp.concatenate(d_mid[::-1]) + norm_back(layer_in.astype(f32), gain_attn, scatter_end(*moving))
    g_a_gu, g_b_out, g_b_down, g_a_qkv, g_b_gu, g_a_out, g_a_down, g_b_qkv, s_gu, s_out, s_down, s_qkv = unpack(
        plan, back, over_all + over_seq, [m_gateup, m_out[None], m_down[None], m_qkv]
    )
    return (
        layer_out,
        grad_in,
        g_a_qkv.reshape(3, rank, width).transpose(0, 2, 1),
        g_b_qkv,
        s_qkv,
        g_a_out.T,
        g_b_out,
        s_out[0],
        g_a_gu.reshape(2, rank, width).transpose(0, 2, 1),
        g_b_gu,
        s_gu,
        g_a_down.T,
        g_b_down,
        s_down[0],
    )


def solution(mesh):
    split = P(None, ("seq", "tensor"), None)
    in_specs = (
        split, split, P(), P(), P(), P(),
        P(None, None, "tensor"), P(), P(None, None, "tensor"), P(None, "tensor"),
        P("tensor", None), P("tensor", None), P(), P(),
        P(None, None, "tensor"), P(), P(None, None, "tensor"), P(None, "tensor"),
        P("tensor", None), P("tensor", None), P(), P(),
    )
    out_specs = (
        split, split,
        P(), P(None, None, "tensor"), P(None, "tensor"),
        P("tensor", None), P(), P(),
        P(), P(None, None, "tensor"), P(None, "tensor"),
        P("tensor", None), P(), P(),
    )
    return jax.shard_map(local, mesh=mesh, in_specs=in_specs, out_specs=out_specs, check_vma=False)
```
